32 devices in a mesh: date: 2 (over y), slab: 16 (over z, x, core).
Axes of the slice: x: 2, y: 2, z: 4, core: 2. Of those that a mesh axis runs over, the one named last changes fastest.
Arguments:
- pressure: float32 [16, 12288], P('slab', 'date'), parts along dimension 1, may hold values from -6 to 6
- density: float32 [16, 12288], P('slab', 'date'), parts along dimension 1, may hold values from -6 to 6
- vertical_wind: float32 [16, 12288], P('slab', 'date'), parts along dimension 1, may hold values from -6 to 6
- horizontal_wind: float32 [2, 16, 12288], P(None, 'slab', 'date'), parts along dimension 2, may hold values from -6 to 6
- metric_terms: float32 [2, 6144], replicated, may hold values from 0.25 to 1
- neighbors: int32 [4, 6144], replicated, may hold values from 0 to 6143, as said below
- level_order: int32 [16], replicated, may hold values from 0 to 15, each once
- stiffness: float32 [16], replicated, may hold values from 0.2 to 5
- coupling: float32 [16], replicated, may hold values from 0.2 to 1
- weight_one: bfloat16 [64, 512], P('slab'), may hold values from -0.75 to 0.75
- weight_two: bfloat16 [512, 512], P('slab'), may hold values from -0.25 to 0.25
- weight_three: bfloat16 [512, 16], P('slab'), may hold values from -0.25 to 0.25
- pressure_adjoint: float32 [16, 12288], P('slab', 'date'), parts along dimension 1, may hold values from -6 to 6
- wind_adjoint: float32 [16, 12288], P('slab', 'date'), parts along dimension 1, may hold values from -6 to 6
Outputs:
- pressure_new: float32 [16, 12288], P('slab', 'date'), parts along dimension 1
- wind_new: float32 [16, 12288], P('slab', 'date'), parts along dimension 1
- pressure_grad: float32 [16, 12288], P('slab', 'date'), parts along dimension 1
- first_grad: float32 [128, 512], P(('date', 'slab')), parts along dimension 0
- second_grad: float32 [1024, 512], P(('date', 'slab')), parts along dimension 0
- third_grad: float32 [1024, 16], P(('date', 'slab')), parts along dimension 0
The draws below stay inside these ranges and needn't reach their ends.
There are 2 independent parts, one for each index of `date`. The reference program is written for one: setup_inputs(seed, part) draws one part's arguments, and reference() takes and returns one part's arrays. A program takes and returns all parts, laid end to end along the dimension named above; an argument that names none is the same for every part. Nothing has to cross between parts.
Inputs may be any that keep to these rules, and one draw needn't show every extreme that they name: `neighbors`: the columns are the cells of a 8 x 768 grid stored in some order; rows 0, 1, 2, 3 give the stored positions of a column's east, west, north and south neighbours, and the column itself where the grid's edge lies on that side. `level_order`: each level appears once.
All inputs are finite; a program needn't handle non-finite values.
Results may differ from the reference program's by a relative error of at most 0.0075.
Values may be sent and summed in bfloat16 or wider, within the bound.
No kernel may reach another device: no remote copies, remote signals or barrier semaphores. Data moves between devices by JAX's collectives and lax.ppermute only.
A program may use at most 128 MiB of HBM per device.

```python
import math
import jax
import jax.numpy as jnp
from jax import lax

NX = 768
HID = 512
L = 16
NCOL = 6144
NY = 8
N_SLAB = 16


def draw_neighbors(key, part):
    order = jax.random.permutation(jax.random.fold_in(key, 7), NCOL).astype(jnp.int32)
    position = jnp.argsort(order).astype(jnp.int32)
    row_index = order // NX
    column_index = order % NX
    east = row_index * NX + jnp.minimum(column_index + 1, NX - 1)
    west = row_index * NX + jnp.maximum(column_index - 1, 0)
    north = jnp.minimum(row_index + 1, NY - 1) * NX + column_index
    south = jnp.maximum(row_index - 1, 0) * NX + column_index
    return jnp.stack([position[east], position[west], position[north], position[south]]).astype(jnp.int32)


def steps_of(rng, dims, split, smallest, largest):
    level, own = 1.0, jax.random.fold_in(rng, 6)
    for dim, shards_of in split:
        draws = jnp.exp(jax.random.uniform(jax.random.fold_in(own, dim), (shards_of,), jnp.float32, smallest / len(split), largest / len(split)))
        level = level * jnp.repeat(draws, dims[dim] // shards_of).reshape([-1 if axis == dim else 1 for axis in range(len(dims))])
    return level


def bell_draw(key, dims, deviation, bound, cuts=(), kind=jnp.bfloat16):
    array = deviation * jax.random.normal(key, dims, jnp.float32)
    if cuts:
        array = array * steps_of(key, dims, cuts, -0.22, 0.18)
    return jnp.clip(array, -bound, bound).astype(kind)


def setup_inputs(seed: int = 0, part: int = 0) -> dict:
    keys = jax.random.split(jax.random.key(seed), 15)
    part_splits = jax.random.split(jax.random.fold_in(keys[14], part), 15)
    pressure = bell_draw(part_splits[0], (L, NCOL), 1.0, 6.0, ((0, 16),), jnp.float32)
    density = bell_draw(part_splits[1], (L, NCOL), 1.0, 6.0, ((0, 16),), jnp.float32)
    vertical_wind = bell_draw(part_splits[2], (L, NCOL), 1.0, 6.0, ((0, 16),), jnp.float32)
    horizontal_wind = bell_draw(part_splits[3], (2, L, NCOL), 1.0, 6.0, ((1, 16),), jnp.float32)
    metric_terms = jnp.clip(jnp.exp(jax.random.uniform(keys[4], (2, NCOL), jnp.float32, math.log(0.25), math.log(1.0))), 0.25, 1.0)
    neighbors = draw_neighbors(jax.random.fold_in(keys[14], 71), part)
    level_order = jax.random.permutation(keys[6], L).astype(jnp.int32)
    stiffness = jnp.clip(jnp.exp(jax.random.uniform(keys[7], (L,), jnp.float32, math.log(0.2), math.log(5.0))), 0.2, 5.0)
    coupling = jnp.clip(jnp.exp(jax.random.uniform(keys[8], (L,), jnp.float32, math.log(0.2), math.log(1.0))), 0.2, 1.0)
    weight_one = bell_draw(keys[9], (4 * L, HID), (4 * L) ** -0.5, 0.75, ((0, 16),))
    weight_two = bell_draw(keys[10], (HID, HID), HID ** -0.5, 0.25, ((0, 16),))
    weight_three = bell_draw(keys[11], (HID, L), HID ** -0.5, 0.25, ((0, 16),))
    pressure_adjoint = bell_draw(part_splits[12], (L, NCOL), 1.0, 6.0, ((0, 16),), jnp.float32)
    wind_adjoint = bell_draw(part_splits[13], (L, NCOL), 1.0, 6.0, ((0, 16),), jnp.float32)
    return {"pressure": pressure, "density": density, "vertical_wind": vertical_wind, "horizontal_wind": horizontal_wind, "metric_terms": metric_terms, "neighbors": neighbors, "level_order": level_order, "stiffness": stiffness, "coupling": coupling, "weight_one": weight_one, "weight_two": weight_two, "weight_three": weight_three, "pressure_adjoint": pressure_adjoint, "wind_adjoint": wind_adjoint}


def lower_diff(field):
    return jnp.concatenate([field[1:] - field[:-1], -field[-1:]], axis=0)

def upper_diff(field):
    return jnp.concatenate([jnp.zeros_like(field[:1]), field[:-1]], axis=0) - field

def build_operator(stiffness):
    below = jnp.concatenate([jnp.zeros((1,), stiffness.dtype), stiffness[:-1]])
    return jnp.diag(1.0 + stiffness + below) - jnp.diag(stiffness[:-1], 1) - jnp.diag(stiffness[:-1], -1)

def column_step(block, operator_matrix, coupling, weight_one, weight_two, weight_three):
    levels = block.shape[1]
    width = block.shape[2]
    star = block[0]
    couple = coupling[:, None]
    column_input = block[:4].reshape(4 * levels, width).astype(jnp.bfloat16)
    pre_one = jnp.dot(weight_one.T.astype(jnp.float32), column_input.astype(jnp.float32), preferred_element_type=jnp.float32)
    tanh_one = jnp.tanh(pre_one)
    act_one = tanh_one.astype(jnp.bfloat16)
    pre_two = jnp.dot(weight_two.T.astype(jnp.float32), act_one.astype(jnp.float32), preferred_element_type=jnp.float32)
    tanh_two = jnp.tanh(pre_two)
    act_two = tanh_two.astype(jnp.bfloat16)
    heating = jnp.dot(weight_three.T.astype(jnp.float32), act_two.astype(jnp.float32), preferred_element_type=jnp.float32)
    rhs = block[2] - couple * lower_diff(star) - 0.5 * block[1] + heating
    wind_next = jnp.linalg.solve(operator_matrix, rhs)
    press_next = star + upper_diff(couple * wind_next)
    wind_grad = block[5] + couple * lower_diff(block[4])
    rhs_grad = jnp.linalg.solve(operator_matrix, wind_grad)
    star_grad = block[4] - upper_diff(couple * rhs_grad)
    heat_grad = rhs_grad.astype(jnp.bfloat16)
    local_three = jnp.dot(act_two.astype(jnp.float32), heat_grad.T.astype(jnp.float32), preferred_element_type=jnp.float32)
    back_two = jnp.dot(weight_three.astype(jnp.float32), heat_grad.astype(jnp.float32), preferred_element_type=jnp.float32)
    pre_two_grad = (back_two * (1.0 - tanh_two * tanh_two)).astype(jnp.bfloat16)
    local_two = jnp.dot(act_one.astype(jnp.float32), pre_two_grad.T.astype(jnp.float32), preferred_element_type=jnp.float32)
    back_one = jnp.dot(weight_two.astype(jnp.float32), pre_two_grad.astype(jnp.float32), preferred_element_type=jnp.float32)
    pre_one_grad = (back_one * (1.0 - tanh_one * tanh_one)).astype(jnp.bfloat16)
    local_one = jnp.dot(column_input.astype(jnp.float32), pre_one_grad.T.astype(jnp.float32), preferred_element_type=jnp.float32)
    input_grad = jnp.dot(weight_one.astype(jnp.float32), pre_one_grad.astype(jnp.float32), preferred_element_type=jnp.float32)
    star_grad = star_grad + input_grad[:levels]
    return (press_next, wind_next, star_grad, local_one, local_two, local_three)

def reference(pressure, density, vertical_wind, horizontal_wind, metric_terms, neighbors, level_order, stiffness, coupling, weight_one, weight_two, weight_three, pressure_adjoint, wind_adjoint):
    east = jnp.take(horizontal_wind[0], neighbors[0], axis=1)
    west = jnp.take(horizontal_wind[0], neighbors[1], axis=1)
    north = jnp.take(horizontal_wind[1], neighbors[2], axis=1)
    south = jnp.take(horizontal_wind[1], neighbors[3], axis=1)
    diverg = metric_terms[0] * (east - west) + metric_terms[1] * (north - south)
    star = pressure - diverg
    inverse = jnp.argsort(level_order).astype(jnp.int32)
    stacked = jnp.take(jnp.stack([star, density, vertical_wind, diverg, pressure_adjoint, wind_adjoint]), inverse, axis=1)
    levels = stacked.shape[1]
    columns = stacked.shape[2]
    blocks = jnp.transpose(stacked.reshape(6, levels, N_SLAB, columns // N_SLAB), (2, 0, 1, 3))
    operator_matrix = build_operator(stiffness)

    def visit(carry, block):
        outs = column_step(block, operator_matrix, coupling, weight_one, weight_two, weight_three)
        return ((carry[0] + outs[3], carry[1] + outs[4], carry[2] + outs[5]), (outs[0], outs[1], outs[2]))
    start = (jnp.zeros(weight_one.shape, jnp.float32), jnp.zeros(weight_two.shape, jnp.float32), jnp.zeros(weight_three.shape, jnp.float32))
    totals, fields = lax.scan(visit, start, blocks)

    def restore(field):
        whole = jnp.transpose(field, (1, 0, 2)).reshape(levels, columns)
        return jnp.take(whole, level_order, axis=0)
    scale = 1.0 / math.sqrt(columns)
    return (restore(fields[0]), restore(fields[1]), restore(fields[2]), totals[0] * scale, totals[1] * scale, totals[2] * scale)
```

```python
import functools
import math

import jax
import jax.numpy as jnp
from jax import lax
from jax.experimental import pallas as pl
from jax.experimental.pallas import tpu as pltpu
from jax.sharding import PartitionSpec as P


def lower_diff(field):
    return jnp.concatenate([field[1:] - field[:-1], -field[-1:]], axis=0)


def upper_diff(field):
    return jnp.concatenate([jnp.zeros_like(field[:1]), field[:-1]], axis=0) - field


def level_inverse(stiffness):
    below = jnp.concatenate([jnp.zeros((1,), jnp.float32), stiffness[:-1]])
    matrix = (
        jnp.diag(1.0 + stiffness + below)
        - jnp.diag(stiffness[:-1], 1)
        - jnp.diag(stiffness[:-1], -1)
    )
    factor = jnp.linalg.cholesky(matrix)
    identity = jnp.eye(stiffness.shape[0], dtype=jnp.float32)
    return jax.scipy.linalg.cho_solve((factor, True), identity)


def apply_inverse(inverse_matrix, rhs):
    return jnp.dot(
        inverse_matrix, rhs, precision=lax.Precision.HIGHEST, preferred_element_type=jnp.float32
    )


def contract_first(left, right):
    return lax.dot_general(
        left, right, (((0,), (0,)), ((), ())), preferred_element_type=jnp.float32
    )


def contract_last(left, right):
    return lax.dot_general(
        left, right, (((1,), (1,)), ((), ())), preferred_element_type=jnp.float32
    )


def body(
    pressure,
    density,
    vertical_wind,
    horizontal_wind,
    metric_terms,
    neighbors,
    level_order,
    stiffness,
    coupling,
    weight_one,
    weight_two,
    weight_three,
    pressure_adjoint,
    wind_adjoint,
):
    east = jnp.take(horizontal_wind[0], neighbors[0], axis=1)
    west = jnp.take(horizontal_wind[0], neighbors[1], axis=1)
    north = jnp.take(horizontal_wind[1], neighbors[2], axis=1)
    south = jnp.take(horizontal_wind[1], neighbors[3], axis=1)
    diverg = metric_terms[0] * (east - west) + metric_terms[1] * (north - south)
    star = pressure - diverg
    inverse = jnp.argsort(level_order)
    scale = 1.0 / math.sqrt(neighbors.shape[1])
    forward_raw = lax.all_to_all(
        jnp.stack([star, density, vertical_wind, diverg]).astype(jnp.bfloat16),
        "slab",
        split_axis=2,
        concat_axis=1,
        tiled=True,
    ).astype(jnp.float32)
    full_one, full_two, full_three = (
        lax.all_gather(weight_one, "slab", axis=0, tiled=True),
        lax.all_gather(weight_two, "slab", axis=0, tiled=True),
        lax.all_gather(weight_three, "slab", axis=0, tiled=True),
    )
    forward_part = jnp.take(forward_raw, inverse, axis=1)
    levels = forward_part.shape[1]
    width = forward_part.shape[2]
    couple = coupling[:, None]
    column_input = forward_part.reshape(4 * levels, width).astype(jnp.bfloat16)
    pre_one = contract_first(full_one, column_input)
    tanh_one = jnp.tanh(pre_one)
    act_one = tanh_one.astype(jnp.bfloat16)
    pre_two = contract_first(full_two, act_one)
    tanh_two = jnp.tanh(pre_two)
    act_two = tanh_two.astype(jnp.bfloat16)
    heating = contract_first(full_three, act_two)
    star_column = forward_part[0]
    rhs = forward_part[2] - couple * lower_diff(star_column) - 0.5 * forward_part[1] + heating
    inverse_matrix = level_inverse(stiffness)
    wind_next = apply_inverse(inverse_matrix, rhs)
    press_next = star_column + upper_diff(couple * wind_next)
    forward_slabs = lax.all_to_all(
        jnp.take(jnp.stack([press_next, wind_next]), level_order, axis=1).astype(jnp.bfloat16),
        "slab",
        split_axis=1,
        concat_axis=2,
        tiled=True,
    ).astype(jnp.float32)
    adjoint_raw = lax.all_to_all(
        jnp.stack([pressure_adjoint, wind_adjoint]), "slab", split_axis=2, concat_axis=1, tiled=True
    )
    adjoint_part = jnp.take(adjoint_raw, inverse, axis=1)
    wind_grad = adjoint_part[1] + couple * lower_diff(adjoint_part[0])
    rhs_grad = apply_inverse(inverse_matrix, wind_grad)
    star_grad = adjoint_part[0] - upper_diff(couple * rhs_grad)
    heat_grad = rhs_grad.astype(jnp.bfloat16)
    local_three = contract_last(act_two, heat_grad) * scale
    back_two = jnp.dot(full_three, heat_grad, preferred_element_type=jnp.float32)
    pre_two_grad = (back_two * (1.0 - tanh_two * tanh_two)).astype(jnp.bfloat16)
    local_two = contract_last(act_one, pre_two_grad) * scale
    back_one = jnp.dot(full_two, pre_two_grad, preferred_element_type=jnp.float32)
    pre_one_grad = (back_one * (1.0 - tanh_one * tanh_one)).astype(jnp.bfloat16)
    local_one = contract_last(column_input, pre_one_grad) * scale
    first_grad, second_grad, third_grad = (
        lax.psum_scatter(local_one, "slab", scatter_dimension=0, tiled=True),
        lax.psum_scatter(local_two, "slab", scatter_dimension=0, tiled=True),
        lax.psum_scatter(local_three, "slab", scatter_dimension=0, tiled=True),
    )
    input_grad = jnp.dot(full_one, pre_one_grad, preferred_element_type=jnp.float32)
    star_grad = star_grad + input_grad[:levels]
    stored_grad = jnp.take(star_grad, level_order, axis=0)
    pressure_new = forward_slabs[0]
    wind_new = forward_slabs[1]
    pressure_grad = lax.all_to_all(
        stored_grad[None].astype(jnp.bfloat16), "slab", split_axis=1, concat_axis=2, tiled=True
    ).astype(jnp.float32)[0]
    return (pressure_new, wind_new, pressure_grad, first_grad, second_grad, third_grad)


LANE = 128
SUB = 8


def spec():
    return pl.BlockSpec(memory_space=pltpu.VMEM)


def call(kernel, outs, n_in, scratch=(), name=None):
    return pl.pallas_call(
        kernel,
        out_shape=outs,
        in_specs=[spec() for _ in range(n_in)],
        out_specs=jax.tree.map(lambda _: spec(), outs),
        scratch_shapes=list(scratch),
        compiler_params=pltpu.CompilerParams(vmem_limit_bytes=48 << 20),
        name=name,
    )


def shape(dims, kind):
    return jax.ShapeDtypeStruct(dims, kind)


def pack_weights_kernel(one_ref, two_ref, three_ref, out_ref, part_ref):
    group = lax.axis_index("slab") % 4
    devices = out_ref.shape[0]
    rows, lanes = lax.broadcasted_iota(jnp.int32, (32, LANE), 0), lax.broadcasted_iota(jnp.int32, (32, LANE), 1)
    place = (lanes == rows + 32 * group).astype(jnp.float32).astype(jnp.bfloat16)
    three = jnp.dot(three_ref[...], place, preferred_element_type=jnp.float32)
    one = one_ref[...].astype(jnp.float32)
    for half in range(2):
        for c in range(4):
            part_ref[2 * c : 2 * c + 2, :] = one[2 * half : 2 * half + 2, LANE * c : LANE * (c + 1)]
        part_ref[8:16, :] = three[8 * half : 8 * half + 8, :]
        part = part_ref[...].astype(jnp.bfloat16)
        for c in range(4):
            block = two_ref[16 * half : 16 * half + 16, LANE * c : LANE * (c + 1)]
            for d in range(half, devices, 2):
                out_ref[d, 16 * c : 16 * c + 16, :] = block
        for d in range(half, devices, 2):
            out_ref[d, 64:80, :] = part


def gather_pair(table, first_index, second_index, first_ref, second_ref):
    rows = table.shape[0]
    count = first_index.shape[0] // SUB
    parts = []
    for index in (first_index, second_index):
        for v in range(count):
            block = index[SUB * v : SUB * v + SUB, :]
            parts.append((block >> 7, block & (LANE - 1)))
    totals = [jnp.zeros((SUB, LANE), jnp.float32) for _ in parts]
    for h in range(rows):
        row = jnp.broadcast_to(table[h : h + 1, :], (SUB, LANE))
        for i, (high, low) in enumerate(parts):
            picked = jnp.take_along_axis(row, low, axis=1, mode="promise_in_bounds")
            totals[i] = jnp.where(high == h, picked, totals[i])
    return totals[:count], totals[count:]


def pack_fields_kernel(p_ref, d_ref, w_ref, u_ref, m_ref, n_ref, pa_ref, wa_ref, out_ref, f_ref):
    blocks = p_ref.shape[0] // SUB
    stride = out_ref.shape[1]
    east, west = gather_pair(u_ref.at[0], n_ref[:, 0, :], n_ref[:, 1, :], None, None)
    north, south = gather_pair(u_ref.at[1], n_ref[:, 2, :], n_ref[:, 3, :], None, None)
    for j in range(blocks):
        rows = slice(SUB * j, SUB * j + SUB)
        diverg = m_ref[rows, 0, :] * (east[j] - west[j]) + m_ref[rows, 1, :] * (north[j] - south[j])
        fields = (p_ref[rows, :] - diverg, d_ref[rows, :], w_ref[rows, :], diverg, pa_ref[rows, :], wa_ref[rows, :])
        for f, field in enumerate(fields):
            f_ref[pl.ds(blocks * f + j, SUB, stride=stride), :] = field
    for k in range(6 * blocks, stride):
        f_ref[pl.ds(k, SUB, stride=stride), :] = jnp.zeros((SUB, LANE), jnp.float32)
    for c in range(SUB):
        block = f_ref[stride * c : stride * (c + 1), :].astype(jnp.bfloat16)
        out_ref[2 * c] = block
        out_ref[2 * c + 1] = block


def unpack_weights_kernel(mine_ref, other_ref, w1t_ref, w1s_ref, w2_ref, w2t_ref, w3t_ref, w3_ref, a_ref, b_ref, one_ref):
    core = lax.axis_index("slab") % 2
    devices = mine_ref.shape[0]
    for s in range(devices):
        for c in range(4):
            cols = slice(LANE * c, LANE * (c + 1))
            w2_ref[pl.ds(pl.multiple_of(32 * s + 16 * core, 16), 16), cols] = mine_ref[s, 16 * c : 16 * c + 16, :]
            w2_ref[pl.ds(pl.multiple_of(32 * s + 16 * (1 - core), 16), 16), cols] = other_ref[s, 16 * c : 16 * c + 16, :]
        a_ref[16 * s : 16 * s + 16, :] = mine_ref[s, 64:80, :].astype(jnp.float32)
        b_ref[16 * s : 16 * s + 16, :] = other_ref[s, 64:80, :].astype(jnp.float32)
    first = core == 0
    for c in range(4):
        for r in range(2):
            a = a_ref[pl.ds(2 * c + r, devices, stride=16), :]
            b = b_ref[pl.ds(2 * c + r, devices, stride=16), :]
            one_ref[pl.ds(4 * devices * c + r, devices, stride=4), :] = jnp.where(first, a, b)
            one_ref[pl.ds(4 * devices * c + 2 + r, devices, stride=4), :] = jnp.where(first, b, a)
    three = []
    for t in range(4):
        a = sum(a_ref[16 * s + 8 : 16 * s + 16, :] for s in range(4 * t, 4 * t + 4))
        b = sum(b_ref[16 * s + 8 : 16 * s + 16, :] for s in range(4 * t, 4 * t + 4))
        three.append(jnp.concatenate([jnp.where(first, a, b), jnp.where(first, b, a)], axis=0))
    three = jnp.concatenate(three, axis=1)
    w3t_ref[...] = three.astype(jnp.bfloat16)
    w3_ref[...] = three.T.astype(jnp.bfloat16)
    one = jnp.concatenate([one_ref[4 * devices * c : 4 * devices * (c + 1), :] for c in range(4)], axis=1)
    w1t_ref[...] = one.T.astype(jnp.bfloat16)
    w1s_ref[...] = one[: w1s_ref.shape[0], :].astype(jnp.bfloat16)
    w2t_ref[...] = w2_ref[...].T


def shifted_up(field, rows):
    return jnp.where(rows < field.shape[0] - 1, pltpu.roll(field, field.shape[0] - 1, 0), 0.0)


def shifted_down(field, rows):
    return jnp.where(rows > 0, pltpu.roll(field, 1, 0), 0.0)


def operator_inverse(stiff, rows):
    size = stiff.shape[0]
    below = shifted_down(stiff, rows)
    lower, diagonal = -below, 1.0 + stiff + below
    upper = jnp.where(rows < size - 1, -stiff, 0.0)
    right = (rows == lax.broadcasted_iota(jnp.int32, (size, size), 1)).astype(jnp.float32)
    distance = 1
    while distance < size:
        down = lambda v: pltpu.roll(v, distance, 0)
        up = lambda v: pltpu.roll(v, size - distance, 0)
        alpha, gamma = -lower / down(diagonal), -upper / up(diagonal)
        right = right + alpha * down(right) + gamma * up(right)
        diagonal = diagonal + alpha * down(upper) + gamma * up(lower)
        lower, upper = alpha * down(lower), gamma * up(upper)
        distance *= 2
    return right / diagonal


def column_kernel(
    f_ref, w1t_ref, w1s_ref, w2_ref, w2t_ref, w3t_ref, w3_ref, order_ref, stiff_ref, couple_ref, out_ref,
    x_ref, y_ref, one_ref, act_ref, sel_ref,
):
    core = lax.axis_index("slab") % 2
    levels, stride = f_ref.shape[0], f_ref.shape[1]
    width = act_ref.shape[1]
    blocks = width // LANE
    chips = out_ref.shape[0]
    f32, bf16 = jnp.float32, jnp.bfloat16
    for s in range(levels):
        x_ref[stride * s : stride * (s + 1), :] = f_ref[s].astype(f32)
    raw = jnp.concatenate([x_ref[pl.ds(k, levels, stride=stride), :] for k in range(6 * blocks)], axis=1).astype(bf16)
    square_rows = lax.broadcasted_iota(jnp.int32, (levels, levels), 0)
    square_cols = lax.broadcasted_iota(jnp.int32, (levels, levels), 1)
    place = (order_ref[...] == square_rows).astype(f32).astype(bf16)
    ordered = jnp.dot(place, raw, preferred_element_type=f32)
    star, density, vertical, diverg, pressure_adjoint, wind_adjoint = (
        ordered[:, width * i : width * (i + 1)] for i in range(6)
    )
    diagonal = square_rows == square_cols
    stiff = jnp.sum(jnp.where(diagonal, stiff_ref[...], 0.0), axis=1, keepdims=True)
    couple = jnp.sum(jnp.where(diagonal, couple_ref[...], 0.0), axis=1, keepdims=True)
    inverse = operator_inverse(jnp.broadcast_to(stiff, (levels, levels)), square_rows)
    couple = jnp.broadcast_to(couple, (levels, width))
    rows = lax.broadcasted_iota(jnp.int32, (levels, width), 0)

    def solve(right):
        return jnp.dot(inverse, right, precision=lax.Precision.HIGHEST, preferred_element_type=f32)

    def lower(field):
        return shifted_up(field, rows) - field

    def upper(field):
        return shifted_down(field, rows) - field

    rhs_grad = solve(wind_adjoint + couple * lower(pressure_adjoint))
    star_part = pressure_adjoint - upper(couple * rhs_grad)
    heat_grad = rhs_grad.astype(bf16)
    column_input = jnp.concatenate([star, density, vertical, diverg], axis=0).astype(bf16)
    tanh_one = jnp.tanh(jnp.dot(w1t_ref[...], column_input, preferred_element_type=f32))
    act_one = tanh_one.astype(bf16)
    act_ref[...] = act_one
    tanh_two = jnp.tanh(jnp.dot(w2t_ref[...], act_one, preferred_element_type=f32))
    act_two = tanh_two.astype(bf16)
    heating = jnp.dot(w3t_ref[...], act_two, preferred_element_type=f32)
    wind_next = solve(vertical - couple * lower(star) - 0.5 * density + heating)
    press_next = star + upper(couple * wind_next)
    back_two = jnp.dot(w3_ref[...], heat_grad, preferred_element_type=f32)
    pre_two_grad = (back_two * (1.0 - tanh_two * tanh_two)).astype(bf16)
    back_one = jnp.dot(w2_ref[...], pre_two_grad, preferred_element_type=f32)
    pre_one_grad = (back_one * (1.0 - tanh_one * tanh_one)).astype(bf16)
    star_grad = star_part + jnp.dot(w1s_ref[...], pre_one_grad, preferred_element_type=f32)
    for c in range(chips):
        sel_ref[32 * c : 32 * c + 32, :] = act_ref[pl.ds(pl.multiple_of(64 * c + 32 * core, 32), 32), :]
    local_two = contract_last(sel_ref[...], pre_two_grad)
    local_three = contract_last(heat_grad, act_two)
    local_one = contract_last(column_input, pre_one_grad)
    first = core == 0
    for c in range(chips):
        mine = jnp.where(first, local_one[8 * c : 8 * c + 4, :], local_one[8 * c + 4 : 8 * c + 8, :])
        for q in range(4):
            cols = slice(LANE * q, LANE * (q + 1))
            out_ref[c, 32 * q : 32 * q + 32, :] = local_two[32 * c : 32 * c + 32, cols].astype(bf16)
            one_ref[4 * q : 4 * q + 4, :] = mine[:, cols]
        out_ref[c, 128:144, :] = one_ref[...].astype(bf16)
        out_ref[c, 144:160, :] = local_three[:, LANE * (c // 2) : LANE * (c // 2 + 1)].astype(bf16)
    fields = jnp.concatenate([press_next, wind_next, star_grad], axis=1).astype(bf16)
    stored = lax.dot_general(place, fields, (((0,), (0,)), ((), ())), preferred_element_type=f32)
    back = y_ref.shape[0] // levels
    for k in range(3 * blocks):
        y_ref[pl.ds(k, levels, stride=back), :] = stored[:, LANE * k : LANE * (k + 1)]
    for k in range(3 * blocks, back):
        y_ref[pl.ds(k, levels, stride=back), :] = jnp.zeros((levels, LANE), f32)
    for c in range(chips):
        out_ref[c, 160 : 160 + back, :] = y_ref[pl.ds(pl.multiple_of(back * (2 * c + core), 8), back), :].astype(bf16)


def finish_kernel(scale, r_ref, p_ref, w_ref, g_ref, one_ref, two_ref, three_ref, y_ref):
    chips = r_ref.shape[0]
    back = r_ref.shape[1] - 160
    blocks = p_ref.shape[0] // chips
    group = lax.axis_index("slab") % 4

    def total(start, stop):
        return sum(r_ref[c, start:stop, :].astype(jnp.float32) for c in range(chips)) * scale

    for q in range(4):
        two_ref[:, LANE * q : LANE * (q + 1)] = total(32 * q, 32 * q + 32)
    one = total(128, 144)
    for q in range(4):
        one_ref[:, LANE * q : LANE * (q + 1)] = one[4 * q : 4 * q + 4, :]
    three = total(144, 160)
    picked = three[:, 0:32]
    for q in range(1, 4):
        picked = jnp.where(group == q, three[:, 32 * q : 32 * q + 32], picked)
    three_ref[...] = picked
    for c in range(chips):
        y_ref[back * c : back * (c + 1), :] = r_ref[c, 160 : 160 + back, :].astype(jnp.float32)
    for f, ref in enumerate((p_ref, w_ref, g_ref)):
        for j in range(blocks):
            ref[chips * j : chips * (j + 1), :] = y_ref[pl.ds(blocks * f + j, chips, stride=back), :]


def fast_body(
    pressure, density, vertical_wind, horizontal_wind, metric_terms, neighbors, level_order, stiffness, coupling,
    weight_one, weight_two, weight_three, pressure_adjoint, wind_adjoint,
):
    devices = level_order.shape[0]
    columns = neighbors.shape[1]
    rows = columns // LANE
    chips = devices // 2
    blocks = rows // chips
    width = blocks * LANE
    hidden = weight_two.shape[1]
    levels = devices
    f32, bf16 = jnp.float32, jnp.bfloat16

    def pad(count):
        return -(-count // SUB) * SUB

    send_weights = call(
        pack_weights_kernel, shape((devices, 80, LANE), bf16), 3, [pltpu.VMEM((16, LANE), f32)], "pack_weights"
    )(weight_one, weight_two, weight_three.T)
    mine = lax.all_to_all(send_weights, "slab", split_axis=0, concat_axis=0, tiled=True)
    other = lax.ppermute(mine, "slab", [(i, i ^ 1) for i in range(devices)])

    def view(field):
        return field.reshape(rows, LANE)

    def lanes(table):
        return table.reshape(table.shape[0], rows, LANE).transpose(1, 0, 2)

    stride = pad(6 * blocks)
    send_fields = call(
        pack_fields_kernel, shape((devices, stride, LANE), bf16), 8, [pltpu.VMEM((chips * stride, LANE), f32)], "pack_fields"
    )(
        view(pressure), view(density), view(vertical_wind), horizontal_wind.reshape(2, rows, LANE),
        lanes(metric_terms), lanes(neighbors), view(pressure_adjoint), view(wind_adjoint),
    )
    fields = lax.all_to_all(send_fields, "slab", split_axis=0, concat_axis=0, tiled=True)
    weights = call(
        unpack_weights_kernel,
        (
            shape((hidden, 4 * levels), bf16), shape((levels, hidden), bf16), shape((hidden, hidden), bf16),
            shape((hidden, hidden), bf16), shape((levels, hidden), bf16), shape((hidden, levels), bf16),
        ),
        2,
        [pltpu.VMEM((devices * 16, LANE), f32), pltpu.VMEM((devices * 16, LANE), f32), pltpu.VMEM((16 * devices, LANE), f32)],
        "unpack_weights",
    )(mine, other)
    back = pad(3 * blocks)
    send_back = call(
        column_kernel,
        shape((chips, 160 + back, LANE), bf16),
        10,
        [
            pltpu.VMEM((devices * stride, LANE), f32), pltpu.VMEM((levels * back, LANE), f32), pltpu.VMEM((16, LANE), f32),
            pltpu.VMEM((hidden, width), bf16), pltpu.VMEM((hidden // 2, width), bf16),
        ],
        "column_step",
    )(fields, *weights, level_order.reshape(1, levels), stiffness.reshape(1, levels), coupling.reshape(1, levels))
    received = lax.all_to_all(
        send_back, "slab", split_axis=0, concat_axis=0, tiled=True,
        axis_index_groups=[list(range(core, devices, 2)) for core in range(2)],
    )
    field_out = shape((rows, LANE), f32)
    new_pressure, new_wind, grad, first_grad, second_grad, third_grad = call(
        functools.partial(finish_kernel, 1.0 / math.sqrt(columns)),
        (
            field_out, field_out, field_out, shape(weight_one.shape, f32), shape(weight_two.shape, f32),
            shape(weight_three.shape[::-1], f32),
        ),
        1,
        [pltpu.VMEM((chips * back, LANE), f32)],
        "finish",
    )(received)
    return (
        new_pressure.reshape(1, columns), new_wind.reshape(1, columns), grad.reshape(1, columns),
        first_grad, second_grad, third_grad.T,
    )


def fits_tiles(*args):
    pressure, level_order, neighbors = args[0], args[6], args[5]
    weight_one, weight_two, weight_three = args[9:12]
    devices = level_order.shape[0]
    return (
        pressure.shape[0] == 1
        and devices == 2 * SUB
        and neighbors.shape[1] % (LANE * SUB) == 0
        and weight_one.shape == (4, 4 * LANE)
        and weight_two.shape == (32, 4 * LANE)
        and weight_three.shape == (32, 16)
    )


def any_body(*args):
    return (fast_body if fits_tiles(*args) else body)(*args)


def solution(mesh):
    in_specs = (
        P("slab", "date"),
        P("slab", "date"),
        P("slab", "date"),
        P(None, "slab", "date"),
        P(),
        P(),
        P(),
        P(),
        P(),
        P("slab", None),
        P("slab", None),
        P("slab", None),
        P("slab", "date"),
        P("slab", "date"),
    )
    out_specs = (
        P("slab", "date"),
        P("slab", "date"),
        P("slab", "date"),
        P(("date", "slab"), None),
        P(("date", "slab"), None),
        P(("date", "slab"), None),
    )
    return jax.shard_map(any_body, mesh=mesh, in_specs=in_specs, out_specs=out_specs, check_vma=False)
```

```python
import functools
import math

import jax
import jax.numpy as jnp
from jax import lax
from jax.experimental import pallas as pl
from jax.experimental.pallas import tpu as pltpu
from jax.sharding import PartitionSpec as P


def lower_diff(field):
    return jnp.concatenate([field[1:] - field[:-1], -field[-1:]], axis=0)


def upper_diff(field):
    return jnp.concatenate([jnp.zeros_like(field[:1]), field[:-1]], axis=0) - field


def level_inverse(stiffness):
    below = jnp.concatenate([jnp.zeros((1,), jnp.float32), stiffness[:-1]])
    matrix = (
        jnp.diag(1.0 + stiffness + below)
        - jnp.diag(stiffness[:-1], 1)
        - jnp.diag(stiffness[:-1], -1)
    )
    factor = jnp.linalg.cholesky(matrix)
    identity = jnp.eye(stiffness.shape[0], dtype=jnp.float32)
    return jax.scipy.linalg.cho_solve((factor, True), identity)


def apply_inverse(inverse_matrix, rhs):
    return jnp.dot(
        inverse_matrix, rhs, precision=lax.Precision.HIGHEST, preferred_element_type=jnp.float32
    )


def contract_first(left, right):
    return lax.dot_general(
        left, right, (((0,), (0,)), ((), ())), preferred_element_type=jnp.float32
    )


def contract_last(left, right):
    return lax.dot_general(
        left, right, (((1,), (1,)), ((), ())), preferred_element_type=jnp.float32
    )


def body(
    pressure,
    density,
    vertical_wind,
    horizontal_wind,
    metric_terms,
    neighbors,
    level_order,
    stiffness,
    coupling,
    weight_one,
    weight_two,
    weight_three,
    pressure_adjoint,
    wind_adjoint,
):
    east = jnp.take(horizontal_wind[0], neighbors[0], axis=1)
    west = jnp.take(horizontal_wind[0], neighbors[1], axis=1)
    north = jnp.take(horizontal_wind[1], neighbors[2], axis=1)
    south = jnp.take(horizontal_wind[1], neighbors[3], axis=1)
    diverg = metric_terms[0] * (east - west) + metric_terms[1] * (north - south)
    star = pressure - diverg
    inverse = jnp.argsort(level_order)
    scale = 1.0 / math.sqrt(neighbors.shape[1])
    forward_raw = lax.all_to_all(
        jnp.stack([star, density, vertical_wind, diverg]).astype(jnp.bfloat16),
        "slab",
        split_axis=2,
        concat_axis=1,
        tiled=True,
    ).astype(jnp.float32)
    full_one, full_two, full_three = (
        lax.all_gather(weight_one, "slab", axis=0, tiled=True),
        lax.all_gather(weight_two, "slab", axis=0, tiled=True),
        lax.all_gather(weight_three, "slab", axis=0, tiled=True),
    )
    forward_part = jnp.take(forward_raw, inverse, axis=1)
    levels = forward_part.shape[1]
    width = forward_part.shape[2]
    couple = coupling[:, None]
    column_input = forward_part.reshape(4 * levels, width).astype(jnp.bfloat16)
    pre_one = contract_first(full_one, column_input)
    tanh_one = jnp.tanh(pre_one)
    act_one = tanh_one.astype(jnp.bfloat16)
    pre_two = contract_first(full_two, act_one)
    tanh_two = jnp.tanh(pre_two)
    act_two = tanh_two.astype(jnp.bfloat16)
    heating = contract_first(full_three, act_two)
    star_column = forward_part[0]
    rhs = forward_part[2] - couple * lower_diff(star_column) - 0.5 * forward_part[1] + heating
    inverse_matrix = level_inverse(stiffness)
    wind_next = apply_inverse(inverse_matrix, rhs)
    press_next = star_column + upper_diff(couple * wind_next)
    forward_slabs = lax.all_to_all(
        jnp.take(jnp.stack([press_next, wind_next]), level_order, axis=1).astype(jnp.bfloat16),
        "slab",
        split_axis=1,
        concat_axis=2,
        tiled=True,
    ).astype(jnp.float32)
    adjoint_raw = lax.all_to_all(
        jnp.stack([pressure_adjoint, wind_adjoint]), "slab", split_axis=2, concat_axis=1, tiled=True
    )
    adjoint_part = jnp.take(adjoint_raw, inverse, axis=1)
    wind_grad = adjoint_part[1] + couple * lower_diff(adjoint_part[0])
    rhs_grad = apply_inverse(inverse_matrix, wind_grad)
    star_grad = adjoint_part[0] - upper_diff(couple * rhs_grad)
    heat_grad = rhs_grad.astype(jnp.bfloat16)
    local_three = contract_last(act_two, heat_grad) * scale
    back_two = jnp.dot(full_three, heat_grad, preferred_element_type=jnp.float32)
    pre_two_grad = (back_two * (1.0 - tanh_two * tanh_two)).astype(jnp.bfloat16)
    local_two = contract_last(act_one, pre_two_grad) * scale
    back_one = jnp.dot(full_two, pre_two_grad, preferred_element_type=jnp.float32)
    pre_one_grad = (back_one * (1.0 - tanh_one * tanh_one)).astype(jnp.bfloat16)
    local_one = contract_last(column_input, pre_one_grad) * scale
    first_grad, second_grad, third_grad = (
        lax.psum_scatter(local_one, "slab", scatter_dimension=0, tiled=True),
        lax.psum_scatter(local_two, "slab", scatter_dimension=0, tiled=True),
        lax.psum_scatter(local_three, "slab", scatter_dimension=0, tiled=True),
    )
    input_grad = jnp.dot(full_one, pre_one_grad, preferred_element_type=jnp.float32)
    star_grad = star_grad + input_grad[:levels]
    stored_grad = jnp.take(star_grad, level_order, axis=0)
    pressure_new = forward_slabs[0]
    wind_new = forward_slabs[1]
    pressure_grad = lax.all_to_all(
        stored_grad[None].astype(jnp.bfloat16), "slab", split_axis=1, concat_axis=2, tiled=True
    ).astype(jnp.float32)[0]
    return (pressure_new, wind_new, pressure_grad, first_grad, second_grad, third_grad)


LANE = 128
SUB = 8
PIECE = 32
HEAD = 4 * PIECE
TAIL = HEAD + 16


def call(kernel, name, outs, n_in, scratch=(), space=pltpu.VMEM):
    return pl.pallas_call(
        kernel,
        out_shape=outs,
        in_specs=[pl.BlockSpec(memory_space=space) for _ in range(n_in)],
        out_specs=jax.tree.map(lambda _: pl.BlockSpec(memory_space=pltpu.VMEM), outs),
        scratch_shapes=list(scratch),
        compiler_params=pltpu.CompilerParams(vmem_limit_bytes=48 << 20),
        name=name,
    )


def shape(dims, kind):
    return jax.ShapeDtypeStruct(dims, kind)


def difference(table_ref, first, second):
    groups = table_ref.shape[0] // SUB
    sublanes = lax.broadcasted_iota(jnp.int32, (SUB, LANE), 0)
    out = []
    for r in range(SUB):
        kept = []
        for index in (first, second):
            high = jnp.broadcast_to(index[r : r + 1, :] >> 7, (SUB, LANE))
            low = jnp.broadcast_to(index[r : r + 1, :] & (LANE - 1), (SUB, LANE))
            total = jnp.zeros((SUB, LANE), jnp.float32)
            for g in range(groups):
                picked = jnp.take_along_axis(table_ref[SUB * g : SUB * g + SUB, :], low, axis=1, mode="promise_in_bounds")
                total = jnp.where(high == sublanes + SUB * g, picked, total)
            kept.append(total)
        out.append(jnp.sum(kept[0] - kept[1], axis=0, keepdims=True))
    return jnp.concatenate(out, axis=0)


def lane_group(lanes, q):
    return (lanes >= PIECE * q) & (lanes < PIECE * (q + 1))


def pack_kernel(
    p_hbm, d_hbm, w_hbm, u_hbm, m_hbm, n_hbm, one_hbm, two_hbm, three_hbm, pa_hbm, wa_hbm, out_ref,
    p_ref, d_ref, w_ref, u_ref, m_ref, n_ref, one_ref, two_ref, three_ref, pa_ref, wa_ref, part_ref, f_ref, sems,
):
    pairs = (
        (n_hbm, n_ref), (u_hbm, u_ref), (m_hbm, m_ref), (p_hbm, p_ref), (d_hbm, d_ref), (w_hbm, w_ref),
        (pa_hbm, pa_ref), (wa_hbm, wa_ref), (one_hbm, one_ref), (two_hbm, two_ref), (three_hbm, three_ref),
    )
    copies = [pltpu.make_async_copy(source, target, sems.at[i]) for i, (source, target) in enumerate(pairs)]
    for copy in copies:
        copy.start()
    f32, bf16 = jnp.float32, jnp.bfloat16
    chips = out_ref.shape[0]
    rest = out_ref.shape[1] - TAIL
    blocks = p_ref.shape[0] // chips
    for copy in copies:
        copy.wait()

    def put(f, j, tile):
        f_ref[pl.ds(4 + blocks * f + j, chips, stride=rest), :] = tile

    for j in range(blocks):
        rows = slice(SUB * j, SUB * j + SUB)
        along = difference(u_ref.at[0], n_ref[rows, 0, :], n_ref[rows, 1, :])
        across = difference(u_ref.at[1], n_ref[rows, 2, :], n_ref[rows, 3, :])
        diverg = m_ref[rows, 0, :] * along + m_ref[rows, 1, :] * across
        for f, tile in enumerate((p_ref[rows, :] - diverg, d_ref[rows, :], w_ref[rows, :], diverg, pa_ref[rows, :], wa_ref[rows, :])):
            put(f, j, tile)
    lanes = lax.broadcasted_iota(jnp.int32, (PIECE, LANE), 1)
    spread = (lanes % PIECE == lax.broadcasted_iota(jnp.int32, (PIECE, LANE), 0)).astype(f32).astype(bf16)
    part_ref[...] = jnp.dot(three_ref[...], spread, preferred_element_type=f32)
    lanes = lax.broadcasted_iota(jnp.int32, (4, LANE), 1)
    three = jnp.zeros((4, LANE), f32)
    for q in range(4):
        three = jnp.where(lane_group(lanes, q), part_ref[4 * q : 4 * q + 4, :], three)
    one = one_ref[...].astype(f32)
    for q in range(4):
        part_ref[4 * q : 4 * q + 4, :] = one[:, LANE * q : LANE * (q + 1)]
    one = part_ref[...].astype(bf16)
    for c in range(chips):
        for q in range(4):
            out_ref[c, PIECE * q : PIECE * (q + 1), :] = two_ref[:, LANE * q : LANE * (q + 1)]
        out_ref[c, HEAD:TAIL, :] = one
        f_ref[rest * c : rest * c + 4, :] = three
        if rest > 4 + 6 * blocks:
            f_ref[rest * c + 4 + 6 * blocks : rest * (c + 1), :] = jnp.zeros((rest - 4 - 6 * blocks, LANE), f32)
        out_ref[c, TAIL:, :] = f_ref[rest * c : rest * (c + 1), :].astype(bf16)


def shifted_up(field, rows):
    return jnp.where(rows < field.shape[0] - 1, pltpu.roll(field, field.shape[0] - 1, 0), 0.0)


def shifted_down(field, rows):
    return jnp.where(rows > 0, pltpu.roll(field, 1, 0), 0.0)


def operator_inverse(stiff, rows):
    size = stiff.shape[0]
    below = shifted_down(stiff, rows)
    lower, diagonal = -below, 1.0 + stiff + below
    upper = jnp.where(rows < size - 1, -stiff, 0.0)
    right = (rows == lax.broadcasted_iota(jnp.int32, (size, size), 1)).astype(jnp.float32)
    distance = 1
    while distance < size:
        down = lambda v: pltpu.roll(v, distance, 0)
        up = lambda v: pltpu.roll(v, size - distance, 0)
        alpha, gamma = -lower / down(diagonal), -upper / up(diagonal)
        right = right + alpha * down(right) + gamma * up(right)
        diagonal = diagonal + alpha * down(upper) + gamma * up(lower)
        lower, upper = alpha * down(lower), gamma * up(upper)
        distance *= 2
    return right / diagonal


def operator_kernel(order_ref, stiff_ref, couple_ref, place_ref, inverse_ref, column_ref):
    levels = inverse_ref.shape[0]
    rows = lax.broadcasted_iota(jnp.int32, (levels, levels), 0)
    diagonal = rows == lax.broadcasted_iota(jnp.int32, (levels, levels), 1)
    place_ref[...] = (order_ref[...] == rows).astype(jnp.float32).astype(jnp.bfloat16)
    stiff = jnp.sum(jnp.where(diagonal, stiff_ref[...], 0.0), axis=1, keepdims=True)
    couple = jnp.sum(jnp.where(diagonal, couple_ref[...], 0.0), axis=1, keepdims=True)
    inverse_ref[...] = operator_inverse(jnp.broadcast_to(stiff, (levels, levels)), rows)
    column_ref[...] = jnp.broadcast_to(couple, column_ref.shape)


def column_kernel(
    mine_ref, other_ref, place_ref, inverse_ref, column_ref, out_ref,
    a_ref, one_ref, w2_ref, w3_ref, act_ref, sel_ref, g_ref, y_ref, t_ref,
):
    f32, bf16 = jnp.float32, jnp.bfloat16
    core = lax.axis_index("slab") % 2
    first = core == 0
    chips = mine_ref.shape[0]
    devices = 2 * chips
    levels = inverse_ref.shape[0]
    width = act_ref.shape[1]
    blocks = width // LANE
    stride = mine_ref.shape[1] - HEAD
    for ref, which in ((mine_ref, core), (other_ref, 1 - core)):
        for c in range(chips):
            for q in range(4):
                rows = pl.ds(pl.multiple_of(2 * PIECE * c + PIECE * which, PIECE), PIECE)
                w2_ref[rows, LANE * q : LANE * (q + 1)] = ref[c, PIECE * q : PIECE * (q + 1), :]
            rows = pl.ds(pl.multiple_of(stride * (2 * c + which), SUB), stride)
            a_ref[rows, :] = ref[c, HEAD:, :].astype(f32)
    for q in range(4):
        for r in range(4):
            one_ref[pl.ds(4 * devices * q + r, devices, stride=4), :] = a_ref[pl.ds(4 * q + r, devices, stride=stride), :]
    one = jnp.concatenate([one_ref[4 * devices * q : 4 * devices * (q + 1), :] for q in range(4)], axis=1)
    lanes = lax.broadcasted_iota(jnp.int32, (4, LANE), 1)
    for t in range(devices // 4):
        packed = [a_ref[stride * (4 * t + s) + 16 : stride * (4 * t + s) + 20, :] for s in range(4)]
        for q in range(4):
            tile = jnp.zeros((4, LANE), f32)
            for s in range(4):
                moved = packed[s] if s == q else pltpu.roll(packed[s], PIECE * ((s - q) % 4), 1)
                tile = jnp.where(lane_group(lanes, s), moved, tile)
            w3_ref[4 * q : 4 * q + 4, LANE * t : LANE * (t + 1)] = tile
    w1t = one.T.astype(bf16)
    w1s = one[:levels, :].astype(bf16)
    w2 = w2_ref[...]
    w3t = w3_ref[...].astype(bf16)
    w3 = w3_ref[...].T.astype(bf16)
    place, inverse = place_ref[...], inverse_ref[...]
    raw = jnp.concatenate([a_ref[pl.ds(20 + k, levels, stride=stride), :] for k in range(6 * blocks)], axis=1)
    ordered = jnp.dot(place, raw.astype(bf16), preferred_element_type=f32)
    star, density, vertical, diverg, pressure_adjoint, wind_adjoint = (
        ordered[:, width * i : width * (i + 1)] for i in range(6)
    )
    couple = jnp.concatenate([column_ref[...]] * blocks, axis=1)
    rows = lax.broadcasted_iota(jnp.int32, (levels, width), 0)

    def solve(right):
        return jnp.dot(inverse, right, precision=lax.Precision.HIGHEST, preferred_element_type=f32)

    def lower(field):
        return shifted_up(field, rows) - field

    def upper(field):
        return shifted_down(field, rows) - field

    column_input = jnp.concatenate([star, density, vertical, diverg], axis=0).astype(bf16)
    tanh_one = jnp.tanh(jnp.dot(w1t, column_input, preferred_element_type=f32))
    act_one = tanh_one.astype(bf16)
    act_ref[...] = act_one
    rhs_grad = solve(wind_adjoint + couple * lower(pressure_adjoint))
    star_part = pressure_adjoint - upper(couple * rhs_grad)
    heat_grad = rhs_grad.astype(bf16)
    tanh_two = jnp.tanh(contract_first(w2, act_one))
    act_two = tanh_two.astype(bf16)
    back_two = jnp.dot(w3, heat_grad, preferred_element_type=f32)
    pre_two_grad = (back_two * (1.0 - tanh_two * tanh_two)).astype(bf16)
    back_one = jnp.dot(w2, pre_two_grad, preferred_element_type=f32)
    pre_one_grad = (back_one * (1.0 - tanh_one * tanh_one)).astype(bf16)
    heating = jnp.dot(w3t, act_two, preferred_element_type=f32)
    wind_next = solve(vertical - couple * lower(star) - 0.5 * density + heating)
    press_next = star + upper(couple * wind_next)
    star_grad = star_part + jnp.dot(w1s, pre_one_grad, preferred_element_type=f32)
    for c in range(chips):
        rows = pl.ds(pl.multiple_of(2 * PIECE * c + PIECE * core, PIECE), PIECE)
        sel_ref[PIECE * c : PIECE * (c + 1), :] = act_ref[rows, :]
    local_two = contract_last(sel_ref[...], pre_two_grad)
    local_three = contract_last(heat_grad, act_two)
    local_one = contract_last(column_input, pre_one_grad)
    fields = jnp.concatenate([press_next, wind_next, star_grad], axis=1).astype(bf16)
    stored = lax.dot_general(place, fields, (((0,), (0,)), ((), ())), preferred_element_type=f32)
    back = out_ref.shape[1] - TAIL
    for k in range(3 * blocks):
        y_ref[pl.ds(4 + k, devices, stride=back), :] = stored[:, LANE * k : LANE * (k + 1)]
    for k in range(4 + 3 * blocks, back):
        y_ref[pl.ds(k, devices, stride=back), :] = jnp.zeros((devices, LANE), f32)
    for t in range(devices // 4):
        tile = local_three[:, LANE * t : LANE * (t + 1)]
        t_ref[16 * t : 16 * t + 16, :] = jnp.where(first, tile, pltpu.roll(tile, LANE - PIECE, 1))
    for c in range(chips):
        mine = jnp.where(first, local_one[8 * c : 8 * c + 4, :], local_one[8 * c + 4 : 8 * c + 8, :])
        three = jnp.zeros((4, LANE), f32)
        for q in range(4):
            cols = slice(LANE * q, LANE * (q + 1))
            out_ref[c, PIECE * q : PIECE * (q + 1), :] = local_two[PIECE * c : PIECE * (c + 1), cols].astype(bf16)
            g_ref[4 * q : 4 * q + 4, :] = mine[:, cols]
            moved = t_ref[16 * (c // 2) + 4 * q : 16 * (c // 2) + 4 * q + 4, :]
            if q != 2 * (c % 2):
                moved = pltpu.roll(moved, PIECE * ((q - 2 * (c % 2)) % 4), 1)
            three = jnp.where(lane_group(lanes, q), moved, three)
        out_ref[c, HEAD:TAIL, :] = g_ref[...].astype(bf16)
        start = pl.multiple_of(back * (2 * c + core), SUB)
        y_ref[pl.ds(start, 4), :] = three
        out_ref[c, TAIL:, :] = y_ref[pl.ds(start, back), :].astype(bf16)


def finish_kernel(scale, r_ref, p_ref, w_ref, g_ref, one_ref, two_ref, three_ref, y_ref):
    chips = r_ref.shape[0]
    back = r_ref.shape[1] - TAIL
    blocks = p_ref.shape[0] // chips

    def total(start, stop):
        return sum(r_ref[c, start:stop, :].astype(jnp.float32) for c in range(chips)) * scale

    for q in range(4):
        two_ref[:, LANE * q : LANE * (q + 1)] = total(PIECE * q, PIECE * (q + 1))
    one = total(HEAD, TAIL)
    for q in range(4):
        one_ref[:, LANE * q : LANE * (q + 1)] = one[4 * q : 4 * q + 4, :]
    for c in range(chips):
        y_ref[back * c : back * (c + 1), :] = r_ref[c, TAIL:, :].astype(jnp.float32)
    three = sum(y_ref[back * c : back * c + 4, :] for c in range(chips)) * scale
    for q in range(4):
        three_ref[4 * q : 4 * q + 4, :] = three[:, PIECE * q : PIECE * (q + 1)]
    for f, ref in enumerate((p_ref, w_ref, g_ref)):
        for j in range(blocks):
            ref[chips * j : chips * (j + 1), :] = y_ref[pl.ds(4 + blocks * f + j, chips, stride=back), :]


def fast_body(
    pressure, density, vertical_wind, horizontal_wind, metric_terms, neighbors, level_order, stiffness, coupling,
    weight_one, weight_two, weight_three, pressure_adjoint, wind_adjoint,
):
    levels = devices = level_order.shape[0]
    columns = neighbors.shape[1]
    rows = columns // LANE
    chips = devices // 2
    blocks = rows // chips
    width = blocks * LANE
    hidden = weight_two.shape[1]
    f32, bf16 = jnp.float32, jnp.bfloat16
    same_core = [list(range(core, devices, 2)) for core in range(2)]

    def pad(count):
        return -(-count // SUB) * SUB

    def view(field):
        return field.reshape(rows, LANE)

    def lanes(table):
        return table.reshape(table.shape[0], rows, LANE).transpose(1, 0, 2)

    def exchange(blocks_of_chips):
        return lax.all_to_all(blocks_of_chips, "slab", split_axis=0, concat_axis=0, tiled=True, axis_index_groups=same_core)

    sources = (
        view(pressure), view(density), view(vertical_wind), horizontal_wind.reshape(2, rows, LANE), lanes(metric_terms),
        lanes(neighbors), weight_one, weight_two, weight_three.T, view(pressure_adjoint), view(wind_adjoint),
    )
    rest, back = pad(4 + 6 * blocks), pad(4 + 3 * blocks)
    send = call(
        pack_kernel, "pack", shape((chips, TAIL + rest, LANE), bf16), len(sources),
        [pltpu.VMEM(source.shape, source.dtype) for source in sources]
        + [pltpu.VMEM((16, LANE), f32), pltpu.VMEM((chips * rest, LANE), f32), pltpu.SemaphoreType.DMA((len(sources),))],
        pltpu.HBM,
    )(*sources)
    operators = call(
        operator_kernel, "operators", (shape((levels, levels), bf16), shape((levels, levels), f32), shape((levels, LANE), f32)), 3
    )(level_order.reshape(1, levels), stiffness.reshape(1, levels), coupling.reshape(1, levels))
    mine = exchange(send)
    other = lax.ppermute(mine, "slab", [(i, i ^ 1) for i in range(devices)])
    send_back = call(
        column_kernel, "column_step", shape((chips, TAIL + back, LANE), bf16), 5,
        [
            pltpu.VMEM((devices * (16 + rest), LANE), f32), pltpu.VMEM((16 * devices, LANE), f32),
            pltpu.VMEM((hidden, hidden), bf16), pltpu.VMEM((levels, hidden), f32), pltpu.VMEM((hidden, width), bf16),
            pltpu.VMEM((hidden // 2, width), bf16), pltpu.VMEM((16, LANE), f32), pltpu.VMEM((devices * back, LANE), f32),
            pltpu.VMEM((4 * devices, LANE), f32),
        ],
    )(mine, other, *operators)
    field_out = shape((rows, LANE), f32)
    new_pressure, new_wind, grad, first_grad, second_grad, third_grad = call(
        functools.partial(finish_kernel, 1.0 / math.sqrt(columns)), "finish",
        (
            field_out, field_out, field_out, shape(weight_one.shape, f32), shape(weight_two.shape, f32),
            shape(weight_three.shape[::-1], f32),
        ),
        1,
        [pltpu.VMEM((chips * back, LANE), f32)],
    )(exchange(send_back))
    return (
        new_pressure.reshape(1, columns), new_wind.reshape(1, columns), grad.reshape(1, columns),
        first_grad, second_grad, third_grad.T,
    )


def fits_tiles(*args):
    pressure, level_order, neighbors = args[0], args[6], args[5]
    weight_one, weight_two, weight_three = args[9:12]
    return (
        pressure.shape[0] == 1
        and level_order.shape[0] == 2 * SUB
        and neighbors.shape[1] % (LANE * SUB) == 0
        and weight_one.shape == (4, 4 * LANE)
        and weight_two.shape == (PIECE, 4 * LANE)
        and weight_three.shape == (PIECE, 2 * SUB)
    )


def any_body(*args):
    return (fast_body if fits_tiles(*args) else body)(*args)


def solution(mesh):
    in_specs = (
        P("slab", "date"),
        P("slab", "date"),
        P("slab", "date"),
        P(None, "slab", "date"),
        P(),
        P(),
        P(),
        P(),
        P(),
        P("slab", None),
        P("slab", None),
        P("slab", None),
        P("slab", "date"),
        P("slab", "date"),
    )
    out_specs = (
        P("slab", "date"),
        P("slab", "date"),
        P("slab", "date"),
        P(("date", "slab"), None),
        P(("date", "slab"), None),
        P(("date", "slab"), None),
    )
    return jax.shard_map(any_body, mesh=mesh, in_specs=in_specs, out_specs=out_specs, check_vma=False)
```

```python
import functools
import math

import jax
import jax.numpy as jnp
from jax import lax
from jax.experimental import pallas as pl
from jax.experimental.pallas import tpu as pltpu
from jax.sharding import PartitionSpec as P


def lower_diff(field):
    return jnp.concatenate([field[1:] - field[:-1], -field[-1:]], axis=0)


def upper_diff(field):
    return jnp.concatenate([jnp.zeros_like(field[:1]), field[:-1]], axis=0) - field


def level_inverse(stiffness):
    below = jnp.concatenate([jnp.zeros((1,), jnp.float32), stiffness[:-1]])
    matrix = (
        jnp.diag(1.0 + stiffness + below)
        - jnp.diag(stiffness[:-1], 1)
        - jnp.diag(stiffness[:-1], -1)
    )
    factor = jnp.linalg.cholesky(matrix)
    identity = jnp.eye(stiffness.shape[0], dtype=jnp.float32)
    return jax.scipy.linalg.cho_solve((factor, True), identity)


def apply_inverse(inverse_matrix, rhs):
    return jnp.dot(
        inverse_matrix, rhs, precision=lax.Precision.HIGHEST, preferred_element_type=jnp.float32
    )


def contract_first(left, right):
    return lax.dot_general(
        left, right, (((0,), (0,)), ((), ())), preferred_element_type=jnp.float32
    )


def contract_last(left, right):
    return lax.dot_general(
        left, right, (((1,), (1,)), ((), ())), preferred_element_type=jnp.float32
    )


def body(
    pressure,
    density,
    vertical_wind,
    horizontal_wind,
    metric_terms,
    neighbors,
    level_order,
    stiffness,
    coupling,
    weight_one,
    weight_two,
    weight_three,
    pressure_adjoint,
    wind_adjoint,
):
    east = jnp.take(horizontal_wind[0], neighbors[0], axis=1)
    west = jnp.take(horizontal_wind[0], neighbors[1], axis=1)
    north = jnp.take(horizontal_wind[1], neighbors[2], axis=1)
    south = jnp.take(horizontal_wind[1], neighbors[3], axis=1)
    diverg = metric_terms[0] * (east - west) + metric_terms[1] * (north - south)
    star = pressure - diverg
    inverse = jnp.argsort(level_order)
    scale = 1.0 / math.sqrt(neighbors.shape[1])
    forward_raw = lax.all_to_all(
        jnp.stack([star, density, vertical_wind, diverg]).astype(jnp.bfloat16),
        "slab",
        split_axis=2,
        concat_axis=1,
        tiled=True,
    ).astype(jnp.float32)
    full_one, full_two, full_three = (
        lax.all_gather(weight_one, "slab", axis=0, tiled=True),
        lax.all_gather(weight_two, "slab", axis=0, tiled=True),
        lax.all_gather(weight_three, "slab", axis=0, tiled=True),
    )
    forward_part = jnp.take(forward_raw, inverse, axis=1)
    levels = forward_part.shape[1]
    width = forward_part.shape[2]
    couple = coupling[:, None]
    column_input = forward_part.reshape(4 * levels, width).astype(jnp.bfloat16)
    pre_one = contract_first(full_one, column_input)
    tanh_one = jnp.tanh(pre_one)
    act_one = tanh_one.astype(jnp.bfloat16)
    pre_two = contract_first(full_two, act_one)
    tanh_two = jnp.tanh(pre_two)
    act_two = tanh_two.astype(jnp.bfloat16)
    heating = contract_first(full_three, act_two)
    star_column = forward_part[0]
    rhs = forward_part[2] - couple * lower_diff(star_column) - 0.5 * forward_part[1] + heating
    inverse_matrix = level_inverse(stiffness)
    wind_next = apply_inverse(inverse_matrix, rhs)
    press_next = star_column + upper_diff(couple * wind_next)
    forward_slabs = lax.all_to_all(
        jnp.take(jnp.stack([press_next, wind_next]), level_order, axis=1).astype(jnp.bfloat16),
        "slab",
        split_axis=1,
        concat_axis=2,
        tiled=True,
    ).astype(jnp.float32)
    adjoint_raw = lax.all_to_all(
        jnp.stack([pressure_adjoint, wind_adjoint]), "slab", split_axis=2, concat_axis=1, tiled=True
    )
    adjoint_part = jnp.take(adjoint_raw, inverse, axis=1)
    wind_grad = adjoint_part[1] + couple * lower_diff(adjoint_part[0])
    rhs_grad = apply_inverse(inverse_matrix, wind_grad)
    star_grad = adjoint_part[0] - upper_diff(couple * rhs_grad)
    heat_grad = rhs_grad.astype(jnp.bfloat16)
    local_three = contract_last(act_two, heat_grad) * scale
    back_two = jnp.dot(full_three, heat_grad, preferred_element_type=jnp.float32)
    pre_two_grad = (back_two * (1.0 - tanh_two * tanh_two)).astype(jnp.bfloat16)
    local_two = contract_last(act_one, pre_two_grad) * scale
    back_one = jnp.dot(full_two, pre_two_grad, preferred_element_type=jnp.float32)
    pre_one_grad = (back_one * (1.0 - tanh_one * tanh_one)).astype(jnp.bfloat16)
    local_one = contract_last(column_input, pre_one_grad) * scale
    first_grad, second_grad, third_grad = (
        lax.psum_scatter(local_one, "slab", scatter_dimension=0, tiled=True),
        lax.psum_scatter(local_two, "slab", scatter_dimension=0, tiled=True),
        lax.psum_scatter(local_three, "slab", scatter_dimension=0, tiled=True),
    )
    input_grad = jnp.dot(full_one, pre_one_grad, preferred_element_type=jnp.float32)
    star_grad = star_grad + input_grad[:levels]
    stored_grad = jnp.take(star_grad, level_order, axis=0)
    pressure_new = forward_slabs[0]
    wind_new = forward_slabs[1]
    pressure_grad = lax.all_to_all(
        stored_grad[None].astype(jnp.bfloat16), "slab", split_axis=1, concat_axis=2, tiled=True
    ).astype(jnp.float32)[0]
    return (pressure_new, wind_new, pressure_grad, first_grad, second_grad, third_grad)


LANE = 128
SUB = 8
PIECE = 32
HEAD = 4 * PIECE
TAIL = HEAD + 16


def call(kernel, name, outs, n_in, scratch=(), space=pltpu.VMEM):
    return pl.pallas_call(
        kernel,
        out_shape=outs,
        in_specs=[pl.BlockSpec(memory_space=space) for _ in range(n_in)],
        out_specs=jax.tree.map(lambda _: pl.BlockSpec(memory_space=pltpu.VMEM), outs),
        scratch_shapes=list(scratch),
        compiler_params=pltpu.CompilerParams(vmem_limit_bytes=48 << 20),
        name=name,
    )


def shape(dims, kind):
    return jax.ShapeDtypeStruct(dims, kind)


def difference(table_ref, first, second):
    groups = table_ref.shape[0] // SUB
    sublanes = lax.broadcasted_iota(jnp.int32, (SUB, LANE), 0)
    out = []
    for r in range(SUB):
        kept = []
        for index in (first, second):
            high = jnp.broadcast_to(index[r : r + 1, :] >> 7, (SUB, LANE))
            low = jnp.broadcast_to(index[r : r + 1, :] & (LANE - 1), (SUB, LANE))
            total = jnp.zeros((SUB, LANE), jnp.float32)
            for g in range(groups):
                picked = jnp.take_along_axis(table_ref[SUB * g : SUB * g + SUB, :], low, axis=1, mode="promise_in_bounds")
                total = jnp.where(high == sublanes + SUB * g, picked, total)
            kept.append(total)
        out.append(jnp.sum(kept[0] - kept[1], axis=0, keepdims=True))
    return jnp.concatenate(out, axis=0)


def lane_group(lanes, q):
    return (lanes >= PIECE * q) & (lanes < PIECE * (q + 1))


def pack_kernel(
    p_hbm, d_hbm, w_hbm, u_hbm, m_hbm, n_hbm, one_hbm, two_hbm, three_hbm, pa_hbm, wa_hbm, out_ref,
    p_ref, d_ref, w_ref, u_ref, m_ref, n_ref, one_ref, two_ref, three_ref, pa_ref, wa_ref, part_ref, f_ref, sems,
):
    pairs = (
        (n_hbm, n_ref), (u_hbm, u_ref), (m_hbm, m_ref), (p_hbm, p_ref), (d_hbm, d_ref), (w_hbm, w_ref),
        (pa_hbm, pa_ref), (wa_hbm, wa_ref), (one_hbm, one_ref), (two_hbm, two_ref), (three_hbm, three_ref),
    )
    copies = [pltpu.make_async_copy(source, target, sems.at[i]) for i, (source, target) in enumerate(pairs)]
    for copy in copies:
        copy.start()
    f32, bf16 = jnp.float32, jnp.bfloat16
    chips = out_ref.shape[0]
    rest = out_ref.shape[1] - TAIL
    blocks = p_ref.shape[0] // chips
    for copy in copies:
        copy.wait()

    def put(f, j, tile):
        f_ref[pl.ds(4 + blocks * f + j, chips, stride=rest), :] = tile

    for j in range(blocks):
        rows = slice(SUB * j, SUB * j + SUB)
        along = difference(u_ref.at[0], n_ref[rows, 0, :], n_ref[rows, 1, :])
        across = difference(u_ref.at[1], n_ref[rows, 2, :], n_ref[rows, 3, :])
        diverg = m_ref[rows, 0, :] * along + m_ref[rows, 1, :] * across
        for f, tile in enumerate((p_ref[rows, :] - diverg, d_ref[rows, :], w_ref[rows, :], diverg, pa_ref[rows, :], wa_ref[rows, :])):
            put(f, j, tile)
    lanes = lax.broadcasted_iota(jnp.int32, (PIECE, LANE), 1)
    spread = (lanes % PIECE == lax.broadcasted_iota(jnp.int32, (PIECE, LANE), 0)).astype(f32).astype(bf16)
    part_ref[...] = jnp.dot(three_ref[...], spread, preferred_element_type=f32)
    lanes = lax.broadcasted_iota(jnp.int32, (4, LANE), 1)
    three = jnp.zeros((4, LANE), f32)
    for q in range(4):
        three = jnp.where(lane_group(lanes, q), part_ref[4 * q : 4 * q + 4, :], three)
    one = one_ref[...].astype(f32)
    for q in range(4):
        part_ref[4 * q : 4 * q + 4, :] = one[:, LANE * q : LANE * (q + 1)]
    one = part_ref[...].astype(bf16)
    for c in range(chips):
        for q in range(4):
            out_ref[c, PIECE * q : PIECE * (q + 1), :] = two_ref[:, LANE * q : LANE * (q + 1)]
        out_ref[c, HEAD:TAIL, :] = one
        f_ref[rest * c : rest * c + 4, :] = three
        if rest > 4 + 6 * blocks:
            f_ref[rest * c + 4 + 6 * blocks : rest * (c + 1), :] = jnp.zeros((rest - 4 - 6 * blocks, LANE), f32)
        out_ref[c, TAIL:, :] = f_ref[rest * c : rest * (c + 1), :].astype(bf16)


def shifted_up(field, rows):
    return jnp.where(rows < field.shape[0] - 1, pltpu.roll(field, field.shape[0] - 1, 0), 0.0)


def shifted_down(field, rows):
    return jnp.where(rows > 0, pltpu.roll(field, 1, 0), 0.0)


def operator_inverse(stiff, rows):
    size = stiff.shape[0]
    below = shifted_down(stiff, rows)
    lower, diagonal = -below, 1.0 + stiff + below
    upper = jnp.where(rows < size - 1, -stiff, 0.0)
    right = (rows == lax.broadcasted_iota(jnp.int32, (size, size), 1)).astype(jnp.float32)
    distance = 1
    while distance < size:
        down = lambda v: pltpu.roll(v, distance, 0)
        up = lambda v: pltpu.roll(v, size - distance, 0)
        alpha, gamma = -lower / down(diagonal), -upper / up(diagonal)
        right = right + alpha * down(right) + gamma * up(right)
        diagonal = diagonal + alpha * down(upper) + gamma * up(lower)
        lower, upper = alpha * down(lower), gamma * up(upper)
        distance *= 2
    return right / diagonal


def operator_kernel(order_ref, stiff_ref, couple_ref, place_ref, inverse_ref, column_ref):
    levels = inverse_ref.shape[0]
    rows = lax.broadcasted_iota(jnp.int32, (levels, levels), 0)
    diagonal = rows == lax.broadcasted_iota(jnp.int32, (levels, levels), 1)
    place_ref[...] = (order_ref[...] == rows).astype(jnp.float32).astype(jnp.bfloat16)
    stiff = jnp.sum(jnp.where(diagonal, stiff_ref[...], 0.0), axis=1, keepdims=True)
    couple = jnp.sum(jnp.where(diagonal, couple_ref[...], 0.0), axis=1, keepdims=True)
    inverse_ref[...] = operator_inverse(jnp.broadcast_to(stiff, (levels, levels)), rows)
    column_ref[...] = jnp.broadcast_to(couple, column_ref.shape)


def column_kernel(
    mine_ref, other_ref, place_ref, inverse_ref, column_ref, out_ref,
    a_ref, one_ref, w2_ref, w3_ref, act_ref, sel_ref, g_ref, y_ref, t_ref,
):
    f32, bf16 = jnp.float32, jnp.bfloat16
    core = lax.axis_index("slab") % 2
    first = core == 0
    chips = mine_ref.shape[0]
    devices = 2 * chips
    levels = inverse_ref.shape[0]
    width = act_ref.shape[1]
    blocks = width // LANE
    stride = mine_ref.shape[1] - HEAD
    for ref, which in ((mine_ref, core), (other_ref, 1 - core)):
        for c in range(chips):
            for q in range(4):
                rows = pl.ds(pl.multiple_of(2 * PIECE * c + PIECE * which, PIECE), PIECE)
                w2_ref[rows, LANE * q : LANE * (q + 1)] = ref[c, PIECE * q : PIECE * (q + 1), :]
            rows = pl.ds(pl.multiple_of(stride * (2 * c + which), SUB), stride)
            a_ref[rows, :] = ref[c, HEAD:, :].astype(f32)
    for q in range(4):
        for r in range(4):
            one_ref[pl.ds(4 * devices * q + r, devices, stride=4), :] = a_ref[pl.ds(4 * q + r, devices, stride=stride), :]
    one = jnp.concatenate([one_ref[4 * devices * q : 4 * devices * (q + 1), :] for q in range(4)], axis=1)
    lanes = lax.broadcasted_iota(jnp.int32, (4, LANE), 1)
    for t in range(devices // 4):
        packed = [a_ref[stride * (4 * t + s) + 16 : stride * (4 * t + s) + 20, :] for s in range(4)]
        for q in range(4):
            tile = jnp.zeros((4, LANE), f32)
            for s in range(4):
                moved = packed[s] if s == q else pltpu.roll(packed[s], PIECE * ((s - q) % 4), 1)
                tile = jnp.where(lane_group(lanes, s), moved, tile)
            w3_ref[4 * q : 4 * q + 4, LANE * t : LANE * (t + 1)] = tile
    w1t = one.T.astype(bf16)
    w1s = one[:levels, :].astype(bf16)
    w2 = w2_ref[...]
    w3t = w3_ref[...].astype(bf16)
    w3 = w3_ref[...].T.astype(bf16)
    place, inverse = place_ref[...], inverse_ref[...]
    raw = jnp.concatenate([a_ref[pl.ds(20 + k, levels, stride=stride), :] for k in range(6 * blocks)], axis=1)
    ordered = jnp.dot(place, raw.astype(bf16), preferred_element_type=f32)
    star, density, vertical, diverg, pressure_adjoint, wind_adjoint = (
        ordered[:, width * i : width * (i + 1)] for i in range(6)
    )
    couple = jnp.concatenate([column_ref[...]] * blocks, axis=1)
    rows = lax.broadcasted_iota(jnp.int32, (levels, width), 0)

    def solve(right):
        return jnp.dot(inverse, right, precision=lax.Precision.HIGHEST, preferred_element_type=f32)

    def lower(field):
        return shifted_up(field, rows) - field

    def upper(field):
        return shifted_down(field, rows) - field

    column_input = jnp.concatenate([star, density, vertical, diverg], axis=0).astype(bf16)
    tanh_one = jnp.tanh(jnp.dot(w1t, column_input, preferred_element_type=f32))
    act_one = tanh_one.astype(bf16)
    act_ref[...] = act_one
    rhs_grad = solve(wind_adjoint + couple * lower(pressure_adjoint))
    star_part = pressure_adjoint - upper(couple * rhs_grad)
    heat_grad = rhs_grad.astype(bf16)
    tanh_two = jnp.tanh(contract_first(w2, act_one))
    act_two = tanh_two.astype(bf16)
    back_two = jnp.dot(w3, heat_grad, preferred_element_type=f32)
    pre_two_grad = (back_two * (1.0 - tanh_two * tanh_two)).astype(bf16)
    back_one = jnp.dot(w2, pre_two_grad, preferred_element_type=f32)
    pre_one_grad = (back_one * (1.0 - tanh_one * tanh_one)).astype(bf16)
    heating = jnp.dot(w3t, act_two, preferred_element_type=f32)
    wind_next = solve(vertical - couple * lower(star) - 0.5 * density + heating)
    press_next = star + upper(couple * wind_next)
    star_grad = star_part + jnp.dot(w1s, pre_one_grad, preferred_element_type=f32)
    for c in range(chips):
        rows = pl.ds(pl.multiple_of(2 * PIECE * c + PIECE * core, PIECE), PIECE)
        sel_ref[PIECE * c : PIECE * (c + 1), :] = act_ref[rows, :]
    local_two = contract_last(sel_ref[...], pre_two_grad)
    local_three = contract_last(heat_grad, act_two)
    local_one = contract_last(column_input, pre_one_grad)
    fields = jnp.concatenate([press_next, wind_next, star_grad], axis=1).astype(bf16)
    stored = lax.dot_general(place, fields, (((0,), (0,)), ((), ())), preferred_element_type=f32)
    back = out_ref.shape[1] - TAIL
    for k in range(3 * blocks):
        y_ref[pl.ds(4 + k, devices, stride=back), :] = stored[:, LANE * k : LANE * (k + 1)]
    for k in range(4 + 3 * blocks, back):
        y_ref[pl.ds(k, devices, stride=back), :] = jnp.zeros((devices, LANE), f32)
    for t in range(devices // 4):
        tile = local_three[:, LANE * t : LANE * (t + 1)]
        t_ref[16 * t : 16 * t + 16, :] = jnp.where(first, tile, pltpu.roll(tile, LANE - PIECE, 1))
    for c in range(chips):
        mine = jnp.where(first, local_one[8 * c : 8 * c + 4, :], local_one[8 * c + 4 : 8 * c + 8, :])
        three = jnp.zeros((4, LANE), f32)
        for q in range(4):
            cols = slice(LANE * q, LANE * (q + 1))
            out_ref[c, PIECE * q : PIECE * (q + 1), :] = local_two[PIECE * c : PIECE * (c + 1), cols].astype(bf16)
            g_ref[4 * q : 4 * q + 4, :] = mine[:, cols]
            moved = t_ref[16 * (c // 2) + 4 * q : 16 * (c // 2) + 4 * q + 4, :]
            if q != 2 * (c % 2):
                moved = pltpu.roll(moved, PIECE * ((q - 2 * (c % 2)) % 4), 1)
            three = jnp.where(lane_group(lanes, q), moved, three)
        out_ref[c, HEAD:TAIL, :] = g_ref[...].astype(bf16)
        start = pl.multiple_of(back * (2 * c + core), SUB)
        y_ref[pl.ds(start, 4), :] = three
        out_ref[c, TAIL:, :] = y_ref[pl.ds(start, back), :].astype(bf16)


def finish_kernel(scale, r_ref, p_ref, w_ref, g_ref, one_ref, two_ref, three_ref, y_ref):
    chips = r_ref.shape[0]
    back = r_ref.shape[1] - TAIL
    blocks = p_ref.shape[0] // chips

    def total(start, stop):
        return sum(r_ref[c, start:stop, :].astype(jnp.float32) for c in range(chips)) * scale

    for q in range(4):
        two_ref[:, LANE * q : LANE * (q + 1)] = total(PIECE * q, PIECE * (q + 1))
    one = total(HEAD, TAIL)
    for q in range(4):
        one_ref[:, LANE * q : LANE * (q + 1)] = one[4 * q : 4 * q + 4, :]
    for c in range(chips):
        y_ref[back * c : back * (c + 1), :] = r_ref[c, TAIL:, :].astype(jnp.float32)
    three = sum(y_ref[back * c : back * c + 4, :] for c in range(chips)) * scale
    for q in range(4):
        three_ref[4 * q : 4 * q + 4, :] = three[:, PIECE * q : PIECE * (q + 1)]
    for f, ref in enumerate((p_ref, w_ref, g_ref)):
        for j in range(blocks):
            ref[chips * j : chips * (j + 1), :] = y_ref[pl.ds(4 + blocks * f + j, chips, stride=back), :]


def fast_body(
    pressure, density, vertical_wind, horizontal_wind, metric_terms, neighbors, level_order, stiffness, coupling,
    weight_one, weight_two, weight_three, pressure_adjoint, wind_adjoint,
):
    levels = devices = level_order.shape[0]
    columns = neighbors.shape[1]
    rows = columns // LANE
    chips = devices // 2
    blocks = rows // chips
    width = blocks * LANE
    hidden = weight_two.shape[1]
    f32, bf16 = jnp.float32, jnp.bfloat16
    same_core = [list(range(core, devices, 2)) for core in range(2)]

    def pad(count):
        return -(-count // SUB) * SUB

    def view(field):
        return field.reshape(rows, LANE)

    def lanes(table):
        return table.reshape(table.shape[0], rows, LANE).transpose(1, 0, 2)

    def exchange(blocks_of_chips):
        return lax.all_to_all(blocks_of_chips, "slab", split_axis=0, concat_axis=0, tiled=True, axis_index_groups=same_core)

    sources = (
        view(pressure), view(density), view(vertical_wind), horizontal_wind.reshape(2, rows, LANE), lanes(metric_terms),
        lanes(neighbors), weight_one, weight_two, weight_three.T, view(pressure_adjoint), view(wind_adjoint),
    )
    rest, back = pad(4 + 6 * blocks), pad(4 + 3 * blocks)
    send = call(
        pack_kernel, "pack", shape((chips, TAIL + rest, LANE), bf16), len(sources),
        [pltpu.VMEM(source.shape, source.dtype) for source in sources]
        + [pltpu.VMEM((16, LANE), f32), pltpu.VMEM((chips * rest, LANE), f32), pltpu.SemaphoreType.DMA((len(sources),))],
        pltpu.HBM,
    )(*(pltpu.with_memory_space_constraint(source, pltpu.HBM) for source in sources))
    operators = call(
        operator_kernel, "operators", (shape((levels, levels), bf16), shape((levels, levels), f32), shape((levels, LANE), f32)), 3
    )(level_order.reshape(1, levels), stiffness.reshape(1, levels), coupling.reshape(1, levels))
    mine = exchange(send)
    other = lax.ppermute(mine, "slab", [(i, i ^ 1) for i in range(devices)])
    send_back = call(
        column_kernel, "column_step", shape((chips, TAIL + back, LANE), bf16), 5,
        [
            pltpu.VMEM((devices * (16 + rest), LANE), f32), pltpu.VMEM((16 * devices, LANE), f32),
            pltpu.VMEM((hidden, hidden), bf16), pltpu.VMEM((levels, hidden), f32), pltpu.VMEM((hidden, width), bf16),
            pltpu.VMEM((hidden // 2, width), bf16), pltpu.VMEM((16, LANE), f32), pltpu.VMEM((devices * back, LANE), f32),
            pltpu.VMEM((4 * devices, LANE), f32),
        ],
    )(mine, other, *operators)
    field_out = shape((rows, LANE), f32)
    new_pressure, new_wind, grad, first_grad, second_grad, third_grad = call(
        functools.partial(finish_kernel, 1.0 / math.sqrt(columns)), "finish",
        (
            field_out, field_out, field_out, shape(weight_one.shape, f32), shape(weight_two.shape, f32),
            shape(weight_three.shape[::-1], f32),
        ),
        1,
        [pltpu.VMEM((chips * back, LANE), f32)],
    )(exchange(send_back))
    return (
        new_pressure.reshape(1, columns), new_wind.reshape(1, columns), grad.reshape(1, columns),
        first_grad, second_grad, third_grad.T,
    )


def fits_tiles(*args):
    pressure, level_order, neighbors = args[0], args[6], args[5]
    weight_one, weight_two, weight_three = args[9:12]
    return (
        pressure.shape[0] == 1
        and level_order.shape[0] == 2 * SUB
        and neighbors.shape[1] % (LANE * SUB) == 0
        and weight_one.shape == (4, 4 * LANE)
        and weight_two.shape == (PIECE, 4 * LANE)
        and weight_three.shape == (PIECE, 2 * SUB)
    )


def any_body(*args):
    return (fast_body if fits_tiles(*args) else body)(*args)


def solution(mesh):
    in_specs = (
        P("slab", "date"),
        P("slab", "date"),
        P("slab", "date"),
        P(None, "slab", "date"),
        P(),
        P(),
        P(),
        P(),
        P(),
        P("slab", None),
        P("slab", None),
        P("slab", None),
        P("slab", "date"),
        P("slab", "date"),
    )
    out_specs = (
        P("slab", "date"),
        P("slab", "date"),
        P("slab", "date"),
        P(("date", "slab"), None),
        P(("date", "slab"), None),
        P(("date", "slab"), None),
    )
    return jax.shard_map(any_body, mesh=mesh, in_specs=in_specs, out_specs=out_specs, check_vma=False)
```

```python
import functools
import math

import jax
import jax.numpy as jnp
from jax import lax
from jax.experimental import pallas as pl
from jax.experimental.pallas import tpu as pltpu
from jax.sharding import PartitionSpec as P


def lower_diff(field):
    return jnp.concatenate([field[1:] - field[:-1], -field[-1:]], axis=0)


def upper_diff(field):
    return jnp.concatenate([jnp.zeros_like(field[:1]), field[:-1]], axis=0) - field


def level_inverse(stiffness):
    below = jnp.concatenate([jnp.zeros((1,), jnp.float32), stiffness[:-1]])
    matrix = (
        jnp.diag(1.0 + stiffness + below)
        - jnp.diag(stiffness[:-1], 1)
        - jnp.diag(stiffness[:-1], -1)
    )
    factor = jnp.linalg.cholesky(matrix)
    identity = jnp.eye(stiffness.shape[0], dtype=jnp.float32)
    return jax.scipy.linalg.cho_solve((factor, True), identity)


def apply_inverse(inverse_matrix, rhs):
    return jnp.dot(
        inverse_matrix, rhs, precision=lax.Precision.HIGHEST, preferred_element_type=jnp.float32
    )


def contract_first(left, right):
    return lax.dot_general(
        left, right, (((0,), (0,)), ((), ())), preferred_element_type=jnp.float32
    )


def contract_last(left, right):
    return lax.dot_general(
        left, right, (((1,), (1,)), ((), ())), preferred_element_type=jnp.float32
    )


def body(
    pressure,
    density,
    vertical_wind,
    horizontal_wind,
    metric_terms,
    neighbors,
    level_order,
    stiffness,
    coupling,
    weight_one,
    weight_two,
    weight_three,
    pressure_adjoint,
    wind_adjoint,
):
    east = jnp.take(horizontal_wind[0], neighbors[0], axis=1)
    west = jnp.take(horizontal_wind[0], neighbors[1], axis=1)
    north = jnp.take(horizontal_wind[1], neighbors[2], axis=1)
    south = jnp.take(horizontal_wind[1], neighbors[3], axis=1)
    diverg = metric_terms[0] * (east - west) + metric_terms[1] * (north - south)
    star = pressure - diverg
    inverse = jnp.argsort(level_order)
    scale = 1.0 / math.sqrt(neighbors.shape[1])
    forward_raw = lax.all_to_all(
        jnp.stack([star, density, vertical_wind, diverg]).astype(jnp.bfloat16),
        "slab",
        split_axis=2,
        concat_axis=1,
        tiled=True,
    ).astype(jnp.float32)
    full_one, full_two, full_three = (
        lax.all_gather(weight_one, "slab", axis=0, tiled=True),
        lax.all_gather(weight_two, "slab", axis=0, tiled=True),
        lax.all_gather(weight_three, "slab", axis=0, tiled=True),
    )
    forward_part = jnp.take(forward_raw, inverse, axis=1)
    levels = forward_part.shape[1]
    width = forward_part.shape[2]
    couple = coupling[:, None]
    column_input = forward_part.reshape(4 * levels, width).astype(jnp.bfloat16)
    pre_one = contract_first(full_one, column_input)
    tanh_one = jnp.tanh(pre_one)
    act_one = tanh_one.astype(jnp.bfloat16)
    pre_two = contract_first(full_two, act_one)
    tanh_two = jnp.tanh(pre_two)
    act_two = tanh_two.astype(jnp.bfloat16)
    heating = contract_first(full_three, act_two)
    star_column = forward_part[0]
    rhs = forward_part[2] - couple * lower_diff(star_column) - 0.5 * forward_part[1] + heating
    inverse_matrix = level_inverse(stiffness)
    wind_next = apply_inverse(inverse_matrix, rhs)
    press_next = star_column + upper_diff(couple * wind_next)
    forward_slabs = lax.all_to_all(
        jnp.take(jnp.stack([press_next, wind_next]), level_order, axis=1).astype(jnp.bfloat16),
        "slab",
        split_axis=1,
        concat_axis=2,
        tiled=True,
    ).astype(jnp.float32)
    adjoint_raw = lax.all_to_all(
        jnp.stack([pressure_adjoint, wind_adjoint]), "slab", split_axis=2, concat_axis=1, tiled=True
    )
    adjoint_part = jnp.take(adjoint_raw, inverse, axis=1)
    wind_grad = adjoint_part[1] + couple * lower_diff(adjoint_part[0])
    rhs_grad = apply_inverse(inverse_matrix, wind_grad)
    star_grad = adjoint_part[0] - upper_diff(couple * rhs_grad)
    heat_grad = rhs_grad.astype(jnp.bfloat16)
    local_three = contract_last(act_two, heat_grad) * scale
    back_two = jnp.dot(full_three, heat_grad, preferred_element_type=jnp.float32)
    pre_two_grad = (back_two * (1.0 - tanh_two * tanh_two)).astype(jnp.bfloat16)
    local_two = contract_last(act_one, pre_two_grad) * scale
    back_one = jnp.dot(full_two, pre_two_grad, preferred_element_type=jnp.float32)
    pre_one_grad = (back_one * (1.0 - tanh_one * tanh_one)).astype(jnp.bfloat16)
    local_one = contract_last(column_input, pre_one_grad) * scale
    first_grad, second_grad, third_grad = (
        lax.psum_scatter(local_one, "slab", scatter_dimension=0, tiled=True),
        lax.psum_scatter(local_two, "slab", scatter_dimension=0, tiled=True),
        lax.psum_scatter(local_three, "slab", scatter_dimension=0, tiled=True),
    )
    input_grad = jnp.dot(full_one, pre_one_grad, preferred_element_type=jnp.float32)
    star_grad = star_grad + input_grad[:levels]
    stored_grad = jnp.take(star_grad, level_order, axis=0)
    pressure_new = forward_slabs[0]
    wind_new = forward_slabs[1]
    pressure_grad = lax.all_to_all(
        stored_grad[None].astype(jnp.bfloat16), "slab", split_axis=1, concat_axis=2, tiled=True
    ).astype(jnp.float32)[0]
    return (pressure_new, wind_new, pressure_grad, first_grad, second_grad, third_grad)


LANE = 128
SUB = 8
GROUPS = 4
PIECE = 32
HEAD = 4 * PIECE
TAIL = HEAD + 16


def call(kernel, name, outs, n_in, scratch=(), space=pltpu.VMEM):
    return pl.pallas_call(
        kernel,
        out_shape=outs,
        in_specs=[pl.BlockSpec(memory_space=space) for _ in range(n_in)],
        out_specs=jax.tree.map(lambda _: pl.BlockSpec(memory_space=pltpu.VMEM), outs),
        scratch_shapes=list(scratch),
        compiler_params=pltpu.CompilerParams(vmem_limit_bytes=48 << 20),
        name=name,
    )


def shape(dims, kind):
    return jax.ShapeDtypeStruct(dims, kind)


def difference(table_ref, first, second):
    groups = table_ref.shape[0] // SUB
    sublanes = lax.broadcasted_iota(jnp.int32, (SUB, LANE), 0)
    out = []
    for r in range(SUB):
        kept = []
        for index in (first, second):
            high = jnp.broadcast_to(index[r : r + 1, :] >> 7, (SUB, LANE))
            low = jnp.broadcast_to(index[r : r + 1, :] & (LANE - 1), (SUB, LANE))
            total = jnp.zeros((SUB, LANE), jnp.float32)
            for g in range(groups):
                picked = jnp.take_along_axis(table_ref[SUB * g : SUB * g + SUB, :], low, axis=1, mode="promise_in_bounds")
                total = jnp.where(high == sublanes + SUB * g, picked, total)
            kept.append(total)
        out.append(jnp.sum(kept[0] - kept[1], axis=0, keepdims=True))
    return jnp.concatenate(out, axis=0)


def lane_group(lanes, q):
    return (lanes >= PIECE * q) & (lanes < PIECE * (q + 1))


def pack_kernel(
    p_hbm, d_hbm, w_hbm, u_hbm, m_hbm, n_hbm, one_hbm, two_hbm, three_hbm, pa_hbm, wa_hbm, out_ref,
    p_ref, d_ref, w_ref, u_ref, m_ref, n_ref, one_ref, two_ref, three_ref, pa_ref, wa_ref, part_ref, f_ref, sems,
):
    pairs = (
        (n_hbm, n_ref), (u_hbm, u_ref), (m_hbm, m_ref), (p_hbm, p_ref), (d_hbm, d_ref), (w_hbm, w_ref),
        (pa_hbm, pa_ref), (wa_hbm, wa_ref), (one_hbm, one_ref), (two_hbm, two_ref), (three_hbm, three_ref),
    )
    copies = [pltpu.make_async_copy(source, target, sems.at[i]) for i, (source, target) in enumerate(pairs)]
    for copy in copies:
        copy.start()
    f32, bf16 = jnp.float32, jnp.bfloat16
    chips = out_ref.shape[0]
    piece = f_ref.shape[0] // SUB
    blocks = p_ref.shape[0] // SUB
    for copy in copies:
        copy.wait()

    def put(f, j, tile):
        f_ref[pl.ds(blocks * f + j, SUB, stride=piece), :] = tile

    for j in range(blocks):
        rows = slice(SUB * j, SUB * j + SUB)
        along = difference(u_ref.at[0], n_ref[rows, 0, :], n_ref[rows, 1, :])
        across = difference(u_ref.at[1], n_ref[rows, 2, :], n_ref[rows, 3, :])
        diverg = m_ref[rows, 0, :] * along + m_ref[rows, 1, :] * across
        for f, tile in enumerate((p_ref[rows, :] - diverg, d_ref[rows, :], w_ref[rows, :], diverg, pa_ref[rows, :], wa_ref[rows, :])):
            put(f, j, tile)
    lanes = lax.broadcasted_iota(jnp.int32, (PIECE, LANE), 1)
    spread = (lanes % PIECE == lax.broadcasted_iota(jnp.int32, (PIECE, LANE), 0)).astype(f32).astype(bf16)
    part_ref[...] = jnp.dot(three_ref[...], spread, preferred_element_type=f32)
    lanes = lax.broadcasted_iota(jnp.int32, (4, LANE), 1)
    three = jnp.zeros((4, LANE), f32)
    for q in range(4):
        three = jnp.where(lane_group(lanes, q), part_ref[4 * q : 4 * q + 4, :], three)
    one = one_ref[...].astype(f32)
    for q in range(4):
        part_ref[4 * q : 4 * q + 4, :] = one[:, LANE * q : LANE * (q + 1)]
    one = part_ref[...].astype(bf16)
    for c in range(chips):
        for q in range(4):
            out_ref[c, PIECE * q : PIECE * (q + 1), :] = two_ref[:, LANE * q : LANE * (q + 1)]
        out_ref[c, HEAD:TAIL, :] = one
        f_ref[piece * c + 6 * blocks : piece * c + 6 * blocks + 4, :] = three
        if piece > 6 * blocks + 4:
            f_ref[piece * c + 6 * blocks + 4 : piece * (c + 1), :] = jnp.zeros((piece - 6 * blocks - 4, LANE), f32)
    for g in range(GROUPS):
        both = jnp.concatenate([f_ref[piece * c : piece * (c + 1), :] for c in (g, g + GROUPS)], axis=0).astype(bf16)
        for c in range(g, chips, GROUPS):
            out_ref[c, TAIL:, :] = both


def shifted_up(field, rows):
    return jnp.where(rows < field.shape[0] - 1, pltpu.roll(field, field.shape[0] - 1, 0), 0.0)


def shifted_down(field, rows):
    return jnp.where(rows > 0, pltpu.roll(field, 1, 0), 0.0)


def operator_inverse(stiff, rows):
    size = stiff.shape[0]
    below = shifted_down(stiff, rows)
    lower, diagonal = -below, 1.0 + stiff + below
    upper = jnp.where(rows < size - 1, -stiff, 0.0)
    right = (rows == lax.broadcasted_iota(jnp.int32, (size, size), 1)).astype(jnp.float32)
    distance = 1
    while distance < size:
        down = lambda v: pltpu.roll(v, distance, 0)
        up = lambda v: pltpu.roll(v, size - distance, 0)
        alpha, gamma = -lower / down(diagonal), -upper / up(diagonal)
        right = right + alpha * down(right) + gamma * up(right)
        diagonal = diagonal + alpha * down(upper) + gamma * up(lower)
        lower, upper = alpha * down(lower), gamma * up(upper)
        distance *= 2
    return right / diagonal


def operator_kernel(order_ref, stiff_ref, couple_ref, place_ref, inverse_ref, column_ref):
    levels = inverse_ref.shape[0]
    rows = lax.broadcasted_iota(jnp.int32, (levels, levels), 0)
    diagonal = rows == lax.broadcasted_iota(jnp.int32, (levels, levels), 1)
    place_ref[...] = (order_ref[...] == rows).astype(jnp.float32).astype(jnp.bfloat16)
    stiff = jnp.sum(jnp.where(diagonal, stiff_ref[...], 0.0), axis=1, keepdims=True)
    couple = jnp.sum(jnp.where(diagonal, couple_ref[...], 0.0), axis=1, keepdims=True)
    inverse_ref[...] = operator_inverse(jnp.broadcast_to(stiff, (levels, levels)), rows)
    column_ref[...] = jnp.broadcast_to(couple, column_ref.shape)


def column_kernel(
    mine_ref, other_ref, place_ref, inverse_ref, column_ref, out0_ref, out1_ref, out2_ref, out3_ref,
    a_ref, one_ref, w2_ref, w3_ref, act_ref, sel_ref, g_ref, h_ref, y_ref, t_ref,
):
    f32, bf16 = jnp.float32, jnp.bfloat16
    device = lax.axis_index("slab")
    core = device % 2
    chips = mine_ref.shape[0]
    devices = 2 * chips
    levels = inverse_ref.shape[0]
    width = act_ref.shape[1]
    blocks = width // LANE
    stride = mine_ref.shape[1] - HEAD
    piece = (stride - 16) // 2
    half = blocks // 2
    for ref, which in ((mine_ref, core), (other_ref, 1 - core)):
        for c in range(chips):
            for q in range(4):
                rows = pl.ds(pl.multiple_of(2 * PIECE * c + PIECE * which, PIECE), PIECE)
                w2_ref[rows, LANE * q : LANE * (q + 1)] = ref[c, PIECE * q : PIECE * (q + 1), :]
            rows = pl.ds(pl.multiple_of(stride * (2 * c + which), SUB), stride)
            a_ref[rows, :] = ref[c, HEAD:, :].astype(f32)
    for q in range(4):
        for r in range(4):
            one_ref[pl.ds(4 * devices * q + r, devices, stride=4), :] = a_ref[pl.ds(4 * q + r, devices, stride=stride), :]
    one = jnp.concatenate([one_ref[4 * devices * q : 4 * devices * (q + 1), :] for q in range(4)], axis=1)
    lanes = lax.broadcasted_iota(jnp.int32, (4, LANE), 1)
    for t in range(devices // 4):
        packed = [a_ref[pl.ds(stride * (4 * t + s) + 16 + 6 * half, 4), :] for s in range(4)]
        for q in range(4):
            tile = jnp.zeros((4, LANE), f32)
            for s in range(4):
                moved = packed[s] if s == q else pltpu.roll(packed[s], PIECE * ((s - q) % 4), 1)
                tile = jnp.where(lane_group(lanes, s), moved, tile)
            w3_ref[4 * q : 4 * q + 4, LANE * t : LANE * (t + 1)] = tile
    w1t = one.T.astype(bf16)
    w1s = one[:levels, :].astype(bf16)
    w2 = w2_ref[...]
    w3t = w3_ref[...].astype(bf16)
    w3 = w3_ref[...].T.astype(bf16)
    place, inverse = place_ref[...], inverse_ref[...]
    order = [16 + piece * b + half * f + j for f in range(6) for b in range(2) for j in range(half)]
    raw = jnp.concatenate([a_ref[pl.ds(k, levels, stride=stride), :] for k in order], axis=1)
    ordered = jnp.dot(place, raw.astype(bf16), preferred_element_type=f32)
    star, density, vertical, diverg, pressure_adjoint, wind_adjoint = (
        ordered[:, width * i : width * (i + 1)] for i in range(6)
    )
    couple = jnp.concatenate([column_ref[...]] * blocks, axis=1)
    rows = lax.broadcasted_iota(jnp.int32, (levels, width), 0)

    def solve(right):
        return jnp.dot(inverse, right, precision=lax.Precision.HIGHEST, preferred_element_type=f32)

    def lower(field):
        return shifted_up(field, rows) - field

    def upper(field):
        return shifted_down(field, rows) - field

    column_input = jnp.concatenate([star, density, vertical, diverg], axis=0).astype(bf16)
    tanh_one = jnp.tanh(jnp.dot(w1t, column_input, preferred_element_type=f32))
    act_one = tanh_one.astype(bf16)
    act_ref[...] = act_one
    rhs_grad = solve(wind_adjoint + couple * lower(pressure_adjoint))
    star_part = pressure_adjoint - upper(couple * rhs_grad)
    heat_grad = rhs_grad.astype(bf16)
    tanh_two = jnp.tanh(contract_first(w2, act_one))
    act_two = tanh_two.astype(bf16)
    back_two = jnp.dot(w3, heat_grad, preferred_element_type=f32)
    pre_two_grad = (back_two * (1.0 - tanh_two * tanh_two)).astype(bf16)
    back_one = jnp.dot(w2, pre_two_grad, preferred_element_type=f32)
    pre_one_grad = (back_one * (1.0 - tanh_one * tanh_one)).astype(bf16)
    heating = jnp.dot(w3t, act_two, preferred_element_type=f32)
    wind_next = solve(vertical - couple * lower(star) - 0.5 * density + heating)
    press_next = star + upper(couple * wind_next)
    star_grad = star_part + jnp.dot(w1s, pre_one_grad, preferred_element_type=f32)
    outs = (out0_ref, out1_ref, out2_ref, out3_ref)
    targets = [device ^ (2 * k) for k in range(GROUPS)]
    for k, target in enumerate(targets):
        sel_ref[PIECE * k : PIECE * (k + 1), :] = act_ref[pl.ds(pl.multiple_of(PIECE * target, PIECE), PIECE), :]
    local_two = contract_last(sel_ref[...], pre_two_grad)
    local_three = contract_last(heat_grad, act_two)
    g_ref[...] = contract_last(column_input, pre_one_grad)
    fields = jnp.concatenate([press_next, wind_next, star_grad], axis=1).astype(bf16)
    stored = lax.dot_general(place, fields, (((0,), (0,)), ((), ())), preferred_element_type=f32)
    back = out0_ref.shape[0] - TAIL
    for k in range(3 * blocks):
        y_ref[pl.ds(4 + k, devices, stride=back), :] = stored[:, LANE * k : LANE * (k + 1)]
    for k in range(4 + 3 * blocks, back):
        y_ref[pl.ds(k, devices, stride=back), :] = jnp.zeros((devices, LANE), f32)
    for t in range(devices // 4):
        t_ref[16 * t : 16 * t + 16, :] = local_three[:, LANE * t : LANE * (t + 1)]
    for k, (target, out_ref) in enumerate(zip(targets, outs)):
        pair = g_ref[pl.ds(pl.multiple_of(SUB * (target // 2), SUB), SUB), :]
        one = jnp.where(core == 0, pair[:4, :], pair[4:, :])
        tile = t_ref[pl.ds(pl.multiple_of(16 * (target // 4), 16), 16), :]
        tile = pltpu.roll(tile, (LANE - PIECE * (target % 4)) % LANE, 1)
        three = tile[:4, :]
        for q in range(4):
            cols = slice(LANE * q, LANE * (q + 1))
            out_ref[PIECE * q : PIECE * (q + 1), :] = local_two[PIECE * k : PIECE * (k + 1), cols].astype(bf16)
            h_ref[4 * q : 4 * q + 4, :] = one[:, cols]
            if q > 0:
                three = jnp.where(lane_group(lanes, q), pltpu.roll(tile[4 * q : 4 * q + 4, :], PIECE * q, 1), three)
        out_ref[HEAD:TAIL, :] = h_ref[...].astype(bf16)
        start = pl.multiple_of(back * target, SUB)
        y_ref[pl.ds(start, 4), :] = three
        out_ref[TAIL:, :] = y_ref[pl.ds(start, back), :].astype(bf16)


def finish_kernel(scale, r0_ref, r1_ref, r2_ref, r3_ref, p_ref, w_ref, g_ref, one_ref, two_ref, three_ref, y_ref):
    received = (r0_ref, r1_ref, r2_ref, r3_ref)
    back = r0_ref.shape[0] - TAIL
    half = p_ref.shape[0] // SUB
    group = lax.axis_index("slab") // 2 % GROUPS

    def total(start, stop):
        return sum(ref[start:stop, :].astype(jnp.float32) for ref in received) * scale

    for q in range(4):
        two_ref[:, LANE * q : LANE * (q + 1)] = total(PIECE * q, PIECE * (q + 1))
    one = total(HEAD, TAIL)
    for q in range(4):
        one_ref[:, LANE * q : LANE * (q + 1)] = one[4 * q : 4 * q + 4, :]
    for k, ref in enumerate(received):
        y_ref[pl.ds(pl.multiple_of(back * (group ^ k), SUB), back), :] = ref[TAIL:, :].astype(jnp.float32)
    three = sum(y_ref[back * g : back * g + 4, :] for g in range(GROUPS)) * scale
    for q in range(4):
        three_ref[4 * q : 4 * q + 4, :] = three[:, PIECE * q : PIECE * (q + 1)]
    for f, ref in enumerate((p_ref, w_ref, g_ref)):
        for j in range(half):
            for b in range(2):
                rows = pl.ds(4 + 2 * half * f + half * b + j, GROUPS, stride=back)
                ref[SUB * j + GROUPS * b : SUB * j + GROUPS * (b + 1), :] = y_ref[rows, :]


def fast_body(
    pressure, density, vertical_wind, horizontal_wind, metric_terms, neighbors, level_order, stiffness, coupling,
    weight_one, weight_two, weight_three, pressure_adjoint, wind_adjoint,
):
    levels = devices = level_order.shape[0]
    columns = neighbors.shape[1]
    rows = columns // LANE
    chips = devices // 2
    blocks = rows // GROUPS
    width = blocks * LANE
    hidden = weight_two.shape[1]
    f32, bf16 = jnp.float32, jnp.bfloat16
    same_core = [list(range(core, devices, 2)) for core in range(2)]

    def pad(count):
        return -(-count // SUB) * SUB

    def view(field):
        return field.reshape(rows, LANE)

    def lanes(table):
        return table.reshape(table.shape[0], rows, LANE).transpose(1, 0, 2)

    def exchange(blocks_of_chips):
        return lax.all_to_all(blocks_of_chips, "slab", split_axis=0, concat_axis=0, tiled=True, axis_index_groups=same_core)

    sources = (
        view(pressure), view(density), view(vertical_wind), horizontal_wind.reshape(2, rows, LANE), lanes(metric_terms),
        lanes(neighbors), weight_one, weight_two, weight_three.T, view(pressure_adjoint), view(wind_adjoint),
    )
    piece, back = pad(4 + 3 * blocks), pad(4 + 3 * blocks)
    send = call(
        pack_kernel, "pack", shape((chips, TAIL + 2 * piece, LANE), bf16), len(sources),
        [pltpu.VMEM(source.shape, source.dtype) for source in sources]
        + [pltpu.VMEM((16, LANE), f32), pltpu.VMEM((SUB * piece, LANE), f32), pltpu.SemaphoreType.DMA((len(sources),))],
        pltpu.HBM,
    )(*(pltpu.with_memory_space_constraint(source, pltpu.HBM) for source in sources))
    operators = call(
        operator_kernel, "operators", (shape((levels, levels), bf16), shape((levels, levels), f32), shape((levels, LANE), f32)), 3
    )(level_order.reshape(1, levels), stiffness.reshape(1, levels), coupling.reshape(1, levels))
    mine = exchange(send)
    other = lax.ppermute(mine, "slab", [(i, i ^ 1) for i in range(devices)])
    block = shape((TAIL + back, LANE), bf16)
    send_back = call(
        column_kernel, "column_step", (block,) * GROUPS, 5,
        [
            pltpu.VMEM((devices * (16 + 2 * piece), LANE), f32), pltpu.VMEM((16 * devices, LANE), f32),
            pltpu.VMEM((hidden, hidden), bf16), pltpu.VMEM((levels, hidden), f32), pltpu.VMEM((hidden, width), bf16),
            pltpu.VMEM((GROUPS * PIECE, width), bf16), pltpu.VMEM((4 * levels, hidden), f32), pltpu.VMEM((16, LANE), f32),
            pltpu.VMEM((devices * back, LANE), f32), pltpu.VMEM((4 * devices, LANE), f32),
        ],
    )(mine, other, *operators)
    received = [send_back[0]] + [
        lax.ppermute(send_back[k], "slab", [(i, i ^ (2 * k)) for i in range(devices)]) for k in range(1, GROUPS)
    ]
    field_out = shape((rows, LANE), f32)
    new_pressure, new_wind, grad, first_grad, second_grad, third_grad = call(
        functools.partial(finish_kernel, 1.0 / math.sqrt(columns)), "finish",
        (
            field_out, field_out, field_out, shape(weight_one.shape, f32), shape(weight_two.shape, f32),
            shape(weight_three.shape[::-1], f32),
        ),
        GROUPS,
        [pltpu.VMEM((GROUPS * back, LANE), f32)],
    )(*received)
    return (
        new_pressure.reshape(1, columns), new_wind.reshape(1, columns), grad.reshape(1, columns),
        first_grad, second_grad, third_grad.T,
    )


def fits_tiles(*args):
    pressure, level_order, neighbors = args[0], args[6], args[5]
    weight_one, weight_two, weight_three = args[9:12]
    return (
        pressure.shape[0] == 1
        and level_order.shape[0] == 2 * SUB
        and neighbors.shape[1] % (LANE * SUB) == 0
        and weight_one.shape == (4, 4 * LANE)
        and weight_two.shape == (PIECE, 4 * LANE)
        and weight_three.shape == (PIECE, 2 * SUB)
    )


def any_body(*args):
    return (fast_body if fits_tiles(*args) else body)(*args)


def solution(mesh):
    in_specs = (
        P("slab", "date"),
        P("slab", "date"),
        P("slab", "date"),
        P(None, "slab", "date"),
        P(),
        P(),
        P(),
        P(),
        P(),
        P("slab", None),
        P("slab", None),
        P("slab", None),
        P("slab", "date"),
        P("slab", "date"),
    )
    out_specs = (
        P("slab", "date"),
        P("slab", "date"),
        P("slab", "date"),
        P(("date", "slab"), None),
        P(("date", "slab"), None),
        P(("date", "slab"), None),
    )
    return jax.shard_map(any_body, mesh=mesh, in_specs=in_specs, out_specs=out_specs, check_vma=False)
```

```python
import functools
import math

import jax
import jax.numpy as jnp
from jax import lax
from jax.experimental import pallas as pl
from jax.experimental.pallas import tpu as pltpu
from jax.sharding import PartitionSpec as P


def lower_diff(field):
    return jnp.concatenate([field[1:] - field[:-1], -field[-1:]], axis=0)


def upper_diff(field):
    return jnp.concatenate([jnp.zeros_like(field[:1]), field[:-1]], axis=0) - field


def level_inverse(stiffness):
    below = jnp.concatenate([jnp.zeros((1,), jnp.float32), stiffness[:-1]])
    matrix = (
        jnp.diag(1.0 + stiffness + below)
        - jnp.diag(stiffness[:-1], 1)
        - jnp.diag(stiffness[:-1], -1)
    )
    factor = jnp.linalg.cholesky(matrix)
    identity = jnp.eye(stiffness.shape[0], dtype=jnp.float32)
    return jax.scipy.linalg.cho_solve((factor, True), identity)


def apply_inverse(inverse_matrix, rhs):
    return jnp.dot(
        inverse_matrix, rhs, precision=lax.Precision.HIGHEST, preferred_element_type=jnp.float32
    )


def contract_first(left, right):
    return lax.dot_general(
        left, right, (((0,), (0,)), ((), ())), preferred_element_type=jnp.float32
    )


def contract_last(left, right):
    return lax.dot_general(
        left, right, (((1,), (1,)), ((), ())), preferred_element_type=jnp.float32
    )


def body(
    pressure,
    density,
    vertical_wind,
    horizontal_wind,
    metric_terms,
    neighbors,
    level_order,
    stiffness,
    coupling,
    weight_one,
    weight_two,
    weight_three,
    pressure_adjoint,
    wind_adjoint,
):
    east = jnp.take(horizontal_wind[0], neighbors[0], axis=1)
    west = jnp.take(horizontal_wind[0], neighbors[1], axis=1)
    north = jnp.take(horizontal_wind[1], neighbors[2], axis=1)
    south = jnp.take(horizontal_wind[1], neighbors[3], axis=1)
    diverg = metric_terms[0] * (east - west) + metric_terms[1] * (north - south)
    star = pressure - diverg
    inverse = jnp.argsort(level_order)
    scale = 1.0 / math.sqrt(neighbors.shape[1])
    forward_raw = lax.all_to_all(
        jnp.stack([star, density, vertical_wind, diverg]).astype(jnp.bfloat16),
        "slab",
        split_axis=2,
        concat_axis=1,
        tiled=True,
    ).astype(jnp.float32)
    full_one, full_two, full_three = (
        lax.all_gather(weight_one, "slab", axis=0, tiled=True),
        lax.all_gather(weight_two, "slab", axis=0, tiled=True),
        lax.all_gather(weight_three, "slab", axis=0, tiled=True),
    )
    forward_part = jnp.take(forward_raw, inverse, axis=1)
    levels = forward_part.shape[1]
    width = forward_part.shape[2]
    couple = coupling[:, None]
    column_input = forward_part.reshape(4 * levels, width).astype(jnp.bfloat16)
    pre_one = contract_first(full_one, column_input)
    tanh_one = jnp.tanh(pre_one)
    act_one = tanh_one.astype(jnp.bfloat16)
    pre_two = contract_first(full_two, act_one)
    tanh_two = jnp.tanh(pre_two)
    act_two = tanh_two.astype(jnp.bfloat16)
    heating = contract_first(full_three, act_two)
    star_column = forward_part[0]
    rhs = forward_part[2] - couple * lower_diff(star_column) - 0.5 * forward_part[1] + heating
    inverse_matrix = level_inverse(stiffness)
    wind_next = apply_inverse(inverse_matrix, rhs)
    press_next = star_column + upper_diff(couple * wind_next)
    forward_slabs = lax.all_to_all(
        jnp.take(jnp.stack([press_next, wind_next]), level_order, axis=1).astype(jnp.bfloat16),
        "slab",
        split_axis=1,
        concat_axis=2,
        tiled=True,
    ).astype(jnp.float32)
    adjoint_raw = lax.all_to_all(
        jnp.stack([pressure_adjoint, wind_adjoint]), "slab", split_axis=2, concat_axis=1, tiled=True
    )
    adjoint_part = jnp.take(adjoint_raw, inverse, axis=1)
    wind_grad = adjoint_part[1] + couple * lower_diff(adjoint_part[0])
    rhs_grad = apply_inverse(inverse_matrix, wind_grad)
    star_grad = adjoint_part[0] - upper_diff(couple * rhs_grad)
    heat_grad = rhs_grad.astype(jnp.bfloat16)
    local_three = contract_last(act_two, heat_grad) * scale
    back_two = jnp.dot(full_three, heat_grad, preferred_element_type=jnp.float32)
    pre_two_grad = (back_two * (1.0 - tanh_two * tanh_two)).astype(jnp.bfloat16)
    local_two = contract_last(act_one, pre_two_grad) * scale
    back_one = jnp.dot(full_two, pre_two_grad, preferred_element_type=jnp.float32)
    pre_one_grad = (back_one * (1.0 - tanh_one * tanh_one)).astype(jnp.bfloat16)
    local_one = contract_last(column_input, pre_one_grad) * scale
    first_grad, second_grad, third_grad = (
        lax.psum_scatter(local_one, "slab", scatter_dimension=0, tiled=True),
        lax.psum_scatter(local_two, "slab", scatter_dimension=0, tiled=True),
        lax.psum_scatter(local_three, "slab", scatter_dimension=0, tiled=True),
    )
    input_grad = jnp.dot(full_one, pre_one_grad, preferred_element_type=jnp.float32)
    star_grad = star_grad + input_grad[:levels]
    stored_grad = jnp.take(star_grad, level_order, axis=0)
    pressure_new = forward_slabs[0]
    wind_new = forward_slabs[1]
    pressure_grad = lax.all_to_all(
        stored_grad[None].astype(jnp.bfloat16), "slab", split_axis=1, concat_axis=2, tiled=True
    ).astype(jnp.float32)[0]
    return (pressure_new, wind_new, pressure_grad, first_grad, second_grad, third_grad)


LANE = 128
SUB = 8
GROUPS = 4
PIECE = 32
HEAD = 4 * PIECE
TAIL = HEAD + 16
FRONT = TAIL + 8


def call(kernel, name, outs, n_in, scratch=(), space=pltpu.VMEM):
    return pl.pallas_call(
        kernel,
        out_shape=outs,
        in_specs=[pl.BlockSpec(memory_space=space) for _ in range(n_in)],
        out_specs=jax.tree.map(lambda _: pl.BlockSpec(memory_space=pltpu.VMEM), outs),
        scratch_shapes=list(scratch),
        compiler_params=pltpu.CompilerParams(vmem_limit_bytes=48 << 20),
        name=name,
    )


def shape(dims, kind):
    return jax.ShapeDtypeStruct(dims, kind)


def difference(table_ref, first, second):
    groups = table_ref.shape[0] // SUB
    sublanes = lax.broadcasted_iota(jnp.int32, (SUB, LANE), 0)
    out = []
    for r in range(SUB):
        kept = []
        for index in (first, second):
            high = jnp.broadcast_to(index[r : r + 1, :] >> 7, (SUB, LANE))
            low = jnp.broadcast_to(index[r : r + 1, :] & (LANE - 1), (SUB, LANE))
            total = jnp.zeros((SUB, LANE), jnp.float32)
            for g in range(groups):
                picked = jnp.take_along_axis(table_ref[SUB * g : SUB * g + SUB, :], low, axis=1, mode="promise_in_bounds")
                total = jnp.where(high == sublanes + SUB * g, picked, total)
            kept.append(total)
        out.append(jnp.sum(kept[0] - kept[1], axis=0, keepdims=True))
    return jnp.concatenate(out, axis=0)


def lane_group(lanes, q):
    return (lanes >= PIECE * q) & (lanes < PIECE * (q + 1))


def pack_kernel(
    d_hbm, w_hbm, one_hbm, two_hbm, three_hbm, pa_hbm, wa_hbm, out_ref,
    d_ref, w_ref, one_ref, two_ref, three_ref, pa_ref, wa_ref, part_ref, f_ref, sems,
):
    pairs = (
        (d_hbm, d_ref), (w_hbm, w_ref), (one_hbm, one_ref), (two_hbm, two_ref), (three_hbm, three_ref),
        (pa_hbm, pa_ref), (wa_hbm, wa_ref),
    )
    copies = [pltpu.make_async_copy(source, target, sems.at[i]) for i, (source, target) in enumerate(pairs)]
    for copy in copies:
        copy.start()
    f32, bf16 = jnp.float32, jnp.bfloat16
    chips = out_ref.shape[0]
    half = d_ref.shape[0] // SUB
    piece = 4 * half
    lanes = lax.broadcasted_iota(jnp.int32, (PIECE, LANE), 1)
    spread = (lanes % PIECE == lax.broadcasted_iota(jnp.int32, (PIECE, LANE), 0)).astype(f32).astype(bf16)
    for copy in copies:
        copy.wait()
    for f, field_ref in enumerate((d_ref, w_ref, pa_ref, wa_ref)):
        for j in range(half):
            f_ref[pl.ds(half * f + j, SUB, stride=piece), :] = field_ref[SUB * j : SUB * j + SUB, :]
    part_ref[...] = jnp.dot(three_ref[...], spread, preferred_element_type=f32)
    lanes = lax.broadcasted_iota(jnp.int32, (4, LANE), 1)
    three = jnp.zeros((4, LANE), f32)
    for q in range(4):
        three = jnp.where(lane_group(lanes, q), part_ref[4 * q : 4 * q + 4, :], three)
    one = one_ref[...].astype(f32)
    for q in range(4):
        part_ref[4 * q : 4 * q + 4, :] = one[:, LANE * q : LANE * (q + 1)]
    one = part_ref[...].astype(bf16)
    part_ref[0:4, :] = three
    part_ref[4:8, :] = jnp.zeros((4, LANE), f32)
    three = part_ref[0:8, :].astype(bf16)
    for g in range(GROUPS):
        both = jnp.concatenate([f_ref[piece * c : piece * (c + 1), :] for c in (g, g + GROUPS)], axis=0).astype(bf16)
        for c in range(g, chips, GROUPS):
            for q in range(4):
                out_ref[c, PIECE * q : PIECE * (q + 1), :] = two_ref[:, LANE * q : LANE * (q + 1)]
            out_ref[c, HEAD:TAIL, :] = one
            out_ref[c, TAIL:FRONT, :] = three
            out_ref[c, FRONT:, :] = both


def star_kernel(p_ref, u_ref, m_ref, n_ref, out0_ref, out1_ref, out2_ref, out3_ref, f_ref):
    half = p_ref.shape[0] // SUB
    size = out0_ref.shape[0]
    for j in range(half):
        rows = slice(SUB * j, SUB * j + SUB)
        along = difference(u_ref.at[0], n_ref[rows, 0, :], n_ref[rows, 1, :])
        across = difference(u_ref.at[1], n_ref[rows, 2, :], n_ref[rows, 3, :])
        diverg = m_ref[rows, 0, :] * along + m_ref[rows, 1, :] * across
        for f, tile in enumerate((p_ref[rows, :] - diverg, diverg)):
            for b in range(2):
                place = pl.ds(2 * half * b + half * f + j, GROUPS, stride=size)
                f_ref[place, :] = tile[GROUPS * b : GROUPS * (b + 1), :]
    group = lax.axis_index("slab") // 2 % GROUPS
    for k, out_ref in enumerate((out0_ref, out1_ref, out2_ref, out3_ref)):
        out_ref[...] = f_ref[pl.ds(pl.multiple_of(size * (group ^ k), SUB), size), :].astype(jnp.bfloat16)


def join_kernel(r0_ref, r1_ref, r2_ref, r3_ref, out_ref, f_ref):
    size = r0_ref.shape[0]
    group = lax.axis_index("slab") // 2 % GROUPS
    for k, ref in enumerate((r0_ref, r1_ref, r2_ref, r3_ref)):
        f_ref[pl.ds(pl.multiple_of(size * (group ^ k), SUB), size), :] = ref[...].astype(jnp.float32)
    out_ref[...] = f_ref[...].astype(jnp.bfloat16)


def shifted_up(field, rows):
    return jnp.where(rows < field.shape[0] - 1, pltpu.roll(field, field.shape[0] - 1, 0), 0.0)


def shifted_down(field, rows):
    return jnp.where(rows > 0, pltpu.roll(field, 1, 0), 0.0)


def operator_inverse(stiff, rows):
    size = stiff.shape[0]
    below = shifted_down(stiff, rows)
    lower, diagonal = -below, 1.0 + stiff + below
    upper = jnp.where(rows < size - 1, -stiff, 0.0)
    right = (rows == lax.broadcasted_iota(jnp.int32, (size, size), 1)).astype(jnp.float32)
    distance = 1
    while distance < size:
        down = lambda v: pltpu.roll(v, distance, 0)
        up = lambda v: pltpu.roll(v, size - distance, 0)
        alpha, gamma = -lower / down(diagonal), -upper / up(diagonal)
        right = right + alpha * down(right) + gamma * up(right)
        diagonal = diagonal + alpha * down(upper) + gamma * up(lower)
        lower, upper = alpha * down(lower), gamma * up(upper)
        distance *= 2
    return right / diagonal


def operator_kernel(order_ref, stiff_ref, couple_ref, place_ref, inverse_ref, column_ref):
    levels = inverse_ref.shape[0]
    rows = lax.broadcasted_iota(jnp.int32, (levels, levels), 0)
    diagonal = rows == lax.broadcasted_iota(jnp.int32, (levels, levels), 1)
    place_ref[...] = (order_ref[...] == rows).astype(jnp.float32).astype(jnp.bfloat16)
    stiff = jnp.sum(jnp.where(diagonal, stiff_ref[...], 0.0), axis=1, keepdims=True)
    couple = jnp.sum(jnp.where(diagonal, couple_ref[...], 0.0), axis=1, keepdims=True)
    inverse_ref[...] = operator_inverse(jnp.broadcast_to(stiff, (levels, levels)), rows)
    column_ref[...] = jnp.broadcast_to(couple, column_ref.shape)


def column_kernel(
    mine_ref, other_ref, near_ref, far_ref, near_other_ref, far_other_ref, place_ref, inverse_ref, column_ref,
    out0_ref, out1_ref, out2_ref, out3_ref, x_ref, a_ref, one_ref, w2_ref, w3_ref, act_ref, sel_ref, g_ref, h_ref, y_ref, t_ref, act2_ref, sel2_ref,
):
    f32, bf16 = jnp.float32, jnp.bfloat16
    device = lax.axis_index("slab")
    core = device % 2
    chips = mine_ref.shape[0]
    devices = 2 * chips
    levels = inverse_ref.shape[0]
    width = act_ref.shape[1]
    blocks = width // LANE
    stride = mine_ref.shape[1] - HEAD
    half = blocks // 2
    upper_half = device // SUB
    for ref, which in ((mine_ref, core), (other_ref, 1 - core)):
        for c in range(chips):
            for q in range(4):
                rows = pl.ds(pl.multiple_of(2 * PIECE * c + PIECE * which, PIECE), PIECE)
                w2_ref[rows, LANE * q : LANE * (q + 1)] = ref[c, PIECE * q : PIECE * (q + 1), :]
            rows = pl.ds(pl.multiple_of(stride * (2 * c + which), SUB), stride)
            a_ref[rows, :] = ref[c, HEAD:, :].astype(f32)
    for q in range(4):
        for r in range(4):
            one_ref[pl.ds(4 * devices * q + r, devices, stride=4), :] = a_ref[pl.ds(4 * q + r, devices, stride=stride), :]
    one = jnp.concatenate([one_ref[4 * devices * q : 4 * devices * (q + 1), :] for q in range(4)], axis=1)
    lanes = lax.broadcasted_iota(jnp.int32, (4, LANE), 1)
    for t in range(devices // 4):
        packed = [a_ref[stride * (4 * t + s) + 16 : stride * (4 * t + s) + 20, :] for s in range(4)]
        for q in range(4):
            tile = jnp.zeros((4, LANE), f32)
            for s in range(4):
                moved = packed[s] if s == q else pltpu.roll(packed[s], PIECE * ((s - q) % 4), 1)
                tile = jnp.where(lane_group(lanes, s), moved, tile)
            w3_ref[4 * q : 4 * q + 4, LANE * t : LANE * (t + 1)] = tile
    w1t = one.T.astype(bf16)
    w1s = one[:levels, :].astype(bf16)
    w2 = w2_ref[...]
    w3t = w3_ref[...].astype(bf16)
    w3 = w3_ref[...].T.astype(bf16)
    place, inverse = place_ref[...], inverse_ref[...]
    size = near_ref.shape[0] // GROUPS
    for ref, side, which in (
        (near_ref, upper_half, core), (far_ref, 1 - upper_half, core),
        (near_other_ref, upper_half, 1 - core), (far_other_ref, 1 - upper_half, 1 - core),
    ):
        for g in range(GROUPS):
            start = pl.multiple_of(size * (SUB * side + 2 * g + which), SUB)
            x_ref[pl.ds(start, size), :] = ref[size * g : size * (g + 1), :].astype(f32)

    def late(f):
        return [x_ref[pl.ds(2 * half * b + half * f + j, levels, stride=size), :] for b in range(2) for j in range(half)]

    def early(f):
        start = 24 + half * f
        return [a_ref[pl.ds(start + 4 * half * b + j, levels, stride=stride), :] for b in range(2) for j in range(half)]

    raw = jnp.concatenate(late(0) + early(0) + early(1) + late(1) + early(2) + early(3), axis=1)
    ordered = jnp.dot(place, raw.astype(bf16), preferred_element_type=f32)
    star, density, vertical, diverg, pressure_adjoint, wind_adjoint = (
        ordered[:, width * i : width * (i + 1)] for i in range(6)
    )
    couple = jnp.concatenate([column_ref[...]] * blocks, axis=1)
    rows = lax.broadcasted_iota(jnp.int32, (levels, width), 0)

    def solve(right):
        return jnp.dot(inverse, right, precision=lax.Precision.HIGHEST, preferred_element_type=f32)

    def lower(field):
        return shifted_up(field, rows) - field

    def upper(field):
        return shifted_down(field, rows) - field

    column_input = jnp.concatenate([star, density, vertical, diverg], axis=0).astype(bf16)
    tanh_one = jnp.tanh(jnp.dot(w1t, column_input, preferred_element_type=f32))
    act_one = tanh_one.astype(bf16)
    act_ref[...] = act_one
    rhs_grad = solve(wind_adjoint + couple * lower(pressure_adjoint))
    star_part = pressure_adjoint - upper(couple * rhs_grad)
    heat_grad = rhs_grad.astype(bf16)
    tanh_two = jnp.tanh(contract_first(w2, act_one))
    act_two = tanh_two.astype(bf16)
    act2_ref[...] = act_two
    back_two = jnp.dot(w3, heat_grad, preferred_element_type=f32)
    pre_two_grad = (back_two * (1.0 - tanh_two * tanh_two)).astype(bf16)
    back_one = jnp.dot(w2, pre_two_grad, preferred_element_type=f32)
    pre_one_grad = (back_one * (1.0 - tanh_one * tanh_one)).astype(bf16)
    heating = jnp.dot(w3t, act_two, preferred_element_type=f32)
    wind_next = solve(vertical - couple * lower(star) - 0.5 * density + heating)
    press_next = star + upper(couple * wind_next)
    star_grad = star_part + jnp.dot(w1s, pre_one_grad, preferred_element_type=f32)
    outs = (out0_ref, out1_ref, out2_ref, out3_ref)
    targets = [device ^ (2 * k) for k in range(GROUPS)]
    for k, target in enumerate(targets):
        hid = pl.ds(pl.multiple_of(PIECE * target, PIECE), PIECE)
        sel_ref[PIECE * k : PIECE * (k + 1), :] = act_ref[hid, :]
        sel2_ref[PIECE * k : PIECE * (k + 1), :] = act2_ref[hid, :]
    local_two = contract_last(sel_ref[...], pre_two_grad)
    local_three = contract_last(heat_grad, sel2_ref[...])
    g_ref[...] = contract_last(column_input, pre_one_grad)
    fields = jnp.concatenate([press_next, wind_next, star_grad], axis=1).astype(bf16)
    stored = lax.dot_general(place, fields, (((0,), (0,)), ((), ())), preferred_element_type=f32)
    back = out0_ref.shape[0] - TAIL
    for k in range(3 * blocks):
        y_ref[pl.ds(4 + k, devices, stride=back), :] = stored[:, LANE * k : LANE * (k + 1)]
    for k in range(4 + 3 * blocks, back):
        y_ref[pl.ds(k, devices, stride=back), :] = jnp.zeros((devices, LANE), f32)
    t_ref[...] = local_three
    for k, (target, out_ref) in enumerate(zip(targets, outs)):
        pair = g_ref[pl.ds(pl.multiple_of(SUB * (target // 2), SUB), SUB), :]
        one = jnp.where(core == 0, pair[:4, :], pair[4:, :])
        tile = t_ref[...] if k == 0 else pltpu.roll(t_ref[...], LANE - PIECE * k, 1)
        three = tile[:4, :]
        for q in range(4):
            cols = slice(LANE * q, LANE * (q + 1))
            out_ref[PIECE * q : PIECE * (q + 1), :] = local_two[PIECE * k : PIECE * (k + 1), cols].astype(bf16)
            h_ref[4 * q : 4 * q + 4, :] = one[:, cols]
            if q > 0:
                three = jnp.where(lane_group(lanes, q), pltpu.roll(tile[4 * q : 4 * q + 4, :], PIECE * q, 1), three)
        out_ref[HEAD:TAIL, :] = h_ref[...].astype(bf16)
        start = pl.multiple_of(back * target, SUB)
        y_ref[pl.ds(start, 4), :] = three
        out_ref[TAIL:, :] = y_ref[pl.ds(start, back), :].astype(bf16)


def finish_kernel(scale, r0_ref, r1_ref, r2_ref, r3_ref, p_ref, w_ref, g_ref, one_ref, two_ref, three_ref, y_ref):
    received = (r0_ref, r1_ref, r2_ref, r3_ref)
    back = r0_ref.shape[0] - TAIL
    half = p_ref.shape[0] // SUB
    group = lax.axis_index("slab") // 2 % GROUPS

    def total(start, stop):
        return sum(ref[start:stop, :].astype(jnp.float32) for ref in received) * scale

    for q in range(4):
        two_ref[:, LANE * q : LANE * (q + 1)] = total(PIECE * q, PIECE * (q + 1))
    one = total(HEAD, TAIL)
    for q in range(4):
        one_ref[:, LANE * q : LANE * (q + 1)] = one[4 * q : 4 * q + 4, :]
    for k, ref in enumerate(received):
        y_ref[pl.ds(pl.multiple_of(back * (group ^ k), SUB), back), :] = ref[TAIL:, :].astype(jnp.float32)
    three = sum(y_ref[back * g : back * g + 4, :] for g in range(GROUPS)) * scale
    for q in range(4):
        three_ref[4 * q : 4 * q + 4, :] = three[:, PIECE * q : PIECE * (q + 1)]
    for f, ref in enumerate((p_ref, w_ref, g_ref)):
        for j in range(half):
            for b in range(2):
                rows = pl.ds(4 + 2 * half * f + half * b + j, GROUPS, stride=back)
                ref[SUB * j + GROUPS * b : SUB * j + GROUPS * (b + 1), :] = y_ref[rows, :]


def fast_body(
    pressure, density, vertical_wind, horizontal_wind, metric_terms, neighbors, level_order, stiffness, coupling,
    weight_one, weight_two, weight_three, pressure_adjoint, wind_adjoint,
):
    levels = devices = level_order.shape[0]
    columns = neighbors.shape[1]
    rows = columns // LANE
    chips = devices // 2
    blocks = rows // GROUPS
    width = blocks * LANE
    hidden = weight_two.shape[1]
    f32, bf16 = jnp.float32, jnp.bfloat16
    same_core = [list(range(core, devices, 2)) for core in range(2)]

    def pad(count):
        return -(-count // SUB) * SUB

    def view(field):
        return field.reshape(rows, LANE)

    def lanes(table):
        return table.reshape(table.shape[0], rows, LANE).transpose(1, 0, 2)

    def exchange(blocks_of_chips):
        return lax.all_to_all(blocks_of_chips, "slab", split_axis=0, concat_axis=0, tiled=True, axis_index_groups=same_core)

    def swap(array, bits):
        return lax.ppermute(array, "slab", [(i, i ^ bits) for i in range(devices)])

    def among_groups(outgoing):
        return [outgoing[0]] + [swap(outgoing[k], 2 * k) for k in range(1, GROUPS)]

    sources = (
        view(density), view(vertical_wind), weight_one, weight_two, weight_three.T, view(pressure_adjoint), view(wind_adjoint),
    )
    half = rows // SUB
    back = pad(4 + 3 * blocks)
    send = call(
        pack_kernel, "pack", shape((chips, FRONT + 8 * half, LANE), bf16), len(sources),
        [pltpu.VMEM(source.shape, source.dtype) for source in sources]
        + [pltpu.VMEM((16, LANE), f32), pltpu.VMEM((SUB * 4 * half, LANE), f32), pltpu.SemaphoreType.DMA((len(sources),))],
        pltpu.HBM,
    )(*(pltpu.with_memory_space_constraint(source, pltpu.HBM) for source in sources))
    star_block, join_scratch = shape((4 * half, LANE), bf16), pltpu.VMEM((GROUPS * 4 * half, LANE), f32)
    star_send = call(star_kernel, "star", (star_block,) * GROUPS, 4, [join_scratch])(
        view(pressure), horizontal_wind.reshape(2, rows, LANE), lanes(metric_terms), lanes(neighbors)
    )
    mine = exchange(send)
    near = call(join_kernel, "join", shape((GROUPS * 4 * half, LANE), bf16), GROUPS, [join_scratch])(*among_groups(star_send))
    far = swap(near, SUB)
    mine, far = lax.optimization_barrier((mine, far))
    other, near_other, far_other = swap(mine, 1), swap(near, 1), swap(far, 1)
    operators = call(
        operator_kernel, "operators", (shape((levels, levels), bf16), shape((levels, levels), f32), shape((levels, LANE), f32)), 3
    )(level_order.reshape(1, levels), stiffness.reshape(1, levels), coupling.reshape(1, levels))
    block = shape((TAIL + back, LANE), bf16)
    send_back = call(
        column_kernel, "column_step", (block,) * GROUPS, 9,
        [
            pltpu.VMEM((devices * 4 * half, LANE), f32), pltpu.VMEM((devices * (FRONT - HEAD + 8 * half), LANE), f32), pltpu.VMEM((16 * devices, LANE), f32),
            pltpu.VMEM((hidden, hidden), bf16), pltpu.VMEM((levels, hidden), f32), pltpu.VMEM((hidden, width), bf16),
            pltpu.VMEM((GROUPS * PIECE, width), bf16), pltpu.VMEM((4 * levels, hidden), f32), pltpu.VMEM((16, LANE), f32),
            pltpu.VMEM((devices * back, LANE), f32), pltpu.VMEM((levels, LANE), f32),
            pltpu.VMEM((hidden, width), bf16), pltpu.VMEM((GROUPS * PIECE, width), bf16),
        ],
    )(mine, other, near, far, near_other, far_other, *operators)
    received = among_groups(send_back)
    field_out = shape((rows, LANE), f32)
    new_pressure, new_wind, grad, first_grad, second_grad, third_grad = call(
        functools.partial(finish_kernel, 1.0 / math.sqrt(columns)), "finish",
        (
            field_out, field_out, field_out, shape(weight_one.shape, f32), shape(weight_two.shape, f32),
            shape(weight_three.shape[::-1], f32),
        ),
        GROUPS,
        [pltpu.VMEM((GROUPS * back, LANE), f32)],
    )(*received)
    return (
        new_pressure.reshape(1, columns), new_wind.reshape(1, columns), grad.reshape(1, columns),
        first_grad, second_grad, third_grad.T,
    )


def fits_tiles(*args):
    pressure, level_order, neighbors = args[0], args[6], args[5]
    weight_one, weight_two, weight_three = args[9:12]
    return (
        pressure.shape[0] == 1
        and level_order.shape[0] == 2 * SUB
        and neighbors.shape[1] % (LANE * SUB) == 0
        and weight_one.shape == (4, 4 * LANE)
        and weight_two.shape == (PIECE, 4 * LANE)
        and weight_three.shape == (PIECE, 2 * SUB)
    )


def any_body(*args):
    return (fast_body if fits_tiles(*args) else body)(*args)


def solution(mesh):
    in_specs = (
        P("slab", "date"),
        P("slab", "date"),
        P("slab", "date"),
        P(None, "slab", "date"),
        P(),
        P(),
        P(),
        P(),
        P(),
        P("slab", None),
        P("slab", None),
        P("slab", None),
        P("slab", "date"),
        P("slab", "date"),
    )
    out_specs = (
        P("slab", "date"),
        P("slab", "date"),
        P("slab", "date"),
        P(("date", "slab"), None),
        P(("date", "slab"), None),
        P(("date", "slab"), None),
    )
    return jax.shard_map(any_body, mesh=mesh, in_specs=in_specs, out_specs=out_specs, check_vma=False)
```

```python
import functools
import math

import jax
import jax.numpy as jnp
from jax import lax
from jax.experimental import pallas as pl
from jax.experimental.pallas import tpu as pltpu
from jax.sharding import PartitionSpec as P


def lower_diff(field):
    return jnp.concatenate([field[1:] - field[:-1], -field[-1:]], axis=0)


def upper_diff(field):
    return jnp.concatenate([jnp.zeros_like(field[:1]), field[:-1]], axis=0) - field


def level_inverse(stiffness):
    below = jnp.concatenate([jnp.zeros((1,), jnp.float32), stiffness[:-1]])
    matrix = (
        jnp.diag(1.0 + stiffness + below)
        - jnp.diag(stiffness[:-1], 1)
        - jnp.diag(stiffness[:-1], -1)
    )
    factor = jnp.linalg.cholesky(matrix)
    identity = jnp.eye(stiffness.shape[0], dtype=jnp.float32)
    return jax.scipy.linalg.cho_solve((factor, True), identity)


def apply_inverse(inverse_matrix, rhs):
    return jnp.dot(
        inverse_matrix, rhs, precision=lax.Precision.HIGHEST, preferred_element_type=jnp.float32
    )


def contract_first(left, right):
    return lax.dot_general(
        left, right, (((0,), (0,)), ((), ())), preferred_element_type=jnp.float32
    )


def contract_last(left, right):
    return lax.dot_general(
        left, right, (((1,), (1,)), ((), ())), preferred_element_type=jnp.float32
    )


def body(
    pressure,
    density,
    vertical_wind,
    horizontal_wind,
    metric_terms,
    neighbors,
    level_order,
    stiffness,
    coupling,
    weight_one,
    weight_two,
    weight_three,
    pressure_adjoint,
    wind_adjoint,
):
    east = jnp.take(horizontal_wind[0], neighbors[0], axis=1)
    west = jnp.take(horizontal_wind[0], neighbors[1], axis=1)
    north = jnp.take(horizontal_wind[1], neighbors[2], axis=1)
    south = jnp.take(horizontal_wind[1], neighbors[3], axis=1)
    diverg = metric_terms[0] * (east - west) + metric_terms[1] * (north - south)
    star = pressure - diverg
    inverse = jnp.argsort(level_order)
    scale = 1.0 / math.sqrt(neighbors.shape[1])
    forward_raw = lax.all_to_all(
        jnp.stack([star, density, vertical_wind, diverg]).astype(jnp.bfloat16),
        "slab",
        split_axis=2,
        concat_axis=1,
        tiled=True,
    ).astype(jnp.float32)
    full_one, full_two, full_three = (
        lax.all_gather(weight_one, "slab", axis=0, tiled=True),
        lax.all_gather(weight_two, "slab", axis=0, tiled=True),
        lax.all_gather(weight_three, "slab", axis=0, tiled=True),
    )
    forward_part = jnp.take(forward_raw, inverse, axis=1)
    levels = forward_part.shape[1]
    width = forward_part.shape[2]
    couple = coupling[:, None]
    column_input = forward_part.reshape(4 * levels, width).astype(jnp.bfloat16)
    pre_one = contract_first(full_one, column_input)
    tanh_one = jnp.tanh(pre_one)
    act_one = tanh_one.astype(jnp.bfloat16)
    pre_two = contract_first(full_two, act_one)
    tanh_two = jnp.tanh(pre_two)
    act_two = tanh_two.astype(jnp.bfloat16)
    heating = contract_first(full_three, act_two)
    star_column = forward_part[0]
    rhs = forward_part[2] - couple * lower_diff(star_column) - 0.5 * forward_part[1] + heating
    inverse_matrix = level_inverse(stiffness)
    wind_next = apply_inverse(inverse_matrix, rhs)
    press_next = star_column + upper_diff(couple * wind_next)
    forward_slabs = lax.all_to_all(
        jnp.take(jnp.stack([press_next, wind_next]), level_order, axis=1).astype(jnp.bfloat16),
        "slab",
        split_axis=1,
        concat_axis=2,
        tiled=True,
    ).astype(jnp.float32)
    adjoint_raw = lax.all_to_all(
        jnp.stack([pressure_adjoint, wind_adjoint]), "slab", split_axis=2, concat_axis=1, tiled=True
    )
    adjoint_part = jnp.take(adjoint_raw, inverse, axis=1)
    wind_grad = adjoint_part[1] + couple * lower_diff(adjoint_part[0])
    rhs_grad = apply_inverse(inverse_matrix, wind_grad)
    star_grad = adjoint_part[0] - upper_diff(couple * rhs_grad)
    heat_grad = rhs_grad.astype(jnp.bfloat16)
    local_three = contract_last(act_two, heat_grad) * scale
    back_two = jnp.dot(full_three, heat_grad, preferred_element_type=jnp.float32)
    pre_two_grad = (back_two * (1.0 - tanh_two * tanh_two)).astype(jnp.bfloat16)
    local_two = contract_last(act_one, pre_two_grad) * scale
    back_one = jnp.dot(full_two, pre_two_grad, preferred_element_type=jnp.float32)
    pre_one_grad = (back_one * (1.0 - tanh_one * tanh_one)).astype(jnp.bfloat16)
    local_one = contract_last(column_input, pre_one_grad) * scale
    first_grad, second_grad, third_grad = (
        lax.psum_scatter(local_one, "slab", scatter_dimension=0, tiled=True),
        lax.psum_scatter(local_two, "slab", scatter_dimension=0, tiled=True),
        lax.psum_scatter(local_three, "slab", scatter_dimension=0, tiled=True),
    )
    input_grad = jnp.dot(full_one, pre_one_grad, preferred_element_type=jnp.float32)
    star_grad = star_grad + input_grad[:levels]
    stored_grad = jnp.take(star_grad, level_order, axis=0)
    pressure_new = forward_slabs[0]
    wind_new = forward_slabs[1]
    pressure_grad = lax.all_to_all(
        stored_grad[None].astype(jnp.bfloat16), "slab", split_axis=1, concat_axis=2, tiled=True
    ).astype(jnp.float32)[0]
    return (pressure_new, wind_new, pressure_grad, first_grad, second_grad, third_grad)


LANE = 128
SUB = 8
STRIDE = 104
GROUPS = 4
PIECE = 32
HEAD = 4 * PIECE
TAIL = HEAD + 16


def call(kernel, name, outs, n_in, scratch=(), space=pltpu.VMEM):
    return pl.pallas_call(
        kernel,
        out_shape=outs,
        in_specs=[pl.BlockSpec(memory_space=space) for _ in range(n_in)],
        out_specs=jax.tree.map(lambda _: pl.BlockSpec(memory_space=pltpu.VMEM), outs),
        scratch_shapes=list(scratch),
        compiler_params=pltpu.CompilerParams(vmem_limit_bytes=48 << 20),
        name=name,
    )


def shape(dims, kind):
    return jax.ShapeDtypeStruct(dims, kind)


def difference(table_ref, first, second):
    groups = table_ref.shape[0] // SUB
    sublanes = lax.broadcasted_iota(jnp.int32, (SUB, LANE), 0)
    out = []
    for r in range(SUB):
        kept = []
        for index in (first, second):
            high = jnp.broadcast_to(index[r : r + 1, :] >> 7, (SUB, LANE))
            low = jnp.broadcast_to(index[r : r + 1, :] & (LANE - 1), (SUB, LANE))
            total = jnp.zeros((SUB, LANE), jnp.float32)
            for g in range(groups):
                picked = jnp.take_along_axis(table_ref[SUB * g : SUB * g + SUB, :], low, axis=1, mode="promise_in_bounds")
                total = jnp.where(high == sublanes + SUB * g, picked, total)
            kept.append(total)
        out.append(jnp.sum(kept[0] - kept[1], axis=0, keepdims=True))
    return jnp.concatenate(out, axis=0)


def lane_group(lanes, q):
    return (lanes >= PIECE * q) & (lanes < PIECE * (q + 1))


def pack_kernel(
    p_hbm, d_hbm, w_hbm, u_hbm, m_hbm, n_hbm, one_hbm, two_hbm, three_hbm, pa_hbm, wa_hbm, out_ref,
    p_ref, d_ref, w_ref, u_ref, m_ref, n_ref, one_ref, two_ref, three_ref, pa_ref, wa_ref, part_ref, f_ref, sems,
):
    pairs = (
        (n_hbm, n_ref), (u_hbm, u_ref), (m_hbm, m_ref), (p_hbm, p_ref), (d_hbm, d_ref), (w_hbm, w_ref),
        (pa_hbm, pa_ref), (wa_hbm, wa_ref), (one_hbm, one_ref), (two_hbm, two_ref), (three_hbm, three_ref),
    )
    copies = [pltpu.make_async_copy(source, target, sems.at[i]) for i, (source, target) in enumerate(pairs)]
    for copy in copies:
        copy.start()
    f32, bf16 = jnp.float32, jnp.bfloat16
    chips = out_ref.shape[0]
    piece = f_ref.shape[0] // SUB
    blocks = p_ref.shape[0] // SUB
    for copy in copies:
        copy.wait()

    def put(f, j, tile):
        f_ref[pl.ds(blocks * f + j, SUB, stride=piece), :] = tile

    for j in range(blocks):
        rows = slice(SUB * j, SUB * j + SUB)
        along = difference(u_ref.at[0], n_ref[rows, 0, :], n_ref[rows, 1, :])
        across = difference(u_ref.at[1], n_ref[rows, 2, :], n_ref[rows, 3, :])
        diverg = m_ref[rows, 0, :] * along + m_ref[rows, 1, :] * across
        for f, tile in enumerate((p_ref[rows, :] - diverg, d_ref[rows, :], w_ref[rows, :], diverg, pa_ref[rows, :], wa_ref[rows, :])):
            put(f, j, tile)
    lanes = lax.broadcasted_iota(jnp.int32, (PIECE, LANE), 1)
    spread = (lanes % PIECE == lax.broadcasted_iota(jnp.int32, (PIECE, LANE), 0)).astype(f32).astype(bf16)
    part_ref[...] = jnp.dot(three_ref[...], spread, preferred_element_type=f32)
    lanes = lax.broadcasted_iota(jnp.int32, (4, LANE), 1)
    three = jnp.zeros((4, LANE), f32)
    for q in range(4):
        three = jnp.where(lane_group(lanes, q), part_ref[4 * q : 4 * q + 4, :], three)
    one = one_ref[...].astype(f32)
    for q in range(4):
        part_ref[4 * q : 4 * q + 4, :] = one[:, LANE * q : LANE * (q + 1)]
    one = part_ref[...].astype(bf16)
    for c in range(chips):
        for q in range(4):
            out_ref[c, PIECE * q : PIECE * (q + 1), :] = two_ref[:, LANE * q : LANE * (q + 1)]
        out_ref[c, HEAD:TAIL, :] = one
        f_ref[piece * c + 6 * blocks : piece * c + 6 * blocks + 4, :] = three
        if piece > 6 * blocks + 4:
            f_ref[piece * c + 6 * blocks + 4 : piece * (c + 1), :] = jnp.zeros((piece - 6 * blocks - 4, LANE), f32)
    for g in range(GROUPS):
        both = jnp.concatenate([f_ref[piece * c : piece * (c + 1), :] for c in (g, g + GROUPS)], axis=0).astype(bf16)
        for c in range(g, chips, GROUPS):
            out_ref[c, TAIL:, :] = both


def shifted_up(field, rows):
    return jnp.where(rows < field.shape[0] - 1, pltpu.roll(field, field.shape[0] - 1, 0), 0.0)


def shifted_down(field, rows):
    return jnp.where(rows > 0, pltpu.roll(field, 1, 0), 0.0)


def operator_inverse(stiff, rows):
    size = stiff.shape[0]
    below = shifted_down(stiff, rows)
    lower, diagonal = -below, 1.0 + stiff + below
    upper = jnp.where(rows < size - 1, -stiff, 0.0)
    right = (rows == lax.broadcasted_iota(jnp.int32, (size, size), 1)).astype(jnp.float32)
    distance = 1
    while distance < size:
        down = lambda v: pltpu.roll(v, distance, 0)
        up = lambda v: pltpu.roll(v, size - distance, 0)
        alpha, gamma = -lower / down(diagonal), -upper / up(diagonal)
        right = right + alpha * down(right) + gamma * up(right)
        diagonal = diagonal + alpha * down(upper) + gamma * up(lower)
        lower, upper = alpha * down(lower), gamma * up(upper)
        distance *= 2
    return right / diagonal


def operator_kernel(order_ref, stiff_ref, couple_ref, place_ref, inverse_ref, column_ref):
    levels = inverse_ref.shape[0]
    rows = lax.broadcasted_iota(jnp.int32, (levels, levels), 0)
    diagonal = rows == lax.broadcasted_iota(jnp.int32, (levels, levels), 1)
    place_ref[...] = (order_ref[...] == rows).astype(jnp.float32).astype(jnp.bfloat16)
    stiff = jnp.sum(jnp.where(diagonal, stiff_ref[...], 0.0), axis=1, keepdims=True)
    couple = jnp.sum(jnp.where(diagonal, couple_ref[...], 0.0), axis=1, keepdims=True)
    inverse_ref[...] = operator_inverse(jnp.broadcast_to(stiff, (levels, levels)), rows)
    column_ref[...] = jnp.broadcast_to(couple, column_ref.shape)


def column_kernel(
    mine_ref, other_ref, place_ref, inverse_ref, column_ref, out0_ref, out1_ref, out2_ref, out3_ref,
    a_ref, one_ref, w2_ref, w3_ref, act_ref, sel_ref, g_ref, h_ref, y_ref, t_ref, act2_ref, sel2_ref,
):
    f32, bf16 = jnp.float32, jnp.bfloat16
    device = lax.axis_index("slab")
    core = device % 2
    chips = mine_ref.shape[0]
    devices = 2 * chips
    levels = inverse_ref.shape[0]
    width = act_ref.shape[1]
    blocks = width // LANE
    size = mine_ref.shape[1] - HEAD
    stride = a_ref.shape[0] // devices
    piece = (size - 16) // 2
    half = blocks // 2
    for ref, which in ((mine_ref, core), (other_ref, 1 - core)):
        for c in range(chips):
            for q in range(4):
                rows = pl.ds(pl.multiple_of(2 * PIECE * c + PIECE * which, PIECE), PIECE)
                w2_ref[rows, LANE * q : LANE * (q + 1)] = ref[c, PIECE * q : PIECE * (q + 1), :]
            rows = pl.ds(pl.multiple_of(stride * (2 * c + which), SUB), size)
            a_ref[rows, :] = ref[c, HEAD:, :].astype(f32)
    for q in range(4):
        for r in range(4):
            one_ref[pl.ds(4 * devices * q + r, devices, stride=4), :] = a_ref[pl.ds(4 * q + r, devices, stride=stride), :]
    one = jnp.concatenate([one_ref[4 * devices * q : 4 * devices * (q + 1), :] for q in range(4)], axis=1)
    lanes = lax.broadcasted_iota(jnp.int32, (4, LANE), 1)
    for t in range(devices // 4):
        packed = [a_ref[pl.ds(stride * (4 * t + s) + 16 + 6 * half, 4), :] for s in range(4)]
        for q in range(4):
            tile = jnp.zeros((4, LANE), f32)
            for s in range(4):
                moved = packed[s] if s == q else pltpu.roll(packed[s], PIECE * ((s - q) % 4), 1)
                tile = jnp.where(lane_group(lanes, s), moved, tile)
            w3_ref[4 * q : 4 * q + 4, LANE * t : LANE * (t + 1)] = tile
    w1t = one.T.astype(bf16)
    w1s = one[:levels, :].astype(bf16)
    w2 = w2_ref[...]
    w3t = w3_ref[...].astype(bf16)
    w3 = w3_ref[...].T.astype(bf16)
    place, inverse = place_ref[...], inverse_ref[...]
    order = [16 + piece * b + half * f + j for f in range(6) for b in range(2) for j in range(half)]
    raw = jnp.concatenate([a_ref[pl.ds(k, levels, stride=stride), :] for k in order], axis=1)
    ordered = jnp.dot(place, raw.astype(bf16), preferred_element_type=f32)
    star, density, vertical, diverg, pressure_adjoint, wind_adjoint = (
        ordered[:, width * i : width * (i + 1)] for i in range(6)
    )
    couple = jnp.concatenate([column_ref[...]] * blocks, axis=1)
    rows = lax.broadcasted_iota(jnp.int32, (levels, width), 0)

    def solve(right):
        return jnp.dot(inverse, right, precision=lax.Precision.HIGHEST, preferred_element_type=f32)

    def lower(field):
        return shifted_up(field, rows) - field

    def upper(field):
        return shifted_down(field, rows) - field

    column_input = jnp.concatenate([star, density, vertical, diverg], axis=0).astype(bf16)
    tanh_one = jnp.tanh(jnp.dot(w1t, column_input, preferred_element_type=f32))
    act_one = tanh_one.astype(bf16)
    act_ref[...] = act_one
    rhs_grad = solve(wind_adjoint + couple * lower(pressure_adjoint))
    star_part = pressure_adjoint - upper(couple * rhs_grad)
    heat_grad = rhs_grad.astype(bf16)
    tanh_two = jnp.tanh(contract_first(w2, act_one))
    act_two = tanh_two.astype(bf16)
    act2_ref[...] = act_two
    back_two = jnp.dot(w3, heat_grad, preferred_element_type=f32)
    pre_two_grad = (back_two * (1.0 - tanh_two * tanh_two)).astype(bf16)
    back_one = jnp.dot(w2, pre_two_grad, preferred_element_type=f32)
    pre_one_grad = (back_one * (1.0 - tanh_one * tanh_one)).astype(bf16)
    heating = jnp.dot(w3t, act_two, preferred_element_type=f32)
    wind_next = solve(vertical - couple * lower(star) - 0.5 * density + heating)
    press_next = star + upper(couple * wind_next)
    star_grad = star_part + jnp.dot(w1s, pre_one_grad, preferred_element_type=f32)
    outs = (out0_ref, out1_ref, out2_ref, out3_ref)
    targets = [device ^ (2 * k) for k in range(GROUPS)]
    for k, target in enumerate(targets):
        hid = pl.ds(pl.multiple_of(PIECE * target, PIECE), PIECE)
        sel_ref[PIECE * k : PIECE * (k + 1), :] = act_ref[hid, :]
        sel2_ref[PIECE * k : PIECE * (k + 1), :] = act2_ref[hid, :]
    local_two = contract_last(sel_ref[...], pre_two_grad)
    local_three = contract_last(heat_grad, sel2_ref[...])
    g_ref[...] = contract_last(column_input, pre_one_grad)
    fields = jnp.concatenate([press_next, wind_next, star_grad], axis=1).astype(bf16)
    stored = lax.dot_general(place, fields, (((0,), (0,)), ((), ())), preferred_element_type=f32)
    back = out0_ref.shape[0] - TAIL
    for k in range(3 * blocks):
        y_ref[pl.ds(4 + k, devices, stride=back), :] = stored[:, LANE * k : LANE * (k + 1)]
    for k in range(4 + 3 * blocks, back):
        y_ref[pl.ds(k, devices, stride=back), :] = jnp.zeros((devices, LANE), f32)
    t_ref[...] = local_three
    for k, (target, out_ref) in enumerate(zip(targets, outs)):
        pair = g_ref[pl.ds(pl.multiple_of(SUB * (target // 2), SUB), SUB), :]
        one = jnp.where(core == 0, pair[:4, :], pair[4:, :])
        tile = t_ref[...] if k == 0 else pltpu.roll(t_ref[...], LANE - PIECE * k, 1)
        three = tile[:4, :]
        for q in range(4):
            cols = slice(LANE * q, LANE * (q + 1))
            out_ref[PIECE * q : PIECE * (q + 1), :] = local_two[PIECE * k : PIECE * (k + 1), cols].astype(bf16)
            h_ref[4 * q : 4 * q + 4, :] = one[:, cols]
            if q > 0:
                three = jnp.where(lane_group(lanes, q), pltpu.roll(tile[4 * q : 4 * q + 4, :], PIECE * q, 1), three)
        out_ref[HEAD:TAIL, :] = h_ref[...].astype(bf16)
        start = pl.multiple_of(back * target, SUB)
        y_ref[pl.ds(start, 4), :] = three
        out_ref[TAIL:, :] = y_ref[pl.ds(start, back), :].astype(bf16)


def finish_kernel(scale, r0_ref, r1_ref, r2_ref, r3_ref, p_ref, w_ref, g_ref, one_ref, two_ref, three_ref, y_ref):
    received = (r0_ref, r1_ref, r2_ref, r3_ref)
    back = r0_ref.shape[0] - TAIL
    half = p_ref.shape[0] // SUB
    group = lax.axis_index("slab") // 2 % GROUPS

    def total(start, stop):
        return sum(ref[start:stop, :].astype(jnp.float32) for ref in received) * scale

    for q in range(4):
        two_ref[:, LANE * q : LANE * (q + 1)] = total(PIECE * q, PIECE * (q + 1))
    one = total(HEAD, TAIL)
    for q in range(4):
        one_ref[:, LANE * q : LANE * (q + 1)] = one[4 * q : 4 * q + 4, :]
    for k, ref in enumerate(received):
        y_ref[pl.ds(pl.multiple_of(back * (group ^ k), SUB), back), :] = ref[TAIL:, :].astype(jnp.float32)
    three = sum(y_ref[back * g : back * g + 4, :] for g in range(GROUPS)) * scale
    for q in range(4):
        three_ref[4 * q : 4 * q + 4, :] = three[:, PIECE * q : PIECE * (q + 1)]
    for f, ref in enumerate((p_ref, w_ref, g_ref)):
        for j in range(half):
            for b in range(2):
                rows = pl.ds(4 + 2 * half * f + half * b + j, GROUPS, stride=back)
                ref[SUB * j + GROUPS * b : SUB * j + GROUPS * (b + 1), :] = y_ref[rows, :]


def fast_body(
    pressure, density, vertical_wind, horizontal_wind, metric_terms, neighbors, level_order, stiffness, coupling,
    weight_one, weight_two, weight_three, pressure_adjoint, wind_adjoint,
):
    levels = devices = level_order.shape[0]
    columns = neighbors.shape[1]
    rows = columns // LANE
    chips = devices // 2
    blocks = rows // GROUPS
    width = blocks * LANE
    hidden = weight_two.shape[1]
    f32, bf16 = jnp.float32, jnp.bfloat16
    same_core = [list(range(core, devices, 2)) for core in range(2)]

    def pad(count):
        return -(-count // SUB) * SUB

    def view(field):
        return field.reshape(rows, LANE)

    def lanes(table):
        return table.reshape(table.shape[0], rows, LANE).transpose(1, 0, 2)

    def exchange(blocks_of_chips):
        return lax.all_to_all(blocks_of_chips, "slab", split_axis=0, concat_axis=0, tiled=True, axis_index_groups=same_core)

    sources = (
        view(pressure), view(density), view(vertical_wind), horizontal_wind.reshape(2, rows, LANE), lanes(metric_terms),
        lanes(neighbors), weight_one, weight_two, weight_three.T, view(pressure_adjoint), view(wind_adjoint),
    )
    piece, back = pad(4 + 3 * blocks), pad(4 + 3 * blocks)
    send = call(
        pack_kernel, "pack", shape((chips, TAIL + 2 * piece, LANE), bf16), len(sources),
        [pltpu.VMEM(source.shape, source.dtype) for source in sources]
        + [pltpu.VMEM((16, LANE), f32), pltpu.VMEM((SUB * piece, LANE), f32), pltpu.SemaphoreType.DMA((len(sources),))],
        pltpu.HBM,
    )(*(pltpu.with_memory_space_constraint(source, pltpu.HBM) for source in sources))
    operators = call(
        operator_kernel, "operators", (shape((levels, levels), bf16), shape((levels, levels), f32), shape((levels, LANE), f32)), 3
    )(level_order.reshape(1, levels), stiffness.reshape(1, levels), coupling.reshape(1, levels))
    mine = exchange(send)
    other = lax.ppermute(mine, "slab", [(i, i ^ 1) for i in range(devices)])
    block = shape((TAIL + back, LANE), bf16)
    send_back = call(
        column_kernel, "column_step", (block,) * GROUPS, 5,
        [
            pltpu.VMEM((devices * STRIDE, LANE), f32), pltpu.VMEM((16 * devices, LANE), f32),
            pltpu.VMEM((hidden, hidden), bf16), pltpu.VMEM((levels, hidden), f32), pltpu.VMEM((hidden, width), bf16),
            pltpu.VMEM((GROUPS * PIECE, width), bf16), pltpu.VMEM((4 * levels, hidden), f32), pltpu.VMEM((16, LANE), f32),
            pltpu.VMEM((devices * back, LANE), f32), pltpu.VMEM((levels, LANE), f32),
            pltpu.VMEM((hidden, width), bf16), pltpu.VMEM((GROUPS * PIECE, width), bf16),
        ],
    )(mine, other, *operators)
    received = [send_back[0]] * GROUPS
    for k in range(GROUPS - 1, 0, -1):
        received[k] = lax.ppermute(send_back[k], "slab", [(i, i ^ (2 * k)) for i in range(devices)])
    field_out = shape((rows, LANE), f32)
    new_pressure, new_wind, grad, first_grad, second_grad, third_grad = call(
        functools.partial(finish_kernel, 1.0 / math.sqrt(columns)), "finish",
        (
            field_out, field_out, field_out, shape(weight_one.shape, f32), shape(weight_two.shape, f32),
            shape(weight_three.shape[::-1], f32),
        ),
        GROUPS,
        [pltpu.VMEM((GROUPS * back, LANE), f32)],
    )(*received)
    return (
        new_pressure.reshape(1, columns), new_wind.reshape(1, columns), grad.reshape(1, columns),
        first_grad, second_grad, third_grad.T,
    )


def fits_tiles(*args):
    pressure, level_order, neighbors = args[0], args[6], args[5]
    weight_one, weight_two, weight_three = args[9:12]
    return (
        pressure.shape[0] == 1
        and level_order.shape[0] == 2 * SUB
        and neighbors.shape[1] % (LANE * SUB) == 0
        and weight_one.shape == (4, 4 * LANE)
        and weight_two.shape == (PIECE, 4 * LANE)
        and weight_three.shape == (PIECE, 2 * SUB)
    )


def any_body(*args):
    return (fast_body if fits_tiles(*args) else body)(*args)


def solution(mesh):
    in_specs = (
        P("slab", "date"),
        P("slab", "date"),
        P("slab", "date"),
        P(None, "slab", "date"),
        P(),
        P(),
        P(),
        P(),
        P(),
        P("slab", None),
        P("slab", None),
        P("slab", None),
        P("slab", "date"),
        P("slab", "date"),
    )
    out_specs = (
        P("slab", "date"),
        P("slab", "date"),
        P("slab", "date"),
        P(("date", "slab"), None),
        P(("date", "slab"), None),
        P(("date", "slab"), None),
    )
    return jax.shard_map(any_body, mesh=mesh, in_specs=in_specs, out_specs=out_specs, check_vma=False)
```

```python
import functools
import math

import jax
import jax.numpy as jnp
from jax import lax
from jax.experimental import pallas as pl
from jax.experimental.pallas import tpu as pltpu
from jax.sharding import PartitionSpec as P


def lower_diff(field):
    return jnp.concatenate([field[1:] - field[:-1], -field[-1:]], axis=0)


def upper_diff(field):
    return jnp.concatenate([jnp.zeros_like(field[:1]), field[:-1]], axis=0) - field


def level_inverse(stiffness):
    below = jnp.concatenate([jnp.zeros((1,), jnp.float32), stiffness[:-1]])
    matrix = (
        jnp.diag(1.0 + stiffness + below)
        - jnp.diag(stiffness[:-1], 1)
        - jnp.diag(stiffness[:-1], -1)
    )
    factor = jnp.linalg.cholesky(matrix)
    identity = jnp.eye(stiffness.shape[0], dtype=jnp.float32)
    return jax.scipy.linalg.cho_solve((factor, True), identity)


def apply_inverse(inverse_matrix, rhs):
    return jnp.dot(
        inverse_matrix, rhs, precision=lax.Precision.HIGHEST, preferred_element_type=jnp.float32
    )


def contract_first(left, right):
    return lax.dot_general(
        left, right, (((0,), (0,)), ((), ())), preferred_element_type=jnp.float32
    )


def contract_last(left, right):
    return lax.dot_general(
        left, right, (((1,), (1,)), ((), ())), preferred_element_type=jnp.float32
    )


def body(
    pressure,
    density,
    vertical_wind,
    horizontal_wind,
    metric_terms,
    neighbors,
    level_order,
    stiffness,
    coupling,
    weight_one,
    weight_two,
    weight_three,
    pressure_adjoint,
    wind_adjoint,
):
    east = jnp.take(horizontal_wind[0], neighbors[0], axis=1)
    west = jnp.take(horizontal_wind[0], neighbors[1], axis=1)
    north = jnp.take(horizontal_wind[1], neighbors[2], axis=1)
    south = jnp.take(horizontal_wind[1], neighbors[3], axis=1)
    diverg = metric_terms[0] * (east - west) + metric_terms[1] * (north - south)
    star = pressure - diverg
    inverse = jnp.argsort(level_order)
    scale = 1.0 / math.sqrt(neighbors.shape[1])
    forward_raw = lax.all_to_all(
        jnp.stack([star, density, vertical_wind, diverg]).astype(jnp.bfloat16),
        "slab",
        split_axis=2,
        concat_axis=1,
        tiled=True,
    ).astype(jnp.float32)
    full_one, full_two, full_three = (
        lax.all_gather(weight_one, "slab", axis=0, tiled=True),
        lax.all_gather(weight_two, "slab", axis=0, tiled=True),
        lax.all_gather(weight_three, "slab", axis=0, tiled=True),
    )
    forward_part = jnp.take(forward_raw, inverse, axis=1)
    levels = forward_part.shape[1]
    width = forward_part.shape[2]
    couple = coupling[:, None]
    column_input = forward_part.reshape(4 * levels, width).astype(jnp.bfloat16)
    pre_one = contract_first(full_one, column_input)
    tanh_one = jnp.tanh(pre_one)
    act_one = tanh_one.astype(jnp.bfloat16)
    pre_two = contract_first(full_two, act_one)
    tanh_two = jnp.tanh(pre_two)
    act_two = tanh_two.astype(jnp.bfloat16)
    heating = contract_first(full_three, act_two)
    star_column = forward_part[0]
    rhs = forward_part[2] - couple * lower_diff(star_column) - 0.5 * forward_part[1] + heating
    inverse_matrix = level_inverse(stiffness)
    wind_next = apply_inverse(inverse_matrix, rhs)
    press_next = star_column + upper_diff(couple * wind_next)
    forward_slabs = lax.all_to_all(
        jnp.take(jnp.stack([press_next, wind_next]), level_order, axis=1).astype(jnp.bfloat16),
        "slab",
        split_axis=1,
        concat_axis=2,
        tiled=True,
    ).astype(jnp.float32)
    adjoint_raw = lax.all_to_all(
        jnp.stack([pressure_adjoint, wind_adjoint]), "slab", split_axis=2, concat_axis=1, tiled=True
    )
    adjoint_part = jnp.take(adjoint_raw, inverse, axis=1)
    wind_grad = adjoint_part[1] + couple * lower_diff(adjoint_part[0])
    rhs_grad = apply_inverse(inverse_matrix, wind_grad)
    star_grad = adjoint_part[0] - upper_diff(couple * rhs_grad)
    heat_grad = rhs_grad.astype(jnp.bfloat16)
    local_three = contract_last(act_two, heat_grad) * scale
    back_two = jnp.dot(full_three, heat_grad, preferred_element_type=jnp.float32)
    pre_two_grad = (back_two * (1.0 - tanh_two * tanh_two)).astype(jnp.bfloat16)
    local_two = contract_last(act_one, pre_two_grad) * scale
    back_one = jnp.dot(full_two, pre_two_grad, preferred_element_type=jnp.float32)
    pre_one_grad = (back_one * (1.0 - tanh_one * tanh_one)).astype(jnp.bfloat16)
    local_one = contract_last(column_input, pre_one_grad) * scale
    first_grad, second_grad, third_grad = (
        lax.psum_scatter(local_one, "slab", scatter_dimension=0, tiled=True),
        lax.psum_scatter(local_two, "slab", scatter_dimension=0, tiled=True),
        lax.psum_scatter(local_three, "slab", scatter_dimension=0, tiled=True),
    )
    input_grad = jnp.dot(full_one, pre_one_grad, preferred_element_type=jnp.float32)
    star_grad = star_grad + input_grad[:levels]
    stored_grad = jnp.take(star_grad, level_order, axis=0)
    pressure_new = forward_slabs[0]
    wind_new = forward_slabs[1]
    pressure_grad = lax.all_to_all(
        stored_grad[None].astype(jnp.bfloat16), "slab", split_axis=1, concat_axis=2, tiled=True
    ).astype(jnp.float32)[0]
    return (pressure_new, wind_new, pressure_grad, first_grad, second_grad, third_grad)


LANE = 128
SUB = 8
STRIDE = 104
GROUPS = 4
PIECE = 32
HEAD = 4 * PIECE
TAIL = HEAD + 16


def call(kernel, name, outs, n_in, scratch=(), space=pltpu.VMEM):
    return pl.pallas_call(
        kernel,
        out_shape=outs,
        in_specs=[pl.BlockSpec(memory_space=space) for _ in range(n_in)],
        out_specs=jax.tree.map(lambda _: pl.BlockSpec(memory_space=pltpu.VMEM), outs),
        scratch_shapes=list(scratch),
        compiler_params=pltpu.CompilerParams(vmem_limit_bytes=48 << 20),
        name=name,
    )


def shape(dims, kind):
    return jax.ShapeDtypeStruct(dims, kind)


def pair_up(table):
    half = table.shape[0] // 2
    largest = jnp.max(jnp.max(jnp.abs(table), axis=0, keepdims=True), axis=1, keepdims=True)
    scale = jnp.where(largest > 0.0, 32767.0 / jnp.maximum(largest, 1e-30), 0.0)
    steps = jnp.floor(table * scale + 0.5).astype(jnp.int32)
    return (steps[half:] << 16) | (steps[:half] & 0xFFFF), largest * (1.0 / 32767.0)


def difference(words, first, second):
    half = words.shape[0]
    sublanes = lax.broadcasted_iota(jnp.int32, (SUB, LANE), 0)
    out = []
    for r in range(SUB):
        kept = []
        for index in (first, second):
            row = jnp.broadcast_to(index[r : r + 1, :], (SUB, LANE))
            high, low = row >> 7, row & (LANE - 1)
            late = high >= half
            high = jnp.where(late, high - half, high)
            total = jnp.zeros((SUB, LANE), jnp.int32)
            for g in range(half // SUB):
                picked = jnp.take_along_axis(words[SUB * g : SUB * g + SUB, :], low, axis=1, mode="promise_in_bounds")
                total = jnp.where(high == sublanes + SUB * g, picked, total)
            kept.append(jnp.where(late, total, total << 16) >> 16)
        out.append(jnp.sum((kept[0] - kept[1]).astype(jnp.float32), axis=0, keepdims=True))
    return jnp.concatenate(out, axis=0)


def lane_group(lanes, q):
    return (lanes >= PIECE * q) & (lanes < PIECE * (q + 1))


def pack_kernel(
    p_hbm, d_hbm, w_hbm, u_hbm, m_hbm, n_hbm, one_hbm, two_hbm, three_hbm, pa_hbm, wa_hbm, out_ref,
    p_ref, d_ref, w_ref, u_ref, m_ref, n_ref, one_ref, two_ref, three_ref, pa_ref, wa_ref, part_ref, f_ref, sems,
):
    pairs = (
        (n_hbm, n_ref), (u_hbm, u_ref), (m_hbm, m_ref), (p_hbm, p_ref), (d_hbm, d_ref), (w_hbm, w_ref),
        (pa_hbm, pa_ref), (wa_hbm, wa_ref), (one_hbm, one_ref), (two_hbm, two_ref), (three_hbm, three_ref),
    )
    copies = [pltpu.make_async_copy(source, target, sems.at[i]) for i, (source, target) in enumerate(pairs)]
    for copy in copies:
        copy.start()
    f32, bf16 = jnp.float32, jnp.bfloat16
    chips = out_ref.shape[0]
    piece = f_ref.shape[0] // SUB
    blocks = p_ref.shape[0] // SUB
    for copy in copies:
        copy.wait()

    def put(f, j, tile):
        f_ref[pl.ds(blocks * f + j, SUB, stride=piece), :] = tile

    words_one, step_one = pair_up(u_ref[0])
    words_two, step_two = pair_up(u_ref[1])
    for j in range(blocks):
        rows = slice(SUB * j, SUB * j + SUB)
        along = difference(words_one, n_ref[rows, 0, :], n_ref[rows, 1, :]) * step_one
        across = difference(words_two, n_ref[rows, 2, :], n_ref[rows, 3, :]) * step_two
        diverg = m_ref[rows, 0, :] * along + m_ref[rows, 1, :] * across
        for f, tile in enumerate((p_ref[rows, :] - diverg, d_ref[rows, :], w_ref[rows, :], diverg, pa_ref[rows, :], wa_ref[rows, :])):
            put(f, j, tile)
    lanes = lax.broadcasted_iota(jnp.int32, (PIECE, LANE), 1)
    spread = (lanes % PIECE == lax.broadcasted_iota(jnp.int32, (PIECE, LANE), 0)).astype(f32).astype(bf16)
    part_ref[...] = jnp.dot(three_ref[...], spread, preferred_element_type=f32)
    lanes = lax.broadcasted_iota(jnp.int32, (4, LANE), 1)
    three = jnp.zeros((4, LANE), f32)
    for q in range(4):
        three = jnp.where(lane_group(lanes, q), part_ref[4 * q : 4 * q + 4, :], three)
    one = one_ref[...].astype(f32)
    for q in range(4):
        part_ref[4 * q : 4 * q + 4, :] = one[:, LANE * q : LANE * (q + 1)]
    one = part_ref[...].astype(bf16)
    for c in range(chips):
        for q in range(4):
            out_ref[c, PIECE * q : PIECE * (q + 1), :] = two_ref[:, LANE * q : LANE * (q + 1)]
        out_ref[c, HEAD:TAIL, :] = one
        f_ref[piece * c + 6 * blocks : piece * c + 6 * blocks + 4, :] = three
        if piece > 6 * blocks + 4:
            f_ref[piece * c + 6 * blocks + 4 : piece * (c + 1), :] = jnp.zeros((piece - 6 * blocks - 4, LANE), f32)
    for g in range(GROUPS):
        both = jnp.concatenate([f_ref[piece * c : piece * (c + 1), :] for c in (g, g + GROUPS)], axis=0).astype(bf16)
        for c in range(g, chips, GROUPS):
            out_ref[c, TAIL:, :] = both


def shifted_up(field, rows):
    return jnp.where(rows < field.shape[0] - 1, pltpu.roll(field, field.shape[0] - 1, 0), 0.0)


def shifted_down(field, rows):
    return jnp.where(rows > 0, pltpu.roll(field, 1, 0), 0.0)


def operator_inverse(stiff, rows):
    size = stiff.shape[0]
    below = shifted_down(stiff, rows)
    lower, diagonal = -below, 1.0 + stiff + below
    upper = jnp.where(rows < size - 1, -stiff, 0.0)
    right = (rows == lax.broadcasted_iota(jnp.int32, (size, size), 1)).astype(jnp.float32)
    distance = 1
    while distance < size:
        down = lambda v: pltpu.roll(v, distance, 0)
        up = lambda v: pltpu.roll(v, size - distance, 0)
        alpha, gamma = -lower / down(diagonal), -upper / up(diagonal)
        right = right + alpha * down(right) + gamma * up(right)
        diagonal = diagonal + alpha * down(upper) + gamma * up(lower)
        lower, upper = alpha * down(lower), gamma * up(upper)
        distance *= 2
    return right / diagonal


def operator_kernel(order_ref, stiff_ref, couple_ref, place_ref, inverse_ref, column_ref):
    levels = inverse_ref.shape[0]
    rows = lax.broadcasted_iota(jnp.int32, (levels, levels), 0)
    diagonal = rows == lax.broadcasted_iota(jnp.int32, (levels, levels), 1)
    place_ref[...] = (order_ref[...] == rows).astype(jnp.float32).astype(jnp.bfloat16)
    stiff = jnp.sum(jnp.where(diagonal, stiff_ref[...], 0.0), axis=1, keepdims=True)
    couple = jnp.sum(jnp.where(diagonal, couple_ref[...], 0.0), axis=1, keepdims=True)
    inverse_ref[...] = operator_inverse(jnp.broadcast_to(stiff, (levels, levels)), rows)
    column_ref[...] = jnp.broadcast_to(couple, column_ref.shape)


def column_kernel(
    mine_ref, other_ref, place_ref, inverse_ref, column_ref, out0_ref, out1_ref, out2_ref, out3_ref,
    a_ref, one_ref, w2_ref, w3_ref, act_ref, sel_ref, g_ref, h_ref, y_ref, t_ref, act2_ref, sel2_ref,
):
    f32, bf16 = jnp.float32, jnp.bfloat16
    device = lax.axis_index("slab")
    core = device % 2
    chips = mine_ref.shape[0]
    devices = 2 * chips
    levels = inverse_ref.shape[0]
    width = act_ref.shape[1]
    blocks = width // LANE
    size = mine_ref.shape[1] - HEAD
    stride = a_ref.shape[0] // devices
    piece = (size - 16) // 2
    half = blocks // 2
    for ref, which in ((mine_ref, core), (other_ref, 1 - core)):
        for c in range(chips):
            for q in range(4):
                rows = pl.ds(pl.multiple_of(2 * PIECE * c + PIECE * which, PIECE), PIECE)
                w2_ref[rows, LANE * q : LANE * (q + 1)] = ref[c, PIECE * q : PIECE * (q + 1), :]
            rows = pl.ds(pl.multiple_of(stride * (2 * c + which), SUB), size)
            a_ref[rows, :] = ref[c, HEAD:, :].astype(f32)
    for q in range(4):
        for r in range(4):
            one_ref[pl.ds(4 * devices * q + r, devices, stride=4), :] = a_ref[pl.ds(4 * q + r, devices, stride=stride), :]
    one = jnp.concatenate([one_ref[4 * devices * q : 4 * devices * (q + 1), :] for q in range(4)], axis=1)
    lanes = lax.broadcasted_iota(jnp.int32, (4, LANE), 1)
    for t in range(devices // 4):
        packed = [a_ref[pl.ds(stride * (4 * t + s) + 16 + 6 * half, 4), :] for s in range(4)]
        for q in range(4):
            tile = jnp.zeros((4, LANE), f32)
            for s in range(4):
                moved = packed[s] if s == q else pltpu.roll(packed[s], PIECE * ((s - q) % 4), 1)
                tile = jnp.where(lane_group(lanes, s), moved, tile)
            w3_ref[4 * q : 4 * q + 4, LANE * t : LANE * (t + 1)] = tile
    w1t = one.T.astype(bf16)
    w1s = one[:levels, :].astype(bf16)
    w2 = w2_ref[...]
    w3t = w3_ref[...].astype(bf16)
    w3 = w3_ref[...].T.astype(bf16)
    place, inverse = place_ref[...], inverse_ref[...]
    order = [16 + piece * b + half * f + j for f in range(6) for b in range(2) for j in range(half)]
    raw = jnp.concatenate([a_ref[pl.ds(k, levels, stride=stride), :] for k in order], axis=1)
    ordered = jnp.dot(place, raw.astype(bf16), preferred_element_type=f32)
    star, density, vertical, diverg, pressure_adjoint, wind_adjoint = (
        ordered[:, width * i : width * (i + 1)] for i in range(6)
    )
    couple = jnp.concatenate([column_ref[...]] * blocks, axis=1)
    rows = lax.broadcasted_iota(jnp.int32, (levels, width), 0)

    def solve(right):
        return jnp.dot(inverse, right, precision=lax.Precision.HIGHEST, preferred_element_type=f32)

    def lower(field):
        return shifted_up(field, rows) - field

    def upper(field):
        return shifted_down(field, rows) - field

    column_input = jnp.concatenate([star, density, vertical, diverg], axis=0).astype(bf16)
    tanh_one = jnp.tanh(jnp.dot(w1t, column_input, preferred_element_type=f32))
    act_one = tanh_one.astype(bf16)
    act_ref[...] = act_one
    rhs_grad = solve(wind_adjoint + couple * lower(pressure_adjoint))
    star_part = pressure_adjoint - upper(couple * rhs_grad)
    heat_grad = rhs_grad.astype(bf16)
    tanh_two = jnp.tanh(contract_first(w2, act_one))
    act_two = tanh_two.astype(bf16)
    act2_ref[...] = act_two
    back_two = jnp.dot(w3, heat_grad, preferred_element_type=f32)
    pre_two_grad = (back_two * (1.0 - tanh_two * tanh_two)).astype(bf16)
    back_one = jnp.dot(w2, pre_two_grad, preferred_element_type=f32)
    pre_one_grad = (back_one * (1.0 - tanh_one * tanh_one)).astype(bf16)
    heating = jnp.dot(w3t, act_two, preferred_element_type=f32)
    wind_next = solve(vertical - couple * lower(star) - 0.5 * density + heating)
    press_next = star + upper(couple * wind_next)
    star_grad = star_part + jnp.dot(w1s, pre_one_grad, preferred_element_type=f32)
    outs = (out0_ref, out1_ref, out2_ref, out3_ref)
    targets = [device ^ (2 * k) for k in range(GROUPS)]
    for k, target in enumerate(targets):
        hid = pl.ds(pl.multiple_of(PIECE * target, PIECE), PIECE)
        sel_ref[PIECE * k : PIECE * (k + 1), :] = act_ref[hid, :]
        sel2_ref[PIECE * k : PIECE * (k + 1), :] = act2_ref[hid, :]
    local_two = contract_last(sel_ref[...], pre_two_grad)
    local_three = contract_last(heat_grad, sel2_ref[...])
    g_ref[...] = contract_last(column_input, pre_one_grad)
    fields = jnp.concatenate([press_next, wind_next, star_grad], axis=1).astype(bf16)
    stored = lax.dot_general(place, fields, (((0,), (0,)), ((), ())), preferred_element_type=f32)
    back = out0_ref.shape[0] - TAIL
    for k in range(3 * blocks):
        y_ref[pl.ds(4 + k, devices, stride=back), :] = stored[:, LANE * k : LANE * (k + 1)]
    for k in range(4 + 3 * blocks, back):
        y_ref[pl.ds(k, devices, stride=back), :] = jnp.zeros((devices, LANE), f32)
    t_ref[...] = local_three
    for k, (target, out_ref) in enumerate(zip(targets, outs)):
        pair = g_ref[pl.ds(pl.multiple_of(SUB * (target // 2), SUB), SUB), :]
        one = jnp.where(core == 0, pair[:4, :], pair[4:, :])
        tile = t_ref[...] if k == 0 else pltpu.roll(t_ref[...], LANE - PIECE * k, 1)
        three = tile[:4, :]
        for q in range(4):
            cols = slice(LANE * q, LANE * (q + 1))
            out_ref[PIECE * q : PIECE * (q + 1), :] = local_two[PIECE * k : PIECE * (k + 1), cols].astype(bf16)
            h_ref[4 * q : 4 * q + 4, :] = one[:, cols]
            if q > 0:
                three = jnp.where(lane_group(lanes, q), pltpu.roll(tile[4 * q : 4 * q + 4, :], PIECE * q, 1), three)
        out_ref[HEAD:TAIL, :] = h_ref[...].astype(bf16)
        start = pl.multiple_of(back * target, SUB)
        y_ref[pl.ds(start, 4), :] = three
        out_ref[TAIL:, :] = y_ref[pl.ds(start, back), :].astype(bf16)


def finish_kernel(scale, r0_ref, r1_ref, r2_ref, r3_ref, p_ref, w_ref, g_ref, one_ref, two_ref, three_ref, y_ref):
    received = (r0_ref, r1_ref, r2_ref, r3_ref)
    back = r0_ref.shape[0] - TAIL
    half = p_ref.shape[0] // SUB
    group = lax.axis_index("slab") // 2 % GROUPS

    def total(start, stop):
        return sum(ref[start:stop, :].astype(jnp.float32) for ref in received) * scale

    for q in range(4):
        two_ref[:, LANE * q : LANE * (q + 1)] = total(PIECE * q, PIECE * (q + 1))
    one = total(HEAD, TAIL)
    for q in range(4):
        one_ref[:, LANE * q : LANE * (q + 1)] = one[4 * q : 4 * q + 4, :]
    for k, ref in enumerate(received):
        y_ref[pl.ds(pl.multiple_of(back * (group ^ k), SUB), back), :] = ref[TAIL:, :].astype(jnp.float32)
    three = sum(y_ref[back * g : back * g + 4, :] for g in range(GROUPS)) * scale
    for q in range(4):
        three_ref[4 * q : 4 * q + 4, :] = three[:, PIECE * q : PIECE * (q + 1)]
    for f, ref in enumerate((p_ref, w_ref, g_ref)):
        for j in range(half):
            for b in range(2):
                rows = pl.ds(4 + 2 * half * f + half * b + j, GROUPS, stride=back)
                ref[SUB * j + GROUPS * b : SUB * j + GROUPS * (b + 1), :] = y_ref[rows, :]


def fast_body(
    pressure, density, vertical_wind, horizontal_wind, metric_terms, neighbors, level_order, stiffness, coupling,
    weight_one, weight_two, weight_three, pressure_adjoint, wind_adjoint,
):
    levels = devices = level_order.shape[0]
    columns = neighbors.shape[1]
    rows = columns // LANE
    chips = devices // 2
    blocks = rows // GROUPS
    width = blocks * LANE
    hidden = weight_two.shape[1]
    f32, bf16 = jnp.float32, jnp.bfloat16
    same_core = [list(range(core, devices, 2)) for core in range(2)]

    def pad(count):
        return -(-count // SUB) * SUB

    def view(field):
        return field.reshape(rows, LANE)

    def lanes(table):
        return table.reshape(table.shape[0], rows, LANE).transpose(1, 0, 2)

    def exchange(blocks_of_chips):
        return lax.all_to_all(blocks_of_chips, "slab", split_axis=0, concat_axis=0, tiled=True, axis_index_groups=same_core)

    sources = (
        view(pressure), view(density), view(vertical_wind), horizontal_wind.reshape(2, rows, LANE), lanes(metric_terms),
        lanes(neighbors), weight_one, weight_two, weight_three.T, view(pressure_adjoint), view(wind_adjoint),
    )
    piece, back = pad(4 + 3 * blocks), pad(4 + 3 * blocks)
    send = call(
        pack_kernel, "pack", shape((chips, TAIL + 2 * piece, LANE), bf16), len(sources),
        [pltpu.VMEM(source.shape, source.dtype) for source in sources]
        + [pltpu.VMEM((16, LANE), f32), pltpu.VMEM((SUB * piece, LANE), f32), pltpu.SemaphoreType.DMA((len(sources),))],
        pltpu.HBM,
    )(*(pltpu.with_memory_space_constraint(source, pltpu.HBM) for source in sources))
    operators = call(
        operator_kernel, "operators", (shape((levels, levels), bf16), shape((levels, levels), f32), shape((levels, LANE), f32)), 3
    )(level_order.reshape(1, levels), stiffness.reshape(1, levels), coupling.reshape(1, levels))
    mine = exchange(send)
    other = lax.ppermute(mine, "slab", [(i, i ^ 1) for i in range(devices)])
    block = shape((TAIL + back, LANE), bf16)
    send_back = call(
        column_kernel, "column_step", (block,) * GROUPS, 5,
        [
            pltpu.VMEM((devices * STRIDE, LANE), f32), pltpu.VMEM((16 * devices, LANE), f32),
            pltpu.VMEM((hidden, hidden), bf16), pltpu.VMEM((levels, hidden), f32), pltpu.VMEM((hidden, width), bf16),
            pltpu.VMEM((GROUPS * PIECE, width), bf16), pltpu.VMEM((4 * levels, hidden), f32), pltpu.VMEM((16, LANE), f32),
            pltpu.VMEM((devices * back, LANE), f32), pltpu.VMEM((levels, LANE), f32),
            pltpu.VMEM((hidden, width), bf16), pltpu.VMEM((GROUPS * PIECE, width), bf16),
        ],
    )(mine, other, *operators)
    received = [send_back[0]] * GROUPS
    for k in range(GROUPS - 1, 0, -1):
        received[k] = lax.ppermute(send_back[k], "slab", [(i, i ^ (2 * k)) for i in range(devices)])
    field_out = shape((rows, LANE), f32)
    new_pressure, new_wind, grad, first_grad, second_grad, third_grad = call(
        functools.partial(finish_kernel, 1.0 / math.sqrt(columns)), "finish",
        (
            field_out, field_out, field_out, shape(weight_one.shape, f32), shape(weight_two.shape, f32),
            shape(weight_three.shape[::-1], f32),
        ),
        GROUPS,
        [pltpu.VMEM((GROUPS * back, LANE), f32)],
    )(*received)
    return (
        new_pressure.reshape(1, columns), new_wind.reshape(1, columns), grad.reshape(1, columns),
        first_grad, second_grad, third_grad.T,
    )


def fits_tiles(*args):
    pressure, level_order, neighbors = args[0], args[6], args[5]
    weight_one, weight_two, weight_three = args[9:12]
    return (
        pressure.shape[0] == 1
        and level_order.shape[0] == 2 * SUB
        and neighbors.shape[1] % (2 * LANE * SUB) == 0
        and weight_one.shape == (4, 4 * LANE)
        and weight_two.shape == (PIECE, 4 * LANE)
        and weight_three.shape == (PIECE, 2 * SUB)
    )


def any_body(*args):
    return (fast_body if fits_tiles(*args) else body)(*args)


def solution(mesh):
    in_specs = (
        P("slab", "date"),
        P("slab", "date"),
        P("slab", "date"),
        P(None, "slab", "date"),
        P(),
        P(),
        P(),
        P(),
        P(),
        P("slab", None),
        P("slab", None),
        P("slab", None),
        P("slab", "date"),
        P("slab", "date"),
    )
    out_specs = (
        P("slab", "date"),
        P("slab", "date"),
        P("slab", "date"),
        P(("date", "slab"), None),
        P(("date", "slab"), None),
        P(("date", "slab"), None),
    )
    return jax.shard_map(any_body, mesh=mesh, in_specs=in_specs, out_specs=out_specs, check_vma=False)
```

```python
import functools
import math

import jax
import jax.numpy as jnp
from jax import lax
from jax.experimental import pallas as pl
from jax.experimental.pallas import tpu as pltpu
from jax.sharding import PartitionSpec as P


def lower_diff(field):
    return jnp.concatenate([field[1:] - field[:-1], -field[-1:]], axis=0)


def upper_diff(field):
    return jnp.concatenate([jnp.zeros_like(field[:1]), field[:-1]], axis=0) - field


def level_inverse(stiffness):
    below = jnp.concatenate([jnp.zeros((1,), jnp.float32), stiffness[:-1]])
    matrix = (
        jnp.diag(1.0 + stiffness + below)
        - jnp.diag(stiffness[:-1], 1)
        - jnp.diag(stiffness[:-1], -1)
    )
    factor = jnp.linalg.cholesky(matrix)
    identity = jnp.eye(stiffness.shape[0], dtype=jnp.float32)
    return jax.scipy.linalg.cho_solve((factor, True), identity)


def apply_inverse(inverse_matrix, rhs):
    return jnp.dot(
        inverse_matrix, rhs, precision=lax.Precision.HIGHEST, preferred_element_type=jnp.float32
    )


def contract_first(left, right):
    return lax.dot_general(
        left, right, (((0,), (0,)), ((), ())), preferred_element_type=jnp.float32
    )


def contract_last(left, right):
    return lax.dot_general(
        left, right, (((1,), (1,)), ((), ())), preferred_element_type=jnp.float32
    )


def body(
    pressure,
    density,
    vertical_wind,
    horizontal_wind,
    metric_terms,
    neighbors,
    level_order,
    stiffness,
    coupling,
    weight_one,
    weight_two,
    weight_three,
    pressure_adjoint,
    wind_adjoint,
):
    east = jnp.take(horizontal_wind[0], neighbors[0], axis=1)
    west = jnp.take(horizontal_wind[0], neighbors[1], axis=1)
    north = jnp.take(horizontal_wind[1], neighbors[2], axis=1)
    south = jnp.take(horizontal_wind[1], neighbors[3], axis=1)
    diverg = metric_terms[0] * (east - west) + metric_terms[1] * (north - south)
    star = pressure - diverg
    inverse = jnp.argsort(level_order)
    scale = 1.0 / math.sqrt(neighbors.shape[1])
    forward_raw = lax.all_to_all(
        jnp.stack([star, density, vertical_wind, diverg]).astype(jnp.bfloat16),
        "slab",
        split_axis=2,
        concat_axis=1,
        tiled=True,
    ).astype(jnp.float32)
    full_one, full_two, full_three = (
        lax.all_gather(weight_one, "slab", axis=0, tiled=True),
        lax.all_gather(weight_two, "slab", axis=0, tiled=True),
        lax.all_gather(weight_three, "slab", axis=0, tiled=True),
    )
    forward_part = jnp.take(forward_raw, inverse, axis=1)
    levels = forward_part.shape[1]
    width = forward_part.shape[2]
    couple = coupling[:, None]
    column_input = forward_part.reshape(4 * levels, width).astype(jnp.bfloat16)
    pre_one = contract_first(full_one, column_input)
    tanh_one = jnp.tanh(pre_one)
    act_one = tanh_one.astype(jnp.bfloat16)
    pre_two = contract_first(full_two, act_one)
    tanh_two = jnp.tanh(pre_two)
    act_two = tanh_two.astype(jnp.bfloat16)
    heating = contract_first(full_three, act_two)
    star_column = forward_part[0]
    rhs = forward_part[2] - couple * lower_diff(star_column) - 0.5 * forward_part[1] + heating
    inverse_matrix = level_inverse(stiffness)
    wind_next = apply_inverse(inverse_matrix, rhs)
    press_next = star_column + upper_diff(couple * wind_next)
    forward_slabs = lax.all_to_all(
        jnp.take(jnp.stack([press_next, wind_next]), level_order, axis=1).astype(jnp.bfloat16),
        "slab",
        split_axis=1,
        concat_axis=2,
        tiled=True,
    ).astype(jnp.float32)
    adjoint_raw = lax.all_to_all(
        jnp.stack([pressure_adjoint, wind_adjoint]), "slab", split_axis=2, concat_axis=1, tiled=True
    )
    adjoint_part = jnp.take(adjoint_raw, inverse, axis=1)
    wind_grad = adjoint_part[1] + couple * lower_diff(adjoint_part[0])
    rhs_grad = apply_inverse(inverse_matrix, wind_grad)
    star_grad = adjoint_part[0] - upper_diff(couple * rhs_grad)
    heat_grad = rhs_grad.astype(jnp.bfloat16)
    local_three = contract_last(act_two, heat_grad) * scale
    back_two = jnp.dot(full_three, heat_grad, preferred_element_type=jnp.float32)
    pre_two_grad = (back_two * (1.0 - tanh_two * tanh_two)).astype(jnp.bfloat16)
    local_two = contract_last(act_one, pre_two_grad) * scale
    back_one = jnp.dot(full_two, pre_two_grad, preferred_element_type=jnp.float32)
    pre_one_grad = (back_one * (1.0 - tanh_one * tanh_one)).astype(jnp.bfloat16)
    local_one = contract_last(column_input, pre_one_grad) * scale
    first_grad, second_grad, third_grad = (
        lax.psum_scatter(local_one, "slab", scatter_dimension=0, tiled=True),
        lax.psum_scatter(local_two, "slab", scatter_dimension=0, tiled=True),
        lax.psum_scatter(local_three, "slab", scatter_dimension=0, tiled=True),
    )
    input_grad = jnp.dot(full_one, pre_one_grad, preferred_element_type=jnp.float32)
    star_grad = star_grad + input_grad[:levels]
    stored_grad = jnp.take(star_grad, level_order, axis=0)
    pressure_new = forward_slabs[0]
    wind_new = forward_slabs[1]
    pressure_grad = lax.all_to_all(
        stored_grad[None].astype(jnp.bfloat16), "slab", split_axis=1, concat_axis=2, tiled=True
    ).astype(jnp.float32)[0]
    return (pressure_new, wind_new, pressure_grad, first_grad, second_grad, third_grad)


LANE = 128
SUB = 8
STRIDE = 104
GROUPS = 4
PIECE = 32
HEAD = 4 * PIECE
TAIL = HEAD + 16
FRONT = TAIL + 8


def call(kernel, name, outs, n_in, scratch=(), space=pltpu.VMEM):
    return pl.pallas_call(
        kernel,
        out_shape=outs,
        in_specs=[pl.BlockSpec(memory_space=space) for _ in range(n_in)],
        out_specs=jax.tree.map(lambda _: pl.BlockSpec(memory_space=pltpu.VMEM), outs),
        scratch_shapes=list(scratch),
        compiler_params=pltpu.CompilerParams(vmem_limit_bytes=48 << 20),
        name=name,
    )


def shape(dims, kind):
    return jax.ShapeDtypeStruct(dims, kind)


def pair_up(table):
    half = table.shape[0] // 2
    largest = jnp.max(jnp.max(jnp.abs(table), axis=0, keepdims=True), axis=1, keepdims=True)
    scale = jnp.where(largest > 0.0, 32767.0 / jnp.maximum(largest, 1e-30), 0.0)
    steps = jnp.floor(table * scale + 0.5).astype(jnp.int32)
    return (steps[half:] << 16) | (steps[:half] & 0xFFFF), largest * (1.0 / 32767.0)


def difference(words, first, second):
    half = words.shape[0]
    sublanes = lax.broadcasted_iota(jnp.int32, (SUB, LANE), 0)
    out = []
    for r in range(SUB):
        kept = []
        for index in (first, second):
            row = jnp.broadcast_to(index[r : r + 1, :], (SUB, LANE))
            high, low = row >> 7, row & (LANE - 1)
            late = high >= half
            high = jnp.where(late, high - half, high)
            total = jnp.zeros((SUB, LANE), jnp.int32)
            for g in range(half // SUB):
                picked = jnp.take_along_axis(words[SUB * g : SUB * g + SUB, :], low, axis=1, mode="promise_in_bounds")
                total = jnp.where(high == sublanes + SUB * g, picked, total)
            kept.append(jnp.where(late, total, total << 16) >> 16)
        out.append(jnp.sum((kept[0] - kept[1]).astype(jnp.float32), axis=0, keepdims=True))
    return jnp.concatenate(out, axis=0)


def lane_group(lanes, q):
    return (lanes >= PIECE * q) & (lanes < PIECE * (q + 1))


def pack_kernel(
    p_hbm, d_hbm, w_hbm, u_hbm, m_hbm, n_hbm, one_hbm, two_hbm, three_hbm, pa_hbm, wa_hbm,
    whole_ref, out0_ref, out1_ref, out2_ref, out3_ref,
    p_ref, d_ref, w_ref, u_ref, m_ref, n_ref, one_ref, two_ref, three_ref, pa_ref, wa_ref, part_ref, f_ref, g_ref, sems,
):
    pairs = (
        (n_hbm, n_ref), (u_hbm, u_ref), (m_hbm, m_ref), (p_hbm, p_ref), (d_hbm, d_ref), (w_hbm, w_ref),
        (pa_hbm, pa_ref), (wa_hbm, wa_ref), (one_hbm, one_ref), (two_hbm, two_ref), (three_hbm, three_ref),
    )
    copies = [pltpu.make_async_copy(source, target, sems.at[i]) for i, (source, target) in enumerate(pairs)]
    for copy in copies:
        copy.start()
    f32, bf16 = jnp.float32, jnp.bfloat16
    piece = f_ref.shape[0] // SUB
    blocks = p_ref.shape[0] // SUB
    for copy in copies:
        copy.wait()

    def put(f, j, tile):
        f_ref[pl.ds(blocks * f + j, SUB, stride=piece), :] = tile

    words_one, step_one = pair_up(u_ref[0])
    words_two, step_two = pair_up(u_ref[1])
    for j in range(blocks):
        rows = slice(SUB * j, SUB * j + SUB)
        along = difference(words_one, n_ref[rows, 0, :], n_ref[rows, 1, :]) * step_one
        across = difference(words_two, n_ref[rows, 2, :], n_ref[rows, 3, :]) * step_two
        diverg = m_ref[rows, 0, :] * along + m_ref[rows, 1, :] * across
        for f, tile in enumerate((p_ref[rows, :] - diverg, d_ref[rows, :], w_ref[rows, :], diverg, pa_ref[rows, :], wa_ref[rows, :])):
            put(f, j, tile)
    lanes = lax.broadcasted_iota(jnp.int32, (PIECE, LANE), 1)
    spread = (lanes % PIECE == lax.broadcasted_iota(jnp.int32, (PIECE, LANE), 0)).astype(f32).astype(bf16)
    part_ref[...] = jnp.dot(three_ref[...], spread, preferred_element_type=f32)
    lanes = lax.broadcasted_iota(jnp.int32, (4, LANE), 1)
    three = jnp.zeros((4, LANE), f32)
    for q in range(4):
        three = jnp.where(lane_group(lanes, q), part_ref[4 * q : 4 * q + 4, :], three)
    one = one_ref[...].astype(f32)
    for q in range(4):
        part_ref[4 * q : 4 * q + 4, :] = one[:, LANE * q : LANE * (q + 1)]
    one = part_ref[...].astype(bf16)
    part_ref[0:4, :] = three
    part_ref[4:8, :] = jnp.zeros((4, LANE), f32)
    three = part_ref[0:8, :].astype(bf16)
    for g in range(GROUPS):
        both = [f_ref[piece * c : piece * (c + 1), :] for c in (g, g + GROUPS)]
        g_ref[2 * piece * g : 2 * piece * (g + 1), :] = jnp.concatenate(both, axis=0)
    group = lax.axis_index("slab") // 2 % GROUPS
    outs = (out0_ref, out1_ref, out2_ref, out3_ref)
    for ref in (whole_ref,) + outs:
        for q in range(4):
            ref[PIECE * q : PIECE * (q + 1), :] = two_ref[:, LANE * q : LANE * (q + 1)]
        ref[HEAD:TAIL, :] = one
        ref[TAIL:FRONT, :] = three
    whole_ref[FRONT:, :] = g_ref[...].astype(bf16)
    for k, ref in enumerate(outs):
        ref[FRONT:, :] = g_ref[pl.ds(pl.multiple_of(2 * piece * (group ^ k), SUB), 2 * piece), :].astype(bf16)


def relay_kernel(whole_ref, out0_ref, out1_ref, out2_ref, out3_ref, g_ref):
    size = out0_ref.shape[0] - FRONT
    group = lax.axis_index("slab") // 2 % GROUPS
    g_ref[...] = whole_ref[FRONT:, :].astype(jnp.float32)
    for k, ref in enumerate((out0_ref, out1_ref, out2_ref, out3_ref)):
        ref[:FRONT, :] = whole_ref[:FRONT, :]
        ref[FRONT:, :] = g_ref[pl.ds(pl.multiple_of(size * (group ^ k), SUB), size), :].astype(jnp.bfloat16)


def shifted_up(field, rows):
    return jnp.where(rows < field.shape[0] - 1, pltpu.roll(field, field.shape[0] - 1, 0), 0.0)


def shifted_down(field, rows):
    return jnp.where(rows > 0, pltpu.roll(field, 1, 0), 0.0)


def operator_inverse(stiff, rows):
    size = stiff.shape[0]
    below = shifted_down(stiff, rows)
    lower, diagonal = -below, 1.0 + stiff + below
    upper = jnp.where(rows < size - 1, -stiff, 0.0)
    right = (rows == lax.broadcasted_iota(jnp.int32, (size, size), 1)).astype(jnp.float32)
    distance = 1
    while distance < size:
        down = lambda v: pltpu.roll(v, distance, 0)
        up = lambda v: pltpu.roll(v, size - distance, 0)
        alpha, gamma = -lower / down(diagonal), -upper / up(diagonal)
        right = right + alpha * down(right) + gamma * up(right)
        diagonal = diagonal + alpha * down(upper) + gamma * up(lower)
        lower, upper = alpha * down(lower), gamma * up(upper)
        distance *= 2
    return right / diagonal


def operator_kernel(order_ref, stiff_ref, couple_ref, place_ref, inverse_ref, column_ref):
    levels = inverse_ref.shape[0]
    rows = lax.broadcasted_iota(jnp.int32, (levels, levels), 0)
    diagonal = rows == lax.broadcasted_iota(jnp.int32, (levels, levels), 1)
    place_ref[...] = (order_ref[...] == rows).astype(jnp.float32).astype(jnp.bfloat16)
    stiff = jnp.sum(jnp.where(diagonal, stiff_ref[...], 0.0), axis=1, keepdims=True)
    couple = jnp.sum(jnp.where(diagonal, couple_ref[...], 0.0), axis=1, keepdims=True)
    inverse_ref[...] = operator_inverse(jnp.broadcast_to(stiff, (levels, levels)), rows)
    column_ref[...] = jnp.broadcast_to(couple, column_ref.shape)


def column_kernel(*refs):
    sources = refs[: 4 * GROUPS]
    place_ref, inverse_ref, column_ref, out0_ref, out1_ref, out2_ref, out3_ref = refs[4 * GROUPS : 4 * GROUPS + 7]
    (
        a_ref, one_ref, w2_ref, w3_ref, act_ref, sel_ref, g_ref, h_ref, y_ref, t_ref, act2_ref, sel2_ref,
    ) = refs[4 * GROUPS + 7 :]
    f32, bf16 = jnp.float32, jnp.bfloat16
    device = lax.axis_index("slab")
    core = device % 2
    devices = 4 * GROUPS
    levels = inverse_ref.shape[0]
    width = act_ref.shape[1]
    blocks = width // LANE
    half = blocks // 2
    stride = a_ref.shape[0] // devices
    size = sources[0].shape[0] - HEAD
    for i, ref in enumerate(sources):
        source = device ^ (2 * (i % GROUPS) + SUB * (i // GROUPS % 2) + i // (2 * GROUPS))
        for q in range(4):
            rows = pl.ds(pl.multiple_of(PIECE * source, PIECE), PIECE)
            w2_ref[rows, LANE * q : LANE * (q + 1)] = ref[PIECE * q : PIECE * (q + 1), :]
        a_ref[pl.ds(pl.multiple_of(stride * source, SUB), size), :] = ref[HEAD:, :].astype(f32)
    for q in range(4):
        for r in range(4):
            one_ref[pl.ds(4 * devices * q + r, devices, stride=4), :] = a_ref[pl.ds(4 * q + r, devices, stride=stride), :]
    one = jnp.concatenate([one_ref[4 * devices * q : 4 * devices * (q + 1), :] for q in range(4)], axis=1)
    lanes = lax.broadcasted_iota(jnp.int32, (4, LANE), 1)
    for t in range(devices // 4):
        packed = [a_ref[stride * (4 * t + s) + 16 : stride * (4 * t + s) + 20, :] for s in range(4)]
        for q in range(4):
            tile = jnp.zeros((4, LANE), f32)
            for s in range(4):
                moved = packed[s] if s == q else pltpu.roll(packed[s], PIECE * ((s - q) % 4), 1)
                tile = jnp.where(lane_group(lanes, s), moved, tile)
            w3_ref[4 * q : 4 * q + 4, LANE * t : LANE * (t + 1)] = tile
    w1t = one.T.astype(bf16)
    w1s = one[:levels, :].astype(bf16)
    w2 = w2_ref[...]
    w3t = w3_ref[...].astype(bf16)
    w3 = w3_ref[...].T.astype(bf16)
    place, inverse = place_ref[...], inverse_ref[...]
    order = [24 + 6 * half * b + half * f + j for f in range(6) for b in range(2) for j in range(half)]
    raw = jnp.concatenate([a_ref[pl.ds(k, levels, stride=stride), :] for k in order], axis=1)
    ordered = jnp.dot(place, raw.astype(bf16), preferred_element_type=f32)
    star, density, vertical, diverg, pressure_adjoint, wind_adjoint = (
        ordered[:, width * i : width * (i + 1)] for i in range(6)
    )
    couple = jnp.concatenate([column_ref[...]] * blocks, axis=1)
    rows = lax.broadcasted_iota(jnp.int32, (levels, width), 0)

    def solve(right):
        return jnp.dot(inverse, right, precision=lax.Precision.HIGHEST, preferred_element_type=f32)

    def lower(field):
        return shifted_up(field, rows) - field

    def upper(field):
        return shifted_down(field, rows) - field

    column_input = jnp.concatenate([star, density, vertical, diverg], axis=0).astype(bf16)
    tanh_one = jnp.tanh(jnp.dot(w1t, column_input, preferred_element_type=f32))
    act_one = tanh_one.astype(bf16)
    act_ref[...] = act_one
    rhs_grad = solve(wind_adjoint + couple * lower(pressure_adjoint))
    star_part = pressure_adjoint - upper(couple * rhs_grad)
    heat_grad = rhs_grad.astype(bf16)
    tanh_two = jnp.tanh(contract_first(w2, act_one))
    act_two = tanh_two.astype(bf16)
    act2_ref[...] = act_two
    back_two = jnp.dot(w3, heat_grad, preferred_element_type=f32)
    pre_two_grad = (back_two * (1.0 - tanh_two * tanh_two)).astype(bf16)
    back_one = jnp.dot(w2, pre_two_grad, preferred_element_type=f32)
    pre_one_grad = (back_one * (1.0 - tanh_one * tanh_one)).astype(bf16)
    heating = jnp.dot(w3t, act_two, preferred_element_type=f32)
    wind_next = solve(vertical - couple * lower(star) - 0.5 * density + heating)
    press_next = star + upper(couple * wind_next)
    star_grad = star_part + jnp.dot(w1s, pre_one_grad, preferred_element_type=f32)
    outs = (out0_ref, out1_ref, out2_ref, out3_ref)
    targets = [device ^ (2 * k) for k in range(GROUPS)]
    for k, target in enumerate(targets):
        hid = pl.ds(pl.multiple_of(PIECE * target, PIECE), PIECE)
        sel_ref[PIECE * k : PIECE * (k + 1), :] = act_ref[hid, :]
        sel2_ref[PIECE * k : PIECE * (k + 1), :] = act2_ref[hid, :]
    local_two = contract_last(sel_ref[...], pre_two_grad)
    local_three = contract_last(heat_grad, sel2_ref[...])
    g_ref[...] = contract_last(column_input, pre_one_grad)
    fields = jnp.concatenate([press_next, wind_next, star_grad], axis=1).astype(bf16)
    stored = lax.dot_general(place, fields, (((0,), (0,)), ((), ())), preferred_element_type=f32)
    back = out0_ref.shape[0] - TAIL
    for k in range(3 * blocks):
        y_ref[pl.ds(4 + k, devices, stride=back), :] = stored[:, LANE * k : LANE * (k + 1)]
    for k in range(4 + 3 * blocks, back):
        y_ref[pl.ds(k, devices, stride=back), :] = jnp.zeros((devices, LANE), f32)
    t_ref[...] = local_three
    for k, (target, out_ref) in enumerate(zip(targets, outs)):
        pair = g_ref[pl.ds(pl.multiple_of(SUB * (target // 2), SUB), SUB), :]
        one = jnp.where(core == 0, pair[:4, :], pair[4:, :])
        tile = t_ref[...] if k == 0 else pltpu.roll(t_ref[...], LANE - PIECE * k, 1)
        three = tile[:4, :]
        for q in range(4):
            cols = slice(LANE * q, LANE * (q + 1))
            out_ref[PIECE * q : PIECE * (q + 1), :] = local_two[PIECE * k : PIECE * (k + 1), cols].astype(bf16)
            h_ref[4 * q : 4 * q + 4, :] = one[:, cols]
            if q > 0:
                three = jnp.where(lane_group(lanes, q), pltpu.roll(tile[4 * q : 4 * q + 4, :], PIECE * q, 1), three)
        out_ref[HEAD:TAIL, :] = h_ref[...].astype(bf16)
        start = pl.multiple_of(back * target, SUB)
        y_ref[pl.ds(start, 4), :] = three
        out_ref[TAIL:, :] = y_ref[pl.ds(start, back), :].astype(bf16)


def finish_kernel(scale, r0_ref, r1_ref, r2_ref, r3_ref, p_ref, w_ref, g_ref, one_ref, two_ref, three_ref, y_ref):
    received = (r0_ref, r1_ref, r2_ref, r3_ref)
    back = r0_ref.shape[0] - TAIL
    half = p_ref.shape[0] // SUB
    group = lax.axis_index("slab") // 2 % GROUPS

    def total(start, stop):
        return sum(ref[start:stop, :].astype(jnp.float32) for ref in received) * scale

    for q in range(4):
        two_ref[:, LANE * q : LANE * (q + 1)] = total(PIECE * q, PIECE * (q + 1))
    one = total(HEAD, TAIL)
    for q in range(4):
        one_ref[:, LANE * q : LANE * (q + 1)] = one[4 * q : 4 * q + 4, :]
    for k, ref in enumerate(received):
        y_ref[pl.ds(pl.multiple_of(back * (group ^ k), SUB), back), :] = ref[TAIL:, :].astype(jnp.float32)
    three = sum(y_ref[back * g : back * g + 4, :] for g in range(GROUPS)) * scale
    for q in range(4):
        three_ref[4 * q : 4 * q + 4, :] = three[:, PIECE * q : PIECE * (q + 1)]
    for f, ref in enumerate((p_ref, w_ref, g_ref)):
        for j in range(half):
            for b in range(2):
                rows = pl.ds(4 + 2 * half * f + half * b + j, GROUPS, stride=back)
                ref[SUB * j + GROUPS * b : SUB * j + GROUPS * (b + 1), :] = y_ref[rows, :]


def fast_body(
    pressure, density, vertical_wind, horizontal_wind, metric_terms, neighbors, level_order, stiffness, coupling,
    weight_one, weight_two, weight_three, pressure_adjoint, wind_adjoint,
):
    levels = devices = level_order.shape[0]
    columns = neighbors.shape[1]
    rows = columns // LANE
    blocks = rows // GROUPS
    width = blocks * LANE
    hidden = weight_two.shape[1]
    f32, bf16 = jnp.float32, jnp.bfloat16

    def pad(count):
        return -(-count // SUB) * SUB

    def view(field):
        return field.reshape(rows, LANE)

    def lanes(table):
        return table.reshape(table.shape[0], rows, LANE).transpose(1, 0, 2)

    def swap(array, bits):
        return lax.ppermute(array, "slab", [(i, i ^ bits) for i in range(devices)])

    def among_groups(outgoing):
        return [outgoing[0]] + [swap(outgoing[k], 2 * k) for k in range(1, GROUPS)]

    sources = (
        view(pressure), view(density), view(vertical_wind), horizontal_wind.reshape(2, rows, LANE), lanes(metric_terms),
        lanes(neighbors), weight_one, weight_two, weight_three.T, view(pressure_adjoint), view(wind_adjoint),
    )
    piece, back = 3 * blocks, pad(4 + 3 * blocks)
    one_group = (shape((FRONT + 2 * piece, LANE), bf16),) * GROUPS
    all_groups = pltpu.VMEM((GROUPS * 2 * piece, LANE), f32)
    whole, *near = call(
        pack_kernel, "pack", (shape((FRONT + GROUPS * 2 * piece, LANE), bf16),) + one_group, len(sources),
        [pltpu.VMEM(source.shape, source.dtype) for source in sources]
        + [pltpu.VMEM((16, LANE), f32), pltpu.VMEM((SUB * piece, LANE), f32), all_groups, pltpu.SemaphoreType.DMA((len(sources),))],
        pltpu.HBM,
    )(*(pltpu.with_memory_space_constraint(source, pltpu.HBM) for source in sources))
    far = call(relay_kernel, "relay", one_group, 1, [all_groups])(swap(whole, SUB))
    same_core = among_groups(near) + among_groups(far)
    other_core = [swap(block, 1) for block in same_core]
    operators = call(
        operator_kernel, "operators", (shape((levels, levels), bf16), shape((levels, levels), f32), shape((levels, LANE), f32)), 3
    )(level_order.reshape(1, levels), stiffness.reshape(1, levels), coupling.reshape(1, levels))
    block = shape((TAIL + back, LANE), bf16)
    send_back = call(
        column_kernel, "column_step", (block,) * GROUPS, 4 * GROUPS + 3,
        [
            pltpu.VMEM((devices * STRIDE, LANE), f32), pltpu.VMEM((16 * devices, LANE), f32),
            pltpu.VMEM((hidden, hidden), bf16), pltpu.VMEM((levels, hidden), f32), pltpu.VMEM((hidden, width), bf16),
            pltpu.VMEM((GROUPS * PIECE, width), bf16), pltpu.VMEM((4 * levels, hidden), f32), pltpu.VMEM((16, LANE), f32),
            pltpu.VMEM((devices * back, LANE), f32), pltpu.VMEM((levels, LANE), f32),
            pltpu.VMEM((hidden, width), bf16), pltpu.VMEM((GROUPS * PIECE, width), bf16),
        ],
    )(*same_core, *other_core, *operators)
    received = among_groups(send_back)
    field_out = shape((rows, LANE), f32)
    new_pressure, new_wind, grad, first_grad, second_grad, third_grad = call(
        functools.partial(finish_kernel, 1.0 / math.sqrt(columns)), "finish",
        (
            field_out, field_out, field_out, shape(weight_one.shape, f32), shape(weight_two.shape, f32),
            shape(weight_three.shape[::-1], f32),
        ),
        GROUPS,
        [pltpu.VMEM((SUB * back, LANE), f32)],
    )(*received)
    return (
        new_pressure.reshape(1, columns), new_wind.reshape(1, columns), grad.reshape(1, columns),
        first_grad, second_grad, third_grad.T,
    )


def fits_tiles(*args):
    pressure, level_order, neighbors = args[0], args[6], args[5]
    weight_one, weight_two, weight_three = args[9:12]
    return (
        pressure.shape[0] == 1
        and level_order.shape[0] == 2 * SUB
        and neighbors.shape[1] % (2 * LANE * SUB) == 0
        and weight_one.shape == (4, 4 * LANE)
        and weight_two.shape == (PIECE, 4 * LANE)
        and weight_three.shape == (PIECE, 2 * SUB)
    )


def any_body(*args):
    return (fast_body if fits_tiles(*args) else body)(*args)


def solution(mesh):
    in_specs = (
        P("slab", "date"),
        P("slab", "date"),
        P("slab", "date"),
        P(None, "slab", "date"),
        P(),
        P(),
        P(),
        P(),
        P(),
        P("slab", None),
        P("slab", None),
        P("slab", None),
        P("slab", "date"),
        P("slab", "date"),
    )
    out_specs = (
        P("slab", "date"),
        P("slab", "date"),
        P("slab", "date"),
        P(("date", "slab"), None),
        P(("date", "slab"), None),
        P(("date", "slab"), None),
    )
    return jax.shard_map(any_body, mesh=mesh, in_specs=in_specs, out_specs=out_specs, check_vma=False)
```

```python
import functools
import math

import jax
import jax.numpy as jnp
from jax import lax
from jax.experimental import pallas as pl
from jax.experimental.pallas import tpu as pltpu
from jax.sharding import PartitionSpec as P


def lower_diff(field):
    return jnp.concatenate([field[1:] - field[:-1], -field[-1:]], axis=0)


def upper_diff(field):
    return jnp.concatenate([jnp.zeros_like(field[:1]), field[:-1]], axis=0) - field


def level_inverse(stiffness):
    below = jnp.concatenate([jnp.zeros((1,), jnp.float32), stiffness[:-1]])
    matrix = (
        jnp.diag(1.0 + stiffness + below)
        - jnp.diag(stiffness[:-1], 1)
        - jnp.diag(stiffness[:-1], -1)
    )
    factor = jnp.linalg.cholesky(matrix)
    identity = jnp.eye(stiffness.shape[0], dtype=jnp.float32)
    return jax.scipy.linalg.cho_solve((factor, True), identity)


def apply_inverse(inverse_matrix, rhs):
    return jnp.dot(
        inverse_matrix, rhs, precision=lax.Precision.HIGHEST, preferred_element_type=jnp.float32
    )


def contract_first(left, right):
    return lax.dot_general(
        left, right, (((0,), (0,)), ((), ())), preferred_element_type=jnp.float32
    )


def contract_last(left, right):
    return lax.dot_general(
        left, right, (((1,), (1,)), ((), ())), preferred_element_type=jnp.float32
    )


def body(
    pressure,
    density,
    vertical_wind,
    horizontal_wind,
    metric_terms,
    neighbors,
    level_order,
    stiffness,
    coupling,
    weight_one,
    weight_two,
    weight_three,
    pressure_adjoint,
    wind_adjoint,
):
    east = jnp.take(horizontal_wind[0], neighbors[0], axis=1)
    west = jnp.take(horizontal_wind[0], neighbors[1], axis=1)
    north = jnp.take(horizontal_wind[1], neighbors[2], axis=1)
    south = jnp.take(horizontal_wind[1], neighbors[3], axis=1)
    diverg = metric_terms[0] * (east - west) + metric_terms[1] * (north - south)
    star = pressure - diverg
    inverse = jnp.argsort(level_order)
    scale = 1.0 / math.sqrt(neighbors.shape[1])
    forward_raw = lax.all_to_all(
        jnp.stack([star, density, vertical_wind, diverg]).astype(jnp.bfloat16),
        "slab",
        split_axis=2,
        concat_axis=1,
        tiled=True,
    ).astype(jnp.float32)
    full_one, full_two, full_three = (
        lax.all_gather(weight_one, "slab", axis=0, tiled=True),
        lax.all_gather(weight_two, "slab", axis=0, tiled=True),
        lax.all_gather(weight_three, "slab", axis=0, tiled=True),
    )
    forward_part = jnp.take(forward_raw, inverse, axis=1)
    levels = forward_part.shape[1]
    width = forward_part.shape[2]
    couple = coupling[:, None]
    column_input = forward_part.reshape(4 * levels, width).astype(jnp.bfloat16)
    pre_one = contract_first(full_one, column_input)
    tanh_one = jnp.tanh(pre_one)
    act_one = tanh_one.astype(jnp.bfloat16)
    pre_two = contract_first(full_two, act_one)
    tanh_two = jnp.tanh(pre_two)
    act_two = tanh_two.astype(jnp.bfloat16)
    heating = contract_first(full_three, act_two)
    star_column = forward_part[0]
    rhs = forward_part[2] - couple * lower_diff(star_column) - 0.5 * forward_part[1] + heating
    inverse_matrix = level_inverse(stiffness)
    wind_next = apply_inverse(inverse_matrix, rhs)
    press_next = star_column + upper_diff(couple * wind_next)
    forward_slabs = lax.all_to_all(
        jnp.take(jnp.stack([press_next, wind_next]), level_order, axis=1).astype(jnp.bfloat16),
        "slab",
        split_axis=1,
        concat_axis=2,
        tiled=True,
    ).astype(jnp.float32)
    adjoint_raw = lax.all_to_all(
        jnp.stack([pressure_adjoint, wind_adjoint]), "slab", split_axis=2, concat_axis=1, tiled=True
    )
    adjoint_part = jnp.take(adjoint_raw, inverse, axis=1)
    wind_grad = adjoint_part[1] + couple * lower_diff(adjoint_part[0])
    rhs_grad = apply_inverse(inverse_matrix, wind_grad)
    star_grad = adjoint_part[0] - upper_diff(couple * rhs_grad)
    heat_grad = rhs_grad.astype(jnp.bfloat16)
    local_three = contract_last(act_two, heat_grad) * scale
    back_two = jnp.dot(full_three, heat_grad, preferred_element_type=jnp.float32)
    pre_two_grad = (back_two * (1.0 - tanh_two * tanh_two)).astype(jnp.bfloat16)
    local_two = contract_last(act_one, pre_two_grad) * scale
    back_one = jnp.dot(full_two, pre_two_grad, preferred_element_type=jnp.float32)
    pre_one_grad = (back_one * (1.0 - tanh_one * tanh_one)).astype(jnp.bfloat16)
    local_one = contract_last(column_input, pre_one_grad) * scale
    first_grad, second_grad, third_grad = (
        lax.psum_scatter(local_one, "slab", scatter_dimension=0, tiled=True),
        lax.psum_scatter(local_two, "slab", scatter_dimension=0, tiled=True),
        lax.psum_scatter(local_three, "slab", scatter_dimension=0, tiled=True),
    )
    input_grad = jnp.dot(full_one, pre_one_grad, preferred_element_type=jnp.float32)
    star_grad = star_grad + input_grad[:levels]
    stored_grad = jnp.take(star_grad, level_order, axis=0)
    pressure_new = forward_slabs[0]
    wind_new = forward_slabs[1]
    pressure_grad = lax.all_to_all(
        stored_grad[None].astype(jnp.bfloat16), "slab", split_axis=1, concat_axis=2, tiled=True
    ).astype(jnp.float32)[0]
    return (pressure_new, wind_new, pressure_grad, first_grad, second_grad, third_grad)


LANE = 128
SUB = 8
STRIDE = 104
NEIGHBORS = (0, 3, 2, 1)
GROUPS = 4
PIECE = 32
HEAD = 4 * PIECE
TAIL = HEAD + 16
FRONT = TAIL + 8


def call(kernel, name, outs, n_in, scratch=(), space=pltpu.VMEM):
    return pl.pallas_call(
        kernel,
        out_shape=outs,
        in_specs=[pl.BlockSpec(memory_space=space) for _ in range(n_in)],
        out_specs=jax.tree.map(lambda _: pl.BlockSpec(memory_space=pltpu.VMEM), outs),
        scratch_shapes=list(scratch),
        compiler_params=pltpu.CompilerParams(vmem_limit_bytes=48 << 20),
        name=name,
    )


def shape(dims, kind):
    return jax.ShapeDtypeStruct(dims, kind)


def pair_up(table):
    half = table.shape[0] // 2
    largest = jnp.max(jnp.max(jnp.abs(table), axis=0, keepdims=True), axis=1, keepdims=True)
    scale = jnp.where(largest > 0.0, 32767.0 / jnp.maximum(largest, 1e-30), 0.0)
    steps = jnp.floor(table * scale + 0.5).astype(jnp.int32)
    return (steps[half:] << 16) | (steps[:half] & 0xFFFF), largest * (1.0 / 32767.0)


def difference(words, first, second):
    half = words.shape[0]
    sublanes = lax.broadcasted_iota(jnp.int32, (SUB, LANE), 0)
    out = []
    for r in range(SUB):
        kept = []
        for index in (first, second):
            row = jnp.broadcast_to(index[r : r + 1, :], (SUB, LANE))
            high, low = row >> 7, row & (LANE - 1)
            late = high >= half
            high = jnp.where(late, high - half, high)
            total = jnp.zeros((SUB, LANE), jnp.int32)
            for g in range(half // SUB):
                picked = jnp.take_along_axis(words[SUB * g : SUB * g + SUB, :], low, axis=1, mode="promise_in_bounds")
                total = jnp.where(high == sublanes + SUB * g, picked, total)
            kept.append(jnp.where(late, total, total << 16) >> 16)
        out.append(jnp.sum((kept[0] - kept[1]).astype(jnp.float32), axis=0, keepdims=True))
    return jnp.concatenate(out, axis=0)


def lane_group(lanes, q):
    return (lanes >= PIECE * q) & (lanes < PIECE * (q + 1))


def pack_kernel(
    p_hbm, d_hbm, w_hbm, u_hbm, m_hbm, n_hbm, one_hbm, two_hbm, three_hbm, pa_hbm, wa_hbm,
    whole_ref, out0_ref, out1_ref, out2_ref, out3_ref,
    p_ref, d_ref, w_ref, u_ref, m_ref, n_ref, one_ref, two_ref, three_ref, pa_ref, wa_ref, part_ref, f_ref, g_ref, sems,
):
    pairs = (
        (n_hbm, n_ref), (u_hbm, u_ref), (m_hbm, m_ref), (p_hbm, p_ref), (d_hbm, d_ref), (w_hbm, w_ref),
        (pa_hbm, pa_ref), (wa_hbm, wa_ref), (one_hbm, one_ref), (two_hbm, two_ref), (three_hbm, three_ref),
    )
    copies = [pltpu.make_async_copy(source, target, sems.at[i]) for i, (source, target) in enumerate(pairs)]
    for copy in copies:
        copy.start()
    f32, bf16 = jnp.float32, jnp.bfloat16
    piece = f_ref.shape[0] // SUB
    blocks = p_ref.shape[0] // SUB
    for copy in copies:
        copy.wait()

    def put(f, j, tile):
        f_ref[pl.ds(blocks * f + j, SUB, stride=piece), :] = tile

    words_one, step_one = pair_up(u_ref[0])
    words_two, step_two = pair_up(u_ref[1])
    for j in range(blocks):
        rows = slice(SUB * j, SUB * j + SUB)
        along = difference(words_one, n_ref[rows, 0, :], n_ref[rows, 1, :]) * step_one
        across = difference(words_two, n_ref[rows, 2, :], n_ref[rows, 3, :]) * step_two
        diverg = m_ref[rows, 0, :] * along + m_ref[rows, 1, :] * across
        for f, tile in enumerate((p_ref[rows, :] - diverg, d_ref[rows, :], w_ref[rows, :], diverg, pa_ref[rows, :], wa_ref[rows, :])):
            put(f, j, tile)
    lanes = lax.broadcasted_iota(jnp.int32, (PIECE, LANE), 1)
    spread = (lanes % PIECE == lax.broadcasted_iota(jnp.int32, (PIECE, LANE), 0)).astype(f32).astype(bf16)
    part_ref[...] = jnp.dot(three_ref[...], spread, preferred_element_type=f32)
    lanes = lax.broadcasted_iota(jnp.int32, (4, LANE), 1)
    three = jnp.zeros((4, LANE), f32)
    for q in range(4):
        three = jnp.where(lane_group(lanes, q), part_ref[4 * q : 4 * q + 4, :], three)
    one = one_ref[...].astype(f32)
    for q in range(4):
        part_ref[4 * q : 4 * q + 4, :] = one[:, LANE * q : LANE * (q + 1)]
    one = part_ref[...].astype(bf16)
    part_ref[0:4, :] = three
    part_ref[4:8, :] = jnp.zeros((4, LANE), f32)
    three = part_ref[0:8, :].astype(bf16)
    for g in range(GROUPS):
        both = [f_ref[piece * c : piece * (c + 1), :] for c in (g, g + GROUPS)]
        g_ref[2 * piece * g : 2 * piece * (g + 1), :] = jnp.concatenate(both, axis=0)
    group = lax.axis_index("slab") // 2 % GROUPS
    outs = (out0_ref, out1_ref, out2_ref, out3_ref)
    for ref in (whole_ref,) + outs:
        for q in range(4):
            ref[PIECE * q : PIECE * (q + 1), :] = two_ref[:, LANE * q : LANE * (q + 1)]
        ref[HEAD:TAIL, :] = one
        ref[TAIL:FRONT, :] = three
    whole_ref[FRONT:, :] = g_ref[...].astype(bf16)
    for k, ref in enumerate(outs):
        ref[FRONT:, :] = g_ref[pl.ds(pl.multiple_of(2 * piece * (group ^ k), SUB), 2 * piece), :].astype(bf16)


def relay_kernel(whole_ref, out0_ref, out1_ref, out2_ref, out3_ref, g_ref):
    size = out0_ref.shape[0] - FRONT
    group = lax.axis_index("slab") // 2 % GROUPS
    g_ref[...] = whole_ref[FRONT:, :].astype(jnp.float32)
    for k, ref in enumerate((out0_ref, out1_ref, out2_ref, out3_ref)):
        ref[:FRONT, :] = whole_ref[:FRONT, :]
        ref[FRONT:, :] = g_ref[pl.ds(pl.multiple_of(size * (group ^ k), SUB), size), :].astype(jnp.bfloat16)


def shifted_up(field, rows):
    return jnp.where(rows < field.shape[0] - 1, pltpu.roll(field, field.shape[0] - 1, 0), 0.0)


def shifted_down(field, rows):
    return jnp.where(rows > 0, pltpu.roll(field, 1, 0), 0.0)


def operator_inverse(stiff, rows):
    size = stiff.shape[0]
    below = shifted_down(stiff, rows)
    lower, diagonal = -below, 1.0 + stiff + below
    upper = jnp.where(rows < size - 1, -stiff, 0.0)
    right = (rows == lax.broadcasted_iota(jnp.int32, (size, size), 1)).astype(jnp.float32)
    distance = 1
    while distance < size:
        down = lambda v: pltpu.roll(v, distance, 0)
        up = lambda v: pltpu.roll(v, size - distance, 0)
        alpha, gamma = -lower / down(diagonal), -upper / up(diagonal)
        right = right + alpha * down(right) + gamma * up(right)
        diagonal = diagonal + alpha * down(upper) + gamma * up(lower)
        lower, upper = alpha * down(lower), gamma * up(upper)
        distance *= 2
    return right / diagonal


def operator_kernel(order_ref, stiff_ref, couple_ref, place_ref, inverse_ref, column_ref):
    levels = inverse_ref.shape[0]
    rows = lax.broadcasted_iota(jnp.int32, (levels, levels), 0)
    diagonal = rows == lax.broadcasted_iota(jnp.int32, (levels, levels), 1)
    place_ref[...] = (order_ref[...] == rows).astype(jnp.float32).astype(jnp.bfloat16)
    stiff = jnp.sum(jnp.where(diagonal, stiff_ref[...], 0.0), axis=1, keepdims=True)
    couple = jnp.sum(jnp.where(diagonal, couple_ref[...], 0.0), axis=1, keepdims=True)
    inverse_ref[...] = operator_inverse(jnp.broadcast_to(stiff, (levels, levels)), rows)
    column_ref[...] = jnp.broadcast_to(couple, column_ref.shape)


def column_kernel(*refs):
    sources = refs[: 4 * GROUPS]
    place_ref, inverse_ref, column_ref, out0_ref, out1_ref, out2_ref, out3_ref = refs[4 * GROUPS : 4 * GROUPS + 7]
    (
        a_ref, one_ref, w2_ref, w3_ref, act_ref, sel_ref, g_ref, h_ref, y_ref, t_ref, act2_ref, sel2_ref,
    ) = refs[4 * GROUPS + 7 :]
    f32, bf16 = jnp.float32, jnp.bfloat16
    device = lax.axis_index("slab")
    core = device % 2
    devices = 4 * GROUPS
    levels = inverse_ref.shape[0]
    width = act_ref.shape[1]
    blocks = width // LANE
    half = blocks // 2
    stride = a_ref.shape[0] // devices
    size = sources[0].shape[0] - HEAD
    for i, ref in enumerate(sources):
        source = device ^ (2 * NEIGHBORS[i % GROUPS] + SUB * (i // GROUPS % 2) + i // (2 * GROUPS))
        for q in range(4):
            rows = pl.ds(pl.multiple_of(PIECE * source, PIECE), PIECE)
            w2_ref[rows, LANE * q : LANE * (q + 1)] = ref[PIECE * q : PIECE * (q + 1), :]
        a_ref[pl.ds(pl.multiple_of(stride * source, SUB), size), :] = ref[HEAD:, :].astype(f32)
    for q in range(4):
        for r in range(4):
            one_ref[pl.ds(4 * devices * q + r, devices, stride=4), :] = a_ref[pl.ds(4 * q + r, devices, stride=stride), :]
    one = jnp.concatenate([one_ref[4 * devices * q : 4 * devices * (q + 1), :] for q in range(4)], axis=1)
    lanes = lax.broadcasted_iota(jnp.int32, (4, LANE), 1)
    for t in range(devices // 4):
        packed = [a_ref[stride * (4 * t + s) + 16 : stride * (4 * t + s) + 20, :] for s in range(4)]
        for q in range(4):
            tile = jnp.zeros((4, LANE), f32)
            for s in range(4):
                moved = packed[s] if s == q else pltpu.roll(packed[s], PIECE * ((s - q) % 4), 1)
                tile = jnp.where(lane_group(lanes, s), moved, tile)
            w3_ref[4 * q : 4 * q + 4, LANE * t : LANE * (t + 1)] = tile
    w1t = one.T.astype(bf16)
    w1s = one[:levels, :].astype(bf16)
    w2 = w2_ref[...]
    w3t = w3_ref[...].astype(bf16)
    w3 = w3_ref[...].T.astype(bf16)
    place, inverse = place_ref[...], inverse_ref[...]
    order = [24 + 6 * half * b + half * f + j for f in range(6) for b in range(2) for j in range(half)]
    raw = jnp.concatenate([a_ref[pl.ds(k, levels, stride=stride), :] for k in order], axis=1)
    ordered = jnp.dot(place, raw.astype(bf16), preferred_element_type=f32)
    star, density, vertical, diverg, pressure_adjoint, wind_adjoint = (
        ordered[:, width * i : width * (i + 1)] for i in range(6)
    )
    couple = jnp.concatenate([column_ref[...]] * blocks, axis=1)
    rows = lax.broadcasted_iota(jnp.int32, (levels, width), 0)

    def solve(right):
        return jnp.dot(inverse, right, precision=lax.Precision.HIGHEST, preferred_element_type=f32)

    def lower(field):
        return shifted_up(field, rows) - field

    def upper(field):
        return shifted_down(field, rows) - field

    column_input = jnp.concatenate([star, density, vertical, diverg], axis=0).astype(bf16)
    tanh_one = jnp.tanh(jnp.dot(w1t, column_input, preferred_element_type=f32))
    act_one = tanh_one.astype(bf16)
    act_ref[...] = act_one
    rhs_grad = solve(wind_adjoint + couple * lower(pressure_adjoint))
    star_part = pressure_adjoint - upper(couple * rhs_grad)
    heat_grad = rhs_grad.astype(bf16)
    tanh_two = jnp.tanh(contract_first(w2, act_one))
    act_two = tanh_two.astype(bf16)
    act2_ref[...] = act_two
    back_two = jnp.dot(w3, heat_grad, preferred_element_type=f32)
    pre_two_grad = (back_two * (1.0 - tanh_two * tanh_two)).astype(bf16)
    back_one = jnp.dot(w2, pre_two_grad, preferred_element_type=f32)
    pre_one_grad = (back_one * (1.0 - tanh_one * tanh_one)).astype(bf16)
    heating = jnp.dot(w3t, act_two, preferred_element_type=f32)
    wind_next = solve(vertical - couple * lower(star) - 0.5 * density + heating)
    press_next = star + upper(couple * wind_next)
    star_grad = star_part + jnp.dot(w1s, pre_one_grad, preferred_element_type=f32)
    outs = (out0_ref, out1_ref, out2_ref, out3_ref)
    targets = [device ^ (2 * k) for k in range(GROUPS)]
    for k, target in enumerate(targets):
        hid = pl.ds(pl.multiple_of(PIECE * target, PIECE), PIECE)
        sel_ref[PIECE * k : PIECE * (k + 1), :] = act_ref[hid, :]
        sel2_ref[PIECE * k : PIECE * (k + 1), :] = act2_ref[hid, :]
    local_two = contract_last(sel_ref[...], pre_two_grad)
    local_three = contract_last(heat_grad, sel2_ref[...])
    g_ref[...] = contract_last(column_input, pre_one_grad)
    fields = jnp.concatenate([press_next, wind_next, star_grad], axis=1).astype(bf16)
    stored = lax.dot_general(place, fields, (((0,), (0,)), ((), ())), preferred_element_type=f32)
    back = out0_ref.shape[0] - TAIL
    for k in range(3 * blocks):
        y_ref[pl.ds(4 + k, devices, stride=back), :] = stored[:, LANE * k : LANE * (k + 1)]
    for k in range(4 + 3 * blocks, back):
        y_ref[pl.ds(k, devices, stride=back), :] = jnp.zeros((devices, LANE), f32)
    t_ref[...] = local_three
    for k, (target, out_ref) in enumerate(zip(targets, outs)):
        pair = g_ref[pl.ds(pl.multiple_of(SUB * (target // 2), SUB), SUB), :]
        one = jnp.where(core == 0, pair[:4, :], pair[4:, :])
        tile = t_ref[...] if k == 0 else pltpu.roll(t_ref[...], LANE - PIECE * k, 1)
        three = tile[:4, :]
        for q in range(4):
            cols = slice(LANE * q, LANE * (q + 1))
            out_ref[PIECE * q : PIECE * (q + 1), :] = local_two[PIECE * k : PIECE * (k + 1), cols].astype(bf16)
            h_ref[4 * q : 4 * q + 4, :] = one[:, cols]
            if q > 0:
                three = jnp.where(lane_group(lanes, q), pltpu.roll(tile[4 * q : 4 * q + 4, :], PIECE * q, 1), three)
        out_ref[HEAD:TAIL, :] = h_ref[...].astype(bf16)
        start = pl.multiple_of(back * target, SUB)
        y_ref[pl.ds(start, 4), :] = three
        out_ref[TAIL:, :] = y_ref[pl.ds(start, back), :].astype(bf16)


def finish_kernel(scale, r0_ref, r3_ref, r2_ref, r1_ref, p_ref, w_ref, g_ref, one_ref, two_ref, three_ref, y_ref):
    received = (r0_ref, r1_ref, r2_ref, r3_ref)
    back = r0_ref.shape[0] - TAIL
    half = p_ref.shape[0] // SUB
    group = lax.axis_index("slab") // 2 % GROUPS

    def total(start, stop):
        return sum(ref[start:stop, :].astype(jnp.float32) for ref in received) * scale

    for q in range(4):
        two_ref[:, LANE * q : LANE * (q + 1)] = total(PIECE * q, PIECE * (q + 1))
    one = total(HEAD, TAIL)
    for q in range(4):
        one_ref[:, LANE * q : LANE * (q + 1)] = one[4 * q : 4 * q + 4, :]
    for k, ref in enumerate(received):
        y_ref[pl.ds(pl.multiple_of(back * (group ^ k), SUB), back), :] = ref[TAIL:, :].astype(jnp.float32)
    three = sum(y_ref[back * g : back * g + 4, :] for g in range(GROUPS)) * scale
    for q in range(4):
        three_ref[4 * q : 4 * q + 4, :] = three[:, PIECE * q : PIECE * (q + 1)]
    for f, ref in enumerate((p_ref, w_ref, g_ref)):
        for j in range(half):
            for b in range(2):
                rows = pl.ds(4 + 2 * half * f + half * b + j, GROUPS, stride=back)
                ref[SUB * j + GROUPS * b : SUB * j + GROUPS * (b + 1), :] = y_ref[rows, :]


def fast_body(
    pressure, density, vertical_wind, horizontal_wind, metric_terms, neighbors, level_order, stiffness, coupling,
    weight_one, weight_two, weight_three, pressure_adjoint, wind_adjoint,
):
    levels = devices = level_order.shape[0]
    columns = neighbors.shape[1]
    rows = columns // LANE
    blocks = rows // GROUPS
    width = blocks * LANE
    hidden = weight_two.shape[1]
    f32, bf16 = jnp.float32, jnp.bfloat16

    def pad(count):
        return -(-count // SUB) * SUB

    def view(field):
        return field.reshape(rows, LANE)

    def lanes(table):
        return table.reshape(table.shape[0], rows, LANE).transpose(1, 0, 2)

    def swap(array, bits):
        return lax.ppermute(array, "slab", [(i, i ^ bits) for i in range(devices)])

    def among_groups(outgoing, order=range(GROUPS)):
        return [outgoing[0]] + [swap(outgoing[k], 2 * k) for k in order[1:]]

    sources = (
        view(pressure), view(density), view(vertical_wind), horizontal_wind.reshape(2, rows, LANE), lanes(metric_terms),
        lanes(neighbors), weight_one, weight_two, weight_three.T, view(pressure_adjoint), view(wind_adjoint),
    )
    piece, back = 3 * blocks, pad(4 + 3 * blocks)
    one_group = (shape((FRONT + 2 * piece, LANE), bf16),) * GROUPS
    all_groups = pltpu.VMEM((GROUPS * 2 * piece, LANE), f32)
    whole, *near = call(
        pack_kernel, "pack", (shape((FRONT + GROUPS * 2 * piece, LANE), bf16),) + one_group, len(sources),
        [pltpu.VMEM(source.shape, source.dtype) for source in sources]
        + [pltpu.VMEM((16, LANE), f32), pltpu.VMEM((SUB * piece, LANE), f32), all_groups, pltpu.SemaphoreType.DMA((len(sources),))],
        pltpu.HBM,
    )(*(pltpu.with_memory_space_constraint(source, pltpu.HBM) for source in sources))
    far = call(relay_kernel, "relay", one_group, 1, [all_groups])(swap(whole, SUB))
    near = among_groups(near, NEIGHBORS)
    far = among_groups(far, NEIGHBORS)
    *near, far[1] = lax.optimization_barrier((*near, far[1]))
    same_core = near + far
    other_core = [swap(block, 1) for block in same_core]
    operators = call(
        operator_kernel, "operators", (shape((levels, levels), bf16), shape((levels, levels), f32), shape((levels, LANE), f32)), 3
    )(level_order.reshape(1, levels), stiffness.reshape(1, levels), coupling.reshape(1, levels))
    block = shape((TAIL + back, LANE), bf16)
    send_back = call(
        column_kernel, "column_step", (block,) * GROUPS, 4 * GROUPS + 3,
        [
            pltpu.VMEM((devices * STRIDE, LANE), f32), pltpu.VMEM((16 * devices, LANE), f32),
            pltpu.VMEM((hidden, hidden), bf16), pltpu.VMEM((levels, hidden), f32), pltpu.VMEM((hidden, width), bf16),
            pltpu.VMEM((GROUPS * PIECE, width), bf16), pltpu.VMEM((4 * levels, hidden), f32), pltpu.VMEM((16, LANE), f32),
            pltpu.VMEM((devices * back, LANE), f32), pltpu.VMEM((levels, LANE), f32),
            pltpu.VMEM((hidden, width), bf16), pltpu.VMEM((GROUPS * PIECE, width), bf16),
        ],
    )(*same_core, *other_core, *operators)
    received = among_groups(send_back, (0, 3, 2, 1))
    field_out = shape((rows, LANE), f32)
    new_pressure, new_wind, grad, first_grad, second_grad, third_grad = call(
        functools.partial(finish_kernel, 1.0 / math.sqrt(columns)), "finish",
        (
            field_out, field_out, field_out, shape(weight_one.shape, f32), shape(weight_two.shape, f32),
            shape(weight_three.shape[::-1], f32),
        ),
        GROUPS,
        [pltpu.VMEM((SUB * back, LANE), f32)],
    )(*received)
    return (
        new_pressure.reshape(1, columns), new_wind.reshape(1, columns), grad.reshape(1, columns),
        first_grad, second_grad, third_grad.T,
    )


def fits_tiles(*args):
    pressure, level_order, neighbors = args[0], args[6], args[5]
    weight_one, weight_two, weight_three = args[9:12]
    return (
        pressure.shape[0] == 1
        and level_order.shape[0] == 2 * SUB
        and neighbors.shape[1] % (2 * LANE * SUB) == 0
        and weight_one.shape == (4, 4 * LANE)
        and weight_two.shape == (PIECE, 4 * LANE)
        and weight_three.shape == (PIECE, 2 * SUB)
    )


def any_body(*args):
    return (fast_body if fits_tiles(*args) else body)(*args)


def solution(mesh):
    in_specs = (
        P("slab", "date"),
        P("slab", "date"),
        P("slab", "date"),
        P(None, "slab", "date"),
        P(),
        P(),
        P(),
        P(),
        P(),
        P("slab", None),
        P("slab", None),
        P("slab", None),
        P("slab", "date"),
        P("slab", "date"),
    )
    out_specs = (
        P("slab", "date"),
        P("slab", "date"),
        P("slab", "date"),
        P(("date", "slab"), None),
        P(("date", "slab"), None),
        P(("date", "slab"), None),
    )
    return jax.shard_map(any_body, mesh=mesh, in_specs=in_specs, out_specs=out_specs, check_vma=False)
```

```python
import functools
import math

import jax
import jax.numpy as jnp
from jax import lax
from jax.experimental import pallas as pl
from jax.experimental.pallas import tpu as pltpu
from jax.sharding import PartitionSpec as P


def lower_diff(field):
    return jnp.concatenate([field[1:] - field[:-1], -field[-1:]], axis=0)


def upper_diff(field):
    return jnp.concatenate([jnp.zeros_like(field[:1]), field[:-1]], axis=0) - field


def level_inverse(stiffness):
    below = jnp.concatenate([jnp.zeros((1,), jnp.float32), stiffness[:-1]])
    matrix = (
        jnp.diag(1.0 + stiffness + below)
        - jnp.diag(stiffness[:-1], 1)
        - jnp.diag(stiffness[:-1], -1)
    )
    factor = jnp.linalg.cholesky(matrix)
    identity = jnp.eye(stiffness.shape[0], dtype=jnp.float32)
    return jax.scipy.linalg.cho_solve((factor, True), identity)


def apply_inverse(inverse_matrix, rhs):
    return jnp.dot(
        inverse_matrix, rhs, precision=lax.Precision.HIGHEST, preferred_element_type=jnp.float32
    )


def contract_first(left, right):
    return lax.dot_general(
        left, right, (((0,), (0,)), ((), ())), preferred_element_type=jnp.float32
    )


def contract_last(left, right):
    return lax.dot_general(
        left, right, (((1,), (1,)), ((), ())), preferred_element_type=jnp.float32
    )


def body(
    pressure,
    density,
    vertical_wind,
    horizontal_wind,
    metric_terms,
    neighbors,
    level_order,
    stiffness,
    coupling,
    weight_one,
    weight_two,
    weight_three,
    pressure_adjoint,
    wind_adjoint,
):
    east = jnp.take(horizontal_wind[0], neighbors[0], axis=1)
    west = jnp.take(horizontal_wind[0], neighbors[1], axis=1)
    north = jnp.take(horizontal_wind[1], neighbors[2], axis=1)
    south = jnp.take(horizontal_wind[1], neighbors[3], axis=1)
    diverg = metric_terms[0] * (east - west) + metric_terms[1] * (north - south)
    star = pressure - diverg
    inverse = jnp.argsort(level_order)
    scale = 1.0 / math.sqrt(neighbors.shape[1])
    forward_raw = lax.all_to_all(
        jnp.stack([star, density, vertical_wind, diverg]).astype(jnp.bfloat16),
        "slab",
        split_axis=2,
        concat_axis=1,
        tiled=True,
    ).astype(jnp.float32)
    full_one, full_two, full_three = (
        lax.all_gather(weight_one, "slab", axis=0, tiled=True),
        lax.all_gather(weight_two, "slab", axis=0, tiled=True),
        lax.all_gather(weight_three, "slab", axis=0, tiled=True),
    )
    forward_part = jnp.take(forward_raw, inverse, axis=1)
    levels = forward_part.shape[1]
    width = forward_part.shape[2]
    couple = coupling[:, None]
    column_input = forward_part.reshape(4 * levels, width).astype(jnp.bfloat16)
    pre_one = contract_first(full_one, column_input)
    tanh_one = jnp.tanh(pre_one)
    act_one = tanh_one.astype(jnp.bfloat16)
    pre_two = contract_first(full_two, act_one)
    tanh_two = jnp.tanh(pre_two)
    act_two = tanh_two.astype(jnp.bfloat16)
    heating = contract_first(full_three, act_two)
    star_column = forward_part[0]
    rhs = forward_part[2] - couple * lower_diff(star_column) - 0.5 * forward_part[1] + heating
    inverse_matrix = level_inverse(stiffness)
    wind_next = apply_inverse(inverse_matrix, rhs)
    press_next = star_column + upper_diff(couple * wind_next)
    forward_slabs = lax.all_to_all(
        jnp.take(jnp.stack([press_next, wind_next]), level_order, axis=1).astype(jnp.bfloat16),
        "slab",
        split_axis=1,
        concat_axis=2,
        tiled=True,
    ).astype(jnp.float32)
    adjoint_raw = lax.all_to_all(
        jnp.stack([pressure_adjoint, wind_adjoint]), "slab", split_axis=2, concat_axis=1, tiled=True
    )
    adjoint_part = jnp.take(adjoint_raw, inverse, axis=1)
    wind_grad = adjoint_part[1] + couple * lower_diff(adjoint_part[0])
    rhs_grad = apply_inverse(inverse_matrix, wind_grad)
    star_grad = adjoint_part[0] - upper_diff(couple * rhs_grad)
    heat_grad = rhs_grad.astype(jnp.bfloat16)
    local_three = contract_last(act_two, heat_grad) * scale
    back_two = jnp.dot(full_three, heat_grad, preferred_element_type=jnp.float32)
    pre_two_grad = (back_two * (1.0 - tanh_two * tanh_two)).astype(jnp.bfloat16)
    local_two = contract_last(act_one, pre_two_grad) * scale
    back_one = jnp.dot(full_two, pre_two_grad, preferred_element_type=jnp.float32)
    pre_one_grad = (back_one * (1.0 - tanh_one * tanh_one)).astype(jnp.bfloat16)
    local_one = contract_last(column_input, pre_one_grad) * scale
    first_grad, second_grad, third_grad = (
        lax.psum_scatter(local_one, "slab", scatter_dimension=0, tiled=True),
        lax.psum_scatter(local_two, "slab", scatter_dimension=0, tiled=True),
        lax.psum_scatter(local_three, "slab", scatter_dimension=0, tiled=True),
    )
    input_grad = jnp.dot(full_one, pre_one_grad, preferred_element_type=jnp.float32)
    star_grad = star_grad + input_grad[:levels]
    stored_grad = jnp.take(star_grad, level_order, axis=0)
    pressure_new = forward_slabs[0]
    wind_new = forward_slabs[1]
    pressure_grad = lax.all_to_all(
        stored_grad[None].astype(jnp.bfloat16), "slab", split_axis=1, concat_axis=2, tiled=True
    ).astype(jnp.float32)[0]
    return (pressure_new, wind_new, pressure_grad, first_grad, second_grad, third_grad)


LANE = 128
SUB = 8
STRIDE = 104
NEIGHBORS = (0, 3, 2, 1)
GROUPS = 4
PIECE = 32
HEAD = 4 * PIECE
TAIL = HEAD + 16
FRONT = TAIL + 8


def call(kernel, name, outs, n_in, scratch=(), space=pltpu.VMEM):
    return pl.pallas_call(
        kernel,
        out_shape=outs,
        in_specs=[pl.BlockSpec(memory_space=space) for _ in range(n_in)],
        out_specs=jax.tree.map(lambda _: pl.BlockSpec(memory_space=pltpu.VMEM), outs),
        scratch_shapes=list(scratch),
        compiler_params=pltpu.CompilerParams(vmem_limit_bytes=48 << 20),
        name=name,
    )


def shape(dims, kind):
    return jax.ShapeDtypeStruct(dims, kind)


def pair_up(table):
    half = table.shape[0] // 2
    largest = jnp.max(jnp.max(jnp.abs(table), axis=0, keepdims=True), axis=1, keepdims=True)
    scale = jnp.where(largest > 0.0, 32767.0 / jnp.maximum(largest, 1e-30), 0.0)
    steps = jnp.floor(table * scale + 0.5).astype(jnp.int32)
    return (steps[half:] << 16) | (steps[:half] & 0xFFFF), largest * (1.0 / 32767.0)


def difference(words, first, second):
    half = words.shape[0]
    sublanes = lax.broadcasted_iota(jnp.int32, (SUB, LANE), 0)
    out = []
    for r in range(SUB):
        kept = []
        for index in (first, second):
            row = jnp.broadcast_to(index[r : r + 1, :], (SUB, LANE))
            high, low = row >> 7, row & (LANE - 1)
            late = high >= half
            high = jnp.where(late, high - half, high)
            total = jnp.zeros((SUB, LANE), jnp.int32)
            for g in range(half // SUB):
                picked = jnp.take_along_axis(words[SUB * g : SUB * g + SUB, :], low, axis=1, mode="promise_in_bounds")
                total = jnp.where(high == sublanes + SUB * g, picked, total)
            kept.append(jnp.where(late, total, total << 16) >> 16)
        out.append(jnp.sum((kept[0] - kept[1]).astype(jnp.float32), axis=0, keepdims=True))
    return jnp.concatenate(out, axis=0)


def lane_group(lanes, q):
    return (lanes >= PIECE * q) & (lanes < PIECE * (q + 1))


def pack_kernel(
    p_hbm, d_hbm, w_hbm, u_hbm, m_hbm, n_hbm, one_hbm, two_hbm, three_hbm, pa_hbm, wa_hbm,
    whole_ref, out0_ref, out1_ref, out2_ref, out3_ref,
    p_ref, d_ref, w_ref, u_ref, m_ref, n_ref, one_ref, two_ref, three_ref, pa_ref, wa_ref, part_ref, f_ref, g_ref, sems,
):
    pairs = (
        (n_hbm, n_ref), (u_hbm, u_ref), (m_hbm, m_ref), (p_hbm, p_ref), (d_hbm, d_ref), (w_hbm, w_ref),
        (pa_hbm, pa_ref), (wa_hbm, wa_ref), (one_hbm, one_ref), (two_hbm, two_ref), (three_hbm, three_ref),
    )
    copies = [pltpu.make_async_copy(source, target, sems.at[i]) for i, (source, target) in enumerate(pairs)]
    for copy in copies:
        copy.start()
    f32, bf16 = jnp.float32, jnp.bfloat16
    piece = f_ref.shape[0] // SUB
    blocks = p_ref.shape[0] // SUB
    for copy in copies:
        copy.wait()

    def put(f, j, tile):
        f_ref[pl.ds(blocks * f + j, SUB, stride=piece), :] = tile

    words_one, step_one = pair_up(u_ref[0])
    words_two, step_two = pair_up(u_ref[1])
    for j in range(blocks):
        rows = slice(SUB * j, SUB * j + SUB)
        along = difference(words_one, n_ref[rows, 0, :], n_ref[rows, 1, :]) * step_one
        across = difference(words_two, n_ref[rows, 2, :], n_ref[rows, 3, :]) * step_two
        diverg = m_ref[rows, 0, :] * along + m_ref[rows, 1, :] * across
        for f, tile in enumerate((p_ref[rows, :] - diverg, d_ref[rows, :], w_ref[rows, :], diverg, pa_ref[rows, :], wa_ref[rows, :])):
            put(f, j, tile)
    lanes = lax.broadcasted_iota(jnp.int32, (PIECE, LANE), 1)
    spread = (lanes % PIECE == lax.broadcasted_iota(jnp.int32, (PIECE, LANE), 0)).astype(f32).astype(bf16)
    part_ref[...] = jnp.dot(three_ref[...], spread, preferred_element_type=f32)
    lanes = lax.broadcasted_iota(jnp.int32, (4, LANE), 1)
    three = jnp.zeros((4, LANE), f32)
    for q in range(4):
        three = jnp.where(lane_group(lanes, q), part_ref[4 * q : 4 * q + 4, :], three)
    one = one_ref[...].astype(f32)
    for q in range(4):
        part_ref[4 * q : 4 * q + 4, :] = one[:, LANE * q : LANE * (q + 1)]
    one = part_ref[...].astype(bf16)
    part_ref[0:4, :] = three
    part_ref[4:8, :] = jnp.zeros((4, LANE), f32)
    three = part_ref[0:8, :].astype(bf16)
    for g in range(GROUPS):
        both = [f_ref[piece * c : piece * (c + 1), :] for c in (g, g + GROUPS)]
        g_ref[2 * piece * g : 2 * piece * (g + 1), :] = jnp.concatenate(both, axis=0)
    group = lax.axis_index("slab") // 2 % GROUPS
    outs = (out0_ref, out1_ref, out2_ref, out3_ref)
    for ref in (whole_ref,) + outs:
        for q in range(4):
            ref[PIECE * q : PIECE * (q + 1), :] = two_ref[:, LANE * q : LANE * (q + 1)]
        ref[HEAD:TAIL, :] = one
        ref[TAIL:FRONT, :] = three
    whole_ref[FRONT:, :] = g_ref[...].astype(bf16)
    for k, ref in enumerate(outs):
        ref[FRONT:, :] = g_ref[pl.ds(pl.multiple_of(2 * piece * (group ^ k), SUB), 2 * piece), :].astype(bf16)


def relay_kernel(whole_ref, out0_ref, out1_ref, out2_ref, out3_ref, g_ref):
    size = out0_ref.shape[0] - FRONT
    group = lax.axis_index("slab") // 2 % GROUPS
    g_ref[...] = whole_ref[FRONT:, :].astype(jnp.float32)
    for k, ref in enumerate((out0_ref, out1_ref, out2_ref, out3_ref)):
        ref[:FRONT, :] = whole_ref[:FRONT, :]
        ref[FRONT:, :] = g_ref[pl.ds(pl.multiple_of(size * (group ^ k), SUB), size), :].astype(jnp.bfloat16)


def shifted_up(field, rows):
    return jnp.where(rows < field.shape[0] - 1, pltpu.roll(field, field.shape[0] - 1, 0), 0.0)


def shifted_down(field, rows):
    return jnp.where(rows > 0, pltpu.roll(field, 1, 0), 0.0)


def operator_inverse(stiff, rows):
    size = stiff.shape[0]
    below = shifted_down(stiff, rows)
    lower, diagonal = -below, 1.0 + stiff + below
    upper = jnp.where(rows < size - 1, -stiff, 0.0)
    right = (rows == lax.broadcasted_iota(jnp.int32, (size, size), 1)).astype(jnp.float32)
    distance = 1
    while distance < size:
        down = lambda v: pltpu.roll(v, distance, 0)
        up = lambda v: pltpu.roll(v, size - distance, 0)
        alpha, gamma = -lower / down(diagonal), -upper / up(diagonal)
        right = right + alpha * down(right) + gamma * up(right)
        diagonal = diagonal + alpha * down(upper) + gamma * up(lower)
        lower, upper = alpha * down(lower), gamma * up(upper)
        distance *= 2
    return right / diagonal


def operator_kernel(order_ref, stiff_ref, couple_ref, place_ref, inverse_ref, column_ref):
    levels = inverse_ref.shape[0]
    rows = lax.broadcasted_iota(jnp.int32, (levels, levels), 0)
    diagonal = rows == lax.broadcasted_iota(jnp.int32, (levels, levels), 1)
    place_ref[...] = (order_ref[...] == rows).astype(jnp.float32).astype(jnp.bfloat16)
    stiff = jnp.sum(jnp.where(diagonal, stiff_ref[...], 0.0), axis=1, keepdims=True)
    couple = jnp.sum(jnp.where(diagonal, couple_ref[...], 0.0), axis=1, keepdims=True)
    inverse_ref[...] = operator_inverse(jnp.broadcast_to(stiff, (levels, levels)), rows)
    column_ref[...] = jnp.broadcast_to(couple, column_ref.shape)


def column_kernel(*refs):
    sources = refs[: 4 * GROUPS]
    place_ref, inverse_ref, column_ref, out0_ref, out1_ref, out2_ref, out3_ref = refs[4 * GROUPS : 4 * GROUPS + 7]
    (
        a_ref, one_ref, w2_ref, w3_ref, act_ref, sel_ref, g_ref, h_ref, y_ref, t_ref, act2_ref, sel2_ref,
    ) = refs[4 * GROUPS + 7 :]
    f32, bf16 = jnp.float32, jnp.bfloat16
    device = lax.axis_index("slab")
    core = device % 2
    devices = 4 * GROUPS
    levels = inverse_ref.shape[0]
    width = act_ref.shape[1]
    blocks = width // LANE
    half = blocks // 2
    stride = a_ref.shape[0] // devices
    size = sources[0].shape[0] - HEAD
    for i, ref in enumerate(sources):
        source = device ^ (2 * NEIGHBORS[i % GROUPS] + SUB * (i // GROUPS % 2) + i // (2 * GROUPS))
        for q in range(4):
            rows = pl.ds(pl.multiple_of(PIECE * source, PIECE), PIECE)
            w2_ref[rows, LANE * q : LANE * (q + 1)] = ref[PIECE * q : PIECE * (q + 1), :]
        a_ref[pl.ds(pl.multiple_of(stride * source, SUB), size), :] = ref[HEAD:, :].astype(f32)
    for q in range(4):
        for r in range(4):
            one_ref[pl.ds(4 * devices * q + r, devices, stride=4), :] = a_ref[pl.ds(4 * q + r, devices, stride=stride), :]
    one = jnp.concatenate([one_ref[4 * devices * q : 4 * devices * (q + 1), :] for q in range(4)], axis=1)
    lanes = lax.broadcasted_iota(jnp.int32, (4, LANE), 1)
    for t in range(devices // 4):
        packed = [a_ref[stride * (4 * t + s) + 16 : stride * (4 * t + s) + 20, :] for s in range(4)]
        for q in range(4):
            tile = jnp.zeros((4, LANE), f32)
            for s in range(4):
                moved = packed[s] if s == q else pltpu.roll(packed[s], PIECE * ((s - q) % 4), 1)
                tile = jnp.where(lane_group(lanes, s), moved, tile)
            w3_ref[4 * q : 4 * q + 4, LANE * t : LANE * (t + 1)] = tile
    w1t = one.T.astype(bf16)
    w1s = one[:levels, :].astype(bf16)
    w2 = w2_ref[...]
    w3t = w3_ref[...].astype(bf16)
    w3 = w3_ref[...].T.astype(bf16)
    place, inverse = place_ref[...], inverse_ref[...]
    order = [24 + 6 * half * b + half * f + j for f in range(6) for b in range(2) for j in range(half)]
    raw = jnp.concatenate([a_ref[pl.ds(k, levels, stride=stride), :] for k in order], axis=1)
    ordered = jnp.dot(place, raw.astype(bf16), preferred_element_type=f32)
    star, density, vertical, diverg, pressure_adjoint, wind_adjoint = (
        ordered[:, width * i : width * (i + 1)] for i in range(6)
    )
    couple = jnp.concatenate([column_ref[...]] * blocks, axis=1)
    rows = lax.broadcasted_iota(jnp.int32, (levels, width), 0)

    def solve(right):
        return jnp.dot(inverse, right, precision=lax.Precision.HIGHEST, preferred_element_type=f32)

    def lower(field):
        return shifted_up(field, rows) - field

    def upper(field):
        return shifted_down(field, rows) - field

    column_input = jnp.concatenate([star, density, vertical, diverg], axis=0).astype(bf16)
    tanh_one = jnp.tanh(jnp.dot(w1t, column_input, preferred_element_type=f32))
    act_one = tanh_one.astype(bf16)
    act_ref[...] = act_one
    rhs_grad = solve(wind_adjoint + couple * lower(pressure_adjoint))
    star_part = pressure_adjoint - upper(couple * rhs_grad)
    heat_grad = rhs_grad.astype(bf16)
    tanh_two = jnp.tanh(contract_first(w2, act_one))
    act_two = tanh_two.astype(bf16)
    act2_ref[...] = act_two
    back_two = jnp.dot(w3, heat_grad, preferred_element_type=f32)
    pre_two_grad = (back_two * (1.0 - tanh_two * tanh_two)).astype(bf16)
    back_one = jnp.dot(w2, pre_two_grad, preferred_element_type=f32)
    pre_one_grad = (back_one * (1.0 - tanh_one * tanh_one)).astype(bf16)
    heating = jnp.dot(w3t, act_two, preferred_element_type=f32)
    wind_next = solve(vertical - couple * lower(star) - 0.5 * density + heating)
    press_next = star + upper(couple * wind_next)
    star_grad = star_part + jnp.dot(w1s, pre_one_grad, preferred_element_type=f32)
    outs = (out0_ref, out1_ref, out2_ref, out3_ref)
    targets = [device ^ (2 * k) for k in range(GROUPS)]
    for k, target in enumerate(targets):
        hid = pl.ds(pl.multiple_of(PIECE * target, PIECE), PIECE)
        sel_ref[PIECE * k : PIECE * (k + 1), :] = act_ref[hid, :]
        sel2_ref[PIECE * k : PIECE * (k + 1), :] = act2_ref[hid, :]
    local_two = contract_last(sel_ref[...], pre_two_grad)
    local_three = contract_last(heat_grad, sel2_ref[...])
    g_ref[...] = contract_last(column_input, pre_one_grad)
    fields = jnp.concatenate([press_next, wind_next, star_grad], axis=1).astype(bf16)
    stored = lax.dot_general(place, fields, (((0,), (0,)), ((), ())), preferred_element_type=f32)
    back = out0_ref.shape[0] - TAIL
    for k in range(3 * blocks):
        y_ref[pl.ds(4 + k, devices, stride=back), :] = stored[:, LANE * k : LANE * (k + 1)]
    for k in range(4 + 3 * blocks, back):
        y_ref[pl.ds(k, devices, stride=back), :] = jnp.zeros((devices, LANE), f32)
    t_ref[...] = local_three
    for k, (target, out_ref) in enumerate(zip(targets, outs)):
        pair = g_ref[pl.ds(pl.multiple_of(SUB * (target // 2), SUB), SUB), :]
        one = jnp.where(core == 0, pair[:4, :], pair[4:, :])
        tile = t_ref[...] if k == 0 else pltpu.roll(t_ref[...], LANE - PIECE * k, 1)
        three = tile[:4, :]
        for q in range(4):
            cols = slice(LANE * q, LANE * (q + 1))
            out_ref[PIECE * q : PIECE * (q + 1), :] = local_two[PIECE * k : PIECE * (k + 1), cols].astype(bf16)
            h_ref[4 * q : 4 * q + 4, :] = one[:, cols]
            if q > 0:
                three = jnp.where(lane_group(lanes, q), pltpu.roll(tile[4 * q : 4 * q + 4, :], PIECE * q, 1), three)
        out_ref[HEAD:TAIL, :] = h_ref[...].astype(bf16)
        start = pl.multiple_of(back * target, SUB)
        y_ref[pl.ds(start, 4), :] = three
        out_ref[TAIL:, :] = y_ref[pl.ds(start, back), :].astype(bf16)


def finish_kernel(scale, r0_ref, r3_ref, r2_ref, r1_ref, p_ref, w_ref, g_ref, one_ref, two_ref, three_ref, y_ref):
    received = (r0_ref, r1_ref, r2_ref, r3_ref)
    back = r0_ref.shape[0] - TAIL
    half = p_ref.shape[0] // SUB
    group = lax.axis_index("slab") // 2 % GROUPS

    def total(start, stop):
        return sum(ref[start:stop, :].astype(jnp.float32) for ref in received) * scale

    for q in range(4):
        two_ref[:, LANE * q : LANE * (q + 1)] = total(PIECE * q, PIECE * (q + 1))
    one = total(HEAD, TAIL)
    for q in range(4):
        one_ref[:, LANE * q : LANE * (q + 1)] = one[4 * q : 4 * q + 4, :]
    for k, ref in enumerate(received):
        y_ref[pl.ds(pl.multiple_of(back * (group ^ k), SUB), back), :] = ref[TAIL:, :].astype(jnp.float32)
    three = sum(y_ref[back * g : back * g + 4, :] for g in range(GROUPS)) * scale
    for q in range(4):
        three_ref[4 * q : 4 * q + 4, :] = three[:, PIECE * q : PIECE * (q + 1)]
    for f, ref in enumerate((p_ref, w_ref, g_ref)):
        for j in range(half):
            for b in range(2):
                rows = pl.ds(4 + 2 * half * f + half * b + j, GROUPS, stride=back)
                ref[SUB * j + GROUPS * b : SUB * j + GROUPS * (b + 1), :] = y_ref[rows, :]


def fast_body(
    pressure, density, vertical_wind, horizontal_wind, metric_terms, neighbors, level_order, stiffness, coupling,
    weight_one, weight_two, weight_three, pressure_adjoint, wind_adjoint,
):
    levels = devices = level_order.shape[0]
    columns = neighbors.shape[1]
    rows = columns // LANE
    blocks = rows // GROUPS
    width = blocks * LANE
    hidden = weight_two.shape[1]
    f32, bf16 = jnp.float32, jnp.bfloat16

    def pad(count):
        return -(-count // SUB) * SUB

    def view(field):
        return field.reshape(rows, LANE)

    def lanes(table):
        return table.reshape(table.shape[0], rows, LANE).transpose(1, 0, 2)

    def swap(array, bits):
        return lax.ppermute(array, "slab", [(i, i ^ bits) for i in range(devices)])

    def among_groups(outgoing, order=range(GROUPS)):
        return [outgoing[0]] + [swap(outgoing[k], 2 * k) for k in order[1:]]

    sources = (
        view(pressure), view(density), view(vertical_wind), horizontal_wind.reshape(2, rows, LANE), lanes(metric_terms),
        lanes(neighbors), weight_one, weight_two, weight_three.T, view(pressure_adjoint), view(wind_adjoint),
    )
    piece, back = 3 * blocks, pad(4 + 3 * blocks)
    one_group = (shape((FRONT + 2 * piece, LANE), bf16),) * GROUPS
    all_groups = pltpu.VMEM((GROUPS * 2 * piece, LANE), f32)
    whole, *near = call(
        pack_kernel, "pack", (shape((FRONT + GROUPS * 2 * piece, LANE), bf16),) + one_group, len(sources),
        [pltpu.VMEM(source.shape, source.dtype) for source in sources]
        + [pltpu.VMEM((16, LANE), f32), pltpu.VMEM((SUB * piece, LANE), f32), all_groups, pltpu.SemaphoreType.DMA((len(sources),))],
        pltpu.HBM,
    )(*(pltpu.with_memory_space_constraint(source, pltpu.HBM) for source in sources))
    operators = call(
        operator_kernel, "operators", (shape((levels, levels), bf16), shape((levels, levels), f32), shape((levels, LANE), f32)), 3
    )(level_order.reshape(1, levels), stiffness.reshape(1, levels), coupling.reshape(1, levels))
    whole, *operators = lax.optimization_barrier((swap(whole, SUB), *operators))
    far = call(relay_kernel, "relay", one_group, 1, [all_groups])(whole)
    near = among_groups(near, NEIGHBORS)
    far = among_groups(far, NEIGHBORS)
    *near, far[1] = lax.optimization_barrier((*near, far[1]))
    same_core = near + far
    other_core = [swap(block, 1) for block in same_core]
    block = shape((TAIL + back, LANE), bf16)
    send_back = call(
        column_kernel, "column_step", (block,) * GROUPS, 4 * GROUPS + 3,
        [
            pltpu.VMEM((devices * STRIDE, LANE), f32), pltpu.VMEM((16 * devices, LANE), f32),
            pltpu.VMEM((hidden, hidden), bf16), pltpu.VMEM((levels, hidden), f32), pltpu.VMEM((hidden, width), bf16),
            pltpu.VMEM((GROUPS * PIECE, width), bf16), pltpu.VMEM((4 * levels, hidden), f32), pltpu.VMEM((16, LANE), f32),
            pltpu.VMEM((devices * back, LANE), f32), pltpu.VMEM((levels, LANE), f32),
            pltpu.VMEM((hidden, width), bf16), pltpu.VMEM((GROUPS * PIECE, width), bf16),
        ],
    )(*same_core, *other_core, *operators)
    received = among_groups(send_back, (0, 3, 2, 1))
    field_out = shape((rows, LANE), f32)
    new_pressure, new_wind, grad, first_grad, second_grad, third_grad = call(
        functools.partial(finish_kernel, 1.0 / math.sqrt(columns)), "finish",
        (
            field_out, field_out, field_out, shape(weight_one.shape, f32), shape(weight_two.shape, f32),
            shape(weight_three.shape[::-1], f32),
        ),
        GROUPS,
        [pltpu.VMEM((SUB * back, LANE), f32)],
    )(*received)
    return (
        new_pressure.reshape(1, columns), new_wind.reshape(1, columns), grad.reshape(1, columns),
        first_grad, second_grad, third_grad.T,
    )


def fits_tiles(*args):
    pressure, level_order, neighbors = args[0], args[6], args[5]
    weight_one, weight_two, weight_three = args[9:12]
    return (
        pressure.shape[0] == 1
        and level_order.shape[0] == 2 * SUB
        and neighbors.shape[1] % (2 * LANE * SUB) == 0
        and weight_one.shape == (4, 4 * LANE)
        and weight_two.shape == (PIECE, 4 * LANE)
        and weight_three.shape == (PIECE, 2 * SUB)
    )


def any_body(*args):
    return (fast_body if fits_tiles(*args) else body)(*args)


def solution(mesh):
    in_specs = (
        P("slab", "date"),
        P("slab", "date"),
        P("slab", "date"),
        P(None, "slab", "date"),
        P(),
        P(),
        P(),
        P(),
        P(),
        P("slab", None),
        P("slab", None),
        P("slab", None),
        P("slab", "date"),
        P("slab", "date"),
    )
    out_specs = (
        P("slab", "date"),
        P("slab", "date"),
        P("slab", "date"),
        P(("date", "slab"), None),
        P(("date", "slab"), None),
        P(("date", "slab"), None),
    )
    return jax.shard_map(any_body, mesh=mesh, in_specs=in_specs, out_specs=out_specs, check_vma=False)
```
